32 devices in a mesh: seq: 8 (over y, x, core), head: 4 (over z).
Axes of the slice: x: 2, y: 2, z: 4, core: 2. Of those that a mesh axis runs over, the one named last changes fastest.
Arguments:
- tokens: bfloat16 [8192, 2048], P(('seq', 'head')), may hold values from -6 to 6
- packing: int32 [8192], replicated, may hold values from 0 to 8191, as said below
- segment_ids: int32 [8192], replicated, may hold values from 0 to 7, never falling along the last dimension, each value on 1 to 4096 neighbouring positions
- norm_gain: float32 [2048], replicated, may hold values from 0.1 to 1.9
- gate_proj: bfloat16 [2048, 4096], P(None, 'head'), may hold values from -0.125 to 0.125
- value_proj: bfloat16 [2048, 4096], P(None, 'head'), may hold values from -0.125 to 0.125
- shared_proj: bfloat16 [2048, 256], replicated, may hold values from -0.125 to 0.125
- step_proj: bfloat16 [2048, 64], P(None, 'head'), may hold values from -0.125 to 0.125
- conv_value: float32 [4, 4096], P(None, 'head'), may hold values from -3 to 3
- conv_value_bias: float32 [4096], P('head'), may hold values from -3 to 3
- conv_shared: float32 [4, 256], replicated, may hold values from -3 to 3
- conv_shared_bias: float32 [256], replicated, may hold values from -3 to 3
- step_bias: float32 [64], P('head'), may hold values from -4.5 to -2.5
- log_decay: float32 [64], P('head'), may hold values from -6.2 to 1.1
- skip_gain: float32 [64], P('head'), may hold values from 0.5 to 1.5
- gated_gain: float32 [4096], P('head'), may hold values from 0.1 to 1.9
- out_proj: bfloat16 [4096, 2048], P('head'), may hold values from -0.09375 to 0.09375
- cotangent: bfloat16 [8192, 2048], P(('seq', 'head')), may hold values from -6 to 6
Outputs:
- mixed: bfloat16 [8192, 2048], P(('seq', 'head'))
- grad_tokens: bfloat16 [8192, 2048], P(('seq', 'head'))
- grad_norm_gain: float32 [2048], replicated
- grad_gate_proj: float32 [2048, 4096], P('seq', 'head')
- grad_value_proj: float32 [2048, 4096], P('seq', 'head')
- grad_shared_proj: float32 [2048, 256], replicated
- grad_step_proj: float32 [2048, 64], P('seq', 'head')
- grad_conv_value: float32 [4, 4096], P(None, 'head')
- grad_conv_value_bias: float32 [4096], P('head')
- grad_conv_shared: float32 [4, 256], replicated
- grad_conv_shared_bias: float32 [256], replicated
- grad_step_bias: float32 [64], P('head')
- grad_log_decay: float32 [64], P('head')
- grad_skip_gain: float32 [64], P('head')
- grad_gated_gain: float32 [4096], P('head')
- grad_out_proj: float32 [4096, 2048], P(('head', 'seq'))
The draws below stay inside these ranges and needn't reach their ends.
Inputs may be any that keep to these rules, and one draw needn't show every extreme that they name: `segment_ids`: never falling along the packed stream; each sequence has 1 to 4096 positions, one exactly 4096. `packing`: A permutation. The packed stream falls into blocks of 32 positions, each holding 32 consecutive given rows that start at a multiple of 32; the 256 given rows of each device form blocks that lie in different ranges of 1024 consecutive packed positions, one in each.
All inputs are finite; a program needn't handle non-finite values.
Results may differ from the reference program's by a relative error of at most 0.015.
Values may be sent and summed in bfloat16 or wider, within the bound.
No kernel may reach another device: no remote copies, remote signals or barrier semaphores. Data moves between devices by JAX's collectives and lax.ppermute only.
A program may use at most 384 MiB of HBM per device.

```python
import math
import jax
import jax.numpy as jnp
import numpy as np
from jax import lax

D = 2048
HEADS = 64
HDIM = 64
STATE = 128
WIDTH = 4
SPAN = 256
TOK_DEV = 256
INNER = 4096
TOKENS = 8192
MOST = 4096
N_SEQ = 8
N_HEAD = 4


def draw_packing(key, part):
    send_key, place_key = jax.random.split(jax.random.fold_in(key, 7))
    source_count = N_SEQ * N_HEAD
    tile_rows = TOK_DEV // N_SEQ
    dest_table = jax.vmap(lambda one_key: jax.random.permutation(one_key, N_SEQ))(jax.random.split(send_key, source_count))
    slot_of = jnp.argsort(dest_table, axis=1).astype(jnp.int32)
    placed = jax.vmap(lambda one_key: jax.random.permutation(one_key, source_count))(jax.random.split(place_key, N_SEQ)).astype(jnp.int32)
    shard_ids = jnp.arange(N_SEQ, dtype=jnp.int32)[:, None] + jnp.zeros((1, source_count), jnp.int32)
    head_src = placed // N_SEQ
    seq_src = placed % N_SEQ
    source_dev = seq_src * N_HEAD + head_src
    slot_index = slot_of[source_dev, shard_ids]
    given_tile = source_dev * N_SEQ + slot_index
    rows_out = given_tile.reshape(-1)[:, None] * tile_rows + jnp.arange(tile_rows, dtype=jnp.int32)[None, :]
    return rows_out.reshape(-1).astype(jnp.int32)


def steps_of(own_key, dims, shards, low, top_value):
    gain = 1.0
    for dim, blocks in shards:
        heights = jax.random.uniform(jax.random.fold_in(jax.random.fold_in(own_key, 6), dim), (blocks,), jnp.float32, low / len(shards), top_value / len(shards))
        gain = gain * jnp.repeat(jnp.exp(heights), dims[dim] // blocks).reshape((-1,) + (1,) * (len(dims) - 1 - dim))
    return gain


def length_profile(amount, total, bound, slope):
    portions = [(1 << 20) // math.isqrt(grade ** slope) + 1 for grade in range(2, amount + 1)]
    spare, counts = total - bound - (amount - 1), [1] * (amount - 1)
    while spare > 0:
        candidates = [i for i in range(amount - 1) if counts[i] < bound]
        pool, left = sum([portions[i] for i in candidates]), spare
        for i in candidates:
            addition = min(bound - counts[i], max(1, left * portions[i] // pool), spare)
            counts[i] = counts[i] + addition
            spare = spare - addition
    return np.array([bound] + counts)


def ragged_sizes(key, count, total, bound, lean):
    if count == 2:
        one = jax.random.randint(key, (), max(1, total - bound), min(bound, total - 1) + 1)
        return jnp.stack([one, total - one])
    tallies = jnp.asarray(length_profile(count, total, bound, lean), jnp.int32)
    pairs = (count - 1) // 2
    source_of, sink = tallies[1:1 + 2 * pairs:2], tallies[2:2 + 2 * pairs:2]
    margin = jnp.minimum(source_of - 1, bound - sink)
    passed = jax.random.randint(jax.random.fold_in(key, 1), (pairs,), 0, 1 << 20) % (margin + 1)
    tallies = tallies.at[1:1 + 2 * pairs:2].set(source_of - passed).at[2:2 + 2 * pairs:2].set(sink + passed)
    return tallies[jax.random.permutation(jax.random.fold_in(key, 2), count)]


def normal_values(stream_key, shape, scale, reach, cuts=(), held_as=jnp.bfloat16):
    values = scale * jax.random.normal(stream_key, shape, jnp.float32)
    if cuts:
        values = values * steps_of(stream_key, shape, cuts, -0.22, 0.18)
    return jnp.clip(values, -reach, reach).astype(held_as)


def setup_inputs(seed: int = 0) -> dict:
    streams_of = jax.random.split(jax.random.key(seed), 19)
    return {
        "tokens": normal_values(streams_of[0], (TOKENS, D), 1.0, 6.0, ((0, 32),)),
        "packing": draw_packing(jax.random.fold_in(streams_of[18], 71), 0),
        "segment_ids": jnp.searchsorted(jnp.cumsum(ragged_sizes(streams_of[2], TOKENS * 4 // MOST, TOKENS, MOST, 1)), jnp.arange(TOKENS), side="right").astype(jnp.int32),
        "norm_gain": jnp.clip(1.0 + 0.18 * jax.random.normal(streams_of[3], (D,), jnp.float32), 0.1, 1.9),
        "gate_proj": normal_values(streams_of[4], (D, INNER), D ** -0.5, 0.125, ((1, 4),)),
        "value_proj": normal_values(streams_of[5], (D, INNER), D ** -0.5, 0.125, ((1, 4),)),
        "shared_proj": normal_values(streams_of[6], (D, 2 * STATE), D ** -0.5, 0.125),
        "step_proj": normal_values(streams_of[7], (D, HEADS), D ** -0.5, 0.125, ((1, 4),)),
        "conv_value": normal_values(streams_of[8], (WIDTH, INNER), WIDTH ** -0.5, 3.0, ((1, 4),), jnp.float32),
        "conv_value_bias": normal_values(streams_of[9], (INNER,), 0.5, 3.0, ((0, 4),), jnp.float32),
        "conv_shared": normal_values(streams_of[10], (WIDTH, 2 * STATE), WIDTH ** -0.5, 3.0, (), jnp.float32),
        "conv_shared_bias": normal_values(streams_of[11], (2 * STATE,), 0.5, 3.0, (), jnp.float32),
        "step_bias": jnp.clip(-4.5 + 2.0 * jax.random.uniform(streams_of[12], (HEADS,), jnp.float32) ** steps_of(streams_of[12], (HEADS,), ((0, 4),), -0.2, 0.2), -4.5, -2.5),
        "log_decay": jnp.clip(-6.2 + 7.2999998 * jax.random.uniform(streams_of[13], (HEADS,), jnp.float32) ** steps_of(streams_of[13], (HEADS,), ((0, 4),), -0.2, 0.2), -6.2, 1.1),
        "skip_gain": jnp.clip(0.5 + 1.0 * jax.random.uniform(streams_of[14], (HEADS,), jnp.float32) ** steps_of(streams_of[14], (HEADS,), ((0, 4),), -0.2, 0.2), 0.5, 1.5),
        "gated_gain": jnp.clip(1.0 + 0.18 * jax.random.normal(streams_of[15], (INNER,), jnp.float32), 0.1, 1.9),
        "out_proj": normal_values(streams_of[16], (INNER, D), INNER ** -0.5, 0.09375, ((0, 4),)),
        "cotangent": normal_values(streams_of[17], (TOKENS, D), 1.0, 6.0, ((0, 32),)),
    }


EPS = 1e-05
HIGH = lax.Precision.HIGHEST

@jax.custom_vjp
def low(v):
    return lax.optimization_barrier(v.astype(jnp.bfloat16)).astype(jnp.float32)

@jax.custom_vjp
def low_back(v):
    return v

def low_keep(v):
    return (low(v), None)

def low_pass(kept, grad):
    return (grad,)

def back_keep(v):
    return (v, None)

def back_low(kept, grad):
    return (low(grad),)
low.defvjp(low_keep, low_pass)
low_back.defvjp(back_keep, back_low)

def ssd_span(carried, pieces):
    ssm_state, prev_seg = carried
    values, decay_log, step_size, b_mat, c_mat, seg_rows = pieces
    row_count = seg_rows.shape[0]
    positions = jnp.arange(row_count)
    causal = positions[:, None] >= positions[None, :]
    same_mask = causal & (seg_rows[:, None] == seg_rows[None, :])
    running = jnp.cumsum(decay_log, axis=0)
    spread_log = running.T[:, :, None] - running.T[:, None, :]
    within = jnp.where(same_mask[None], jnp.exp(jnp.minimum(spread_log, 0.0)), 0.0)
    intersection_cb = jnp.dot(c_mat, b_mat.T, precision=HIGH)
    weighted = values * step_size[:, :, None]
    local_out = jnp.einsum('hts,shp->thp', within * intersection_cb[None], weighted, precision=HIGH)
    continued = (seg_rows == prev_seg).astype(jnp.float32)
    enter_decay = jnp.exp(running) * continued[:, None]
    from_state = jnp.einsum('tn,hnp->thp', c_mat, ssm_state, precision=HIGH) * enter_decay[:, :, None]
    last_same = (seg_rows == seg_rows[-1]).astype(jnp.float32)
    to_end = jnp.exp(jnp.minimum(running[-1][None, :] - running, 0.0)) * last_same[:, None]
    new_state = ssm_state * enter_decay[-1][:, None, None] + jnp.einsum('sn,shp->hnp', b_mat, weighted * to_end[:, :, None], precision=HIGH)
    return ((new_state, seg_rows[-1]), local_out + from_state)

def causal_conv(conv_rows, rim_rows, seg_rows, rim_seg, kernel, bias_vec):
    padded = jnp.concatenate([rim_rows, conv_rows], axis=0)
    padded_seg = jnp.concatenate([rim_seg, seg_rows])
    length = conv_rows.shape[0]
    kernel_width = kernel.shape[0]
    summed = jnp.zeros_like(conv_rows) + bias_vec[None, :]
    for offset in range(kernel_width):
        same_seq = (padded_seg[offset:offset + length] == seg_rows).astype(jnp.float32)
        summed = summed + padded[offset:offset + length] * kernel[offset][None, :] * same_seq[:, None]
    return jax.nn.silu(summed)

def reference(tokens, packing, segment_ids, norm_gain, gate_proj, value_proj, shared_proj, step_proj, conv_value, conv_value_bias, conv_shared, conv_shared_bias, step_bias, log_decay, skip_gain, gated_gain, out_proj, cotangent):
    block_rows = 8 * SPAN
    block_count = TOKENS // block_rows
    span_count = block_rows // SPAN
    inner_width = HEADS * HDIM
    packed_index = packing.astype(jnp.int32)
    seg_all = segment_ids.astype(jnp.int32)
    padded_ids = jnp.concatenate([jnp.full((WIDTH - 1,), -1, jnp.int32), seg_all])
    rim_ids = padded_ids[:TOKENS].reshape(block_count, block_rows)[:, :WIDTH - 1]
    seg_blocks = seg_all.reshape(block_count, block_rows)

    def forward(tok_all, norm_gain, gate_proj, value_proj, shared_proj, step_proj, conv_value, conv_value_bias, conv_shared, conv_shared_bias, step_bias, log_decay, skip_gain, gated_gain, out_proj):

        def block_step(carried, pieces):
            ssm_state, rim_rows = carried
            tok_rows, seg_rows, rim_seg = pieces
            normed = low(tok_rows * lax.rsqrt(lax.optimization_barrier(jnp.mean(tok_rows * tok_rows, axis=1, keepdims=True)) + EPS) * norm_gain[None, :])
            gate_z = low_back(jnp.dot(normed, gate_proj, precision=HIGH))
            value_rows = low_back(jnp.dot(normed, value_proj, precision=HIGH))
            shared_rows = jnp.dot(normed, shared_proj, precision=HIGH)
            step_raw = low_back(jnp.dot(normed, step_proj, precision=HIGH))
            conv_in = jnp.concatenate([value_rows, shared_rows], axis=1)
            kernel = jnp.concatenate([conv_value, conv_shared], axis=1)
            bias_vec = jnp.concatenate([conv_value_bias, conv_shared_bias])
            active = causal_conv(conv_in, rim_rows, seg_rows, rim_seg, kernel, bias_vec)
            values = active[:, :inner_width].reshape(block_rows, HEADS, HDIM)
            b_mat = active[:, inner_width:inner_width + STATE]
            c_mat = active[:, inner_width + STATE:]
            step_size = jax.nn.softplus(step_raw + step_bias[None, :])
            decay_log = -step_size * jnp.exp(log_decay)[None, :]
            span_pieces = (values.reshape(span_count, SPAN, HEADS, HDIM), decay_log.reshape(span_count, SPAN, HEADS), step_size.reshape(span_count, SPAN, HEADS), b_mat.reshape(span_count, SPAN, STATE), c_mat.reshape(span_count, SPAN, STATE), seg_rows.reshape(span_count, SPAN))
            (new_state, last_id), span_out = lax.scan(jax.checkpoint(ssd_span), (ssm_state, rim_seg[-1]), span_pieces)
            scanned = span_out.reshape(block_rows, HEADS, HDIM) + values * skip_gain[None, :, None]
            gated_rows = scanned.reshape(block_rows, inner_width) * jax.nn.silu(gate_z)
            gated_rstd = lax.rsqrt(lax.optimization_barrier(jnp.mean(gated_rows * gated_rows, axis=1, keepdims=True)) + EPS)
            gated_out = low(gated_rows * gated_rstd * gated_gain[None, :])
            out_rows = tok_rows + jnp.dot(gated_out, out_proj, precision=HIGH)
            return ((new_state, conv_in[block_rows - WIDTH + 1:]), out_rows)
        start_carry = (jnp.zeros((HEADS, STATE, HDIM), jnp.float32), jnp.zeros((WIDTH - 1, inner_width + 2 * STATE), jnp.float32))
        final_carry, out_blocks = lax.scan(jax.checkpoint(block_step), start_carry, (tok_all.reshape(block_count, block_rows, D), seg_blocks, rim_ids))
        return out_blocks.reshape(TOKENS, D)
    tok_packed = tokens.astype(jnp.float32)[packed_index]
    cot_packed = cotangent.astype(jnp.float32)[packed_index]
    floats = [norm_gain, gate_proj, value_proj, shared_proj, step_proj, conv_value, conv_value_bias, conv_shared, conv_shared_bias, step_bias, log_decay, skip_gain, gated_gain, out_proj]
    floats = [tok_packed] + [item.astype(jnp.float32) for item in floats]
    mixed_rows, pullback = jax.vjp(forward, *floats)
    gradients = pullback(cot_packed)
    mixed_given = jnp.zeros((TOKENS, D), jnp.float32).at[packed_index].set(mixed_rows)
    grad_given = jnp.zeros((TOKENS, D), jnp.float32).at[packed_index].set(gradients[0])
    return (mixed_given.astype(jnp.bfloat16), grad_given.astype(jnp.bfloat16), gradients[1], gradients[2], gradients[3], gradients[4], gradients[5], gradients[6], gradients[7], gradients[8], gradients[9], gradients[10], gradients[11], gradients[12], gradients[13], gradients[14])
```

```python
import jax
import jax.numpy as jnp
from jax import lax
from jax.experimental import pallas as pl
from jax.experimental.pallas import tpu as pltpu
from jax.sharding import PartitionSpec as P

EPS = 1e-05
ROWS = 128
LANES = 128
HALF = 64
RIM = 8
FAR = -1e30
F32 = jnp.float32
BF16 = jnp.bfloat16
VMEM_BYTES = 56 * 1024 * 1024
CONTRACT_ROWS = (((0,), (0,)), ((), ()))
CONTRACT_COLS = (((1,), (1,)), ((), ()))


def dot(a, b, dims=(((1,), (0,)), ((), ()))):
    return lax.dot_general(a, b, dims, preferred_element_type=F32)


def two_parts(x):
    upper = x.astype(BF16)
    return upper, (x - upper.astype(F32)).astype(BF16)


def three_parts(x):
    upper, rest = x.astype(BF16), x
    rest = x - upper.astype(F32)
    middle = rest.astype(BF16)
    return upper, middle, (rest - middle.astype(F32)).astype(BF16)


def in_two(x):
    return jnp.concatenate(two_parts(x), axis=1)


def twice(x):
    return jnp.concatenate([x, x], axis=0)


def b_parts(bc_ref, at):
    return bc_ref[at, : 2 * LANES]


def c_parts(bc_ref, at):
    return bc_ref[at, 2 * LANES :]


def cross_product(bc_ref, at):
    b, c = b_parts(bc_ref, at), c_parts(bc_ref, at)
    upper = jnp.concatenate([b[:, :LANES], b[:, :LANES]], axis=1)
    return dot(c, upper, CONTRACT_COLS) + dot(c[:, :LANES], b[:, LANES:], CONTRACT_COLS)


def lane_ids(rows):
    return lax.broadcasted_iota(jnp.int32, (rows, LANES), 1)


def row_ids(rows):
    return lax.broadcasted_iota(jnp.int32, (rows, LANES), 0)


def head_cols(block, pair):
    shift = lax.rem(LANES - 2 * pair, LANES)
    turned = pltpu.roll(block, shift, axis=1)
    first = jnp.broadcast_to(turned[:, 0:1], block.shape)
    second = jnp.broadcast_to(turned[:, 1:2], block.shape)
    return first, second


def paired(first, second):
    return jnp.where(lane_ids(first.shape[0]) < HALF, first, second)


def head_selector(pair):
    lane = row_ids(LANES)
    head = 2 * pair + jnp.where(lane < HALF, 0, 1)
    return (lane_ids(LANES) == head).astype(F32).astype(BF16)


def split_sum(x, selector):
    upper, lower = two_parts(x)
    stacked = jnp.concatenate([upper, lower], axis=1)
    return dot(stacked, jnp.concatenate([selector, selector], axis=0))


def lower_ones():
    return (row_ids(ROWS) >= lane_ids(ROWS)).astype(F32).astype(BF16)


def upper_ones():
    return (row_ids(ROWS) <= lane_ids(ROWS)).astype(F32).astype(BF16)


def spread(ref, row, col):
    return jnp.broadcast_to(ref[pl.ds(row, ROWS), col : col + 1], (ROWS, LANES))


def softplus(x):
    return jnp.maximum(x, 0.0) + jnp.log1p(jnp.exp(-jnp.abs(x)))


def sigmoid(x):
    return 1.0 / (1.0 + jnp.exp(-x))


def span_start(q):
    return pl.multiple_of(q * ROWS, ROWS)


def loop(count, body):
    def step(q, carry):
        body(q)
        return carry

    lax.fori_loop(0, count, step, 0)


def conv_span(pad_ref, same_ref, row, taps, bias):
    long = pad_ref[pl.ds(row, ROWS + RIM), :]
    total = bias + taps[3:4] * long[RIM:]
    shifted = []
    for back in (1, 2, 3):
        moved = pltpu.roll(long, back, axis=0)[RIM:]
        moved = moved * same_ref[back - 1, pl.ds(row, ROWS), :]
        shifted.append(moved)
        total = total + taps[3 - back : 4 - back] * moved
    return total, [long[RIM:]] + shifted


def forward_states_kernel(
    value_ref, ss_ref, rim_v_ref, rim_ss_ref, cols_ref, conv_ref, conv_ss_ref, heads_ref,
    x_ref, bc_ref, step_ref, run_ref, run_t_ref, state_ref, decay_ref,
    pad, same, cont, last, bt,
):
    pair = pl.program_id(0)
    rows = value_ref.shape[0]
    spans = rows // ROWS
    width = run_t_ref.shape[1]

    @pl.when(pair == 0)
    def _():
        def masks(q):
            row = span_start(q)
            for k in range(3):
                same[k, pl.ds(row, ROWS), :] = spread(cols_ref, row, k)
            cont[pl.ds(row, ROWS), :] = spread(cols_ref, row, 3)
            last[pl.ds(row, ROWS), :] = spread(cols_ref, row, 4)

        loop(spans, masks)
        for part in range(2):
            lanes = slice(part * LANES, (part + 1) * LANES)
            pad[0:RIM, :] = rim_ss_ref[:, lanes]
            pad[RIM:, :] = ss_ref[:, lanes]
            taps, bias = conv_ss_ref[0:4, lanes], conv_ss_ref[4:5, lanes]

            def shared(q):
                row = span_start(q)
                pre, _ = conv_span(pad, same, row, taps, bias)
                act = pre * sigmoid(pre)
                bc_ref[pl.ds(row, ROWS), 2 * part * LANES : 2 * (part + 1) * LANES] = in_two(act)
                if part == 0:
                    bt[q] = in_two(jnp.transpose(act))

            loop(spans, shared)

        bias, rate = heads_ref[0:1, :], heads_ref[1:2, :]
        tri, tri_t = lower_ones(), upper_ones()

        def steps(q):
            row = span_start(q)
            size = softplus(ss_ref[pl.ds(row, ROWS), 2 * LANES :] + bias)
            step_ref[pl.ds(row, ROWS), :] = size
            parts = three_parts(-size * rate)
            run_ref[pl.ds(row, ROWS), :] = sum(dot(tri, part) for part in parts)
            turned = sum(dot(part, tri_t, CONTRACT_ROWS) for part in parts)
            run_t_ref[q] = turned[:width]

        loop(spans, steps)

    pad[0:RIM, :] = rim_v_ref[...]
    pad[RIM:, :] = value_ref[...]
    taps, bias = conv_ref[0:4], conv_ref[4:5]

    def span(q, carry):
        state, decay = carry
        row = span_start(q)
        at = pl.ds(row, ROWS)
        pre, _ = conv_span(pad, same, row, taps, bias)
        x = pre * sigmoid(pre)
        x_ref[at, :] = x
        size = paired(*head_cols(step_ref[at, :], pair))
        run = paired(*head_cols(run_ref[at, :], pair))
        enter = jnp.exp(run[ROWS - 1 :]) * cont[pl.ds(row + ROWS - 8, 8), :][7:8]
        to_end = jnp.exp(run[ROWS - 1 :] - run) * last[at, :]
        state = state * enter + dot(bt[q], twice((x * size * to_end).astype(BF16)))
        decay = decay * enter
        state_ref[q] = state
        decay_ref[q] = jnp.broadcast_to(decay, (8, LANES))
        return state, decay

    lax.fori_loop(
        0, spans, span, (jnp.zeros((LANES, LANES), F32), jnp.ones((1, LANES), F32))
    )


def span_masks(cols_ref, seg_rows_ref, bias_ref, spans):
    causal = row_ids(ROWS) >= lane_ids(ROWS)

    def mask(q):
        own = spread(cols_ref, span_start(q), 5)
        other = jnp.broadcast_to(seg_rows_ref[q, 0:1, :], (ROWS, ROWS))
        bias_ref[q] = jnp.where(causal & (own == other), 0.0, FAR)

    loop(spans, mask)


def decay_pair(run_ref, run_t_ref, mask_ref, q, pair):
    first, second = head_cols(run_ref[pl.ds(span_start(q), ROWS), :], pair)
    rows = run_t_ref[q, pl.ds(2 * pair, 2), :]
    mask = mask_ref[q]
    return jnp.exp(first - rows[0:1] + mask), jnp.exp(second - rows[1:2] + mask)


def heads_apart(x):
    lane = lane_ids(x.shape[0])
    zero = jnp.zeros_like(x)
    return jnp.concatenate([jnp.where(lane < HALF, x, zero), jnp.where(lane < HALF, zero, x)], axis=0)


def forward_within_kernel(
    x_ref, bc_ref, step_ref, run_ref, run_t_ref, cols_ref, seg_rows_ref, y_ref, mask, cross
):
    pair = pl.program_id(0)
    spans = x_ref.shape[0] // ROWS

    @pl.when(pair == 0)
    def _():
        span_masks(cols_ref, seg_rows_ref, mask, spans)

        def products(q):
            at = pl.ds(span_start(q), ROWS)
            cross[q] = cross_product(bc_ref, at)

        loop(spans, products)

    def span(q):
        at = pl.ds(span_start(q), ROWS)
        size = paired(*head_cols(step_ref[at, :], pair))
        weighted = x_ref[at, :] * size
        first, second = decay_pair(run_ref, run_t_ref, mask, q, pair)
        mix = jnp.concatenate([first * cross[q], second * cross[q]], axis=1).astype(BF16)
        y_ref[at, :] = dot(mix, heads_apart(weighted).astype(BF16))

    loop(spans, span)


def entering(state_ref, decay_ref, incoming, q, before):
    at = jnp.maximum(before, 0)
    local = state_ref[at] + decay_ref[at, 0:1, :] * incoming
    return jnp.where(before >= 0, local, incoming)


def row_sums(acc_ref, out_ref, base, spans):
    ones = jnp.ones((8, LANES), BF16)

    def total(q):
        parts = three_parts(acc_ref[pl.ds(span_start(q), ROWS), :])
        out_ref[q, base : base + 8, :] = sum(dot(ones, part, CONTRACT_COLS) for part in parts)

    loop(spans, total)


def forward_finish_kernel(
    y_ref, x_ref, z_ref, dgo_ref, state_ref, decay_ref, in_ref, bc_ref, run_ref, cols_ref, gains_ref,
    scan_ref, sums_ref, cont, squares, inner,
):
    pair = pl.program_id(0)
    spans = y_ref.shape[0] // ROWS

    @pl.when(pair == 0)
    def _():
        def masks(q):
            row = span_start(q)
            cont[pl.ds(row, ROWS), :] = spread(cols_ref, row, 3)

        loop(spans, masks)
        squares[...] = jnp.zeros_like(squares)
        inner[...] = jnp.zeros_like(inner)

    incoming = in_ref[...]
    skip, gain = gains_ref[0:1], gains_ref[1:2]

    def span(q):
        at = pl.ds(span_start(q), ROWS)
        run = paired(*head_cols(run_ref[at, :], pair))
        state = entering(state_ref, decay_ref, incoming, q, q - 1)
        upper, lower = two_parts(state)
        c = c_parts(bc_ref, at)
        carried = dot(c, twice(upper)) + dot(c[:, :LANES], lower)
        scan = y_ref[at, :] + carried * (jnp.exp(run) * cont[at, :])
        scan_ref[at, :] = scan
        z = z_ref[at, :]
        gated = (scan + skip * x_ref[at, :]) * (z * sigmoid(z))
        squares[at, :] += gated * gated
        inner[at, :] += gain * dgo_ref[at, :] * gated

    loop(spans, span)

    @pl.when(pair == pl.num_programs(0) - 1)
    def _():
        row_sums(squares, sums_ref, 0, spans)
        row_sums(inner, sums_ref, 8, spans)


def gate_back_kernel(
    inner_width,
    scan_ref, x_ref, z_ref, dgo_ref, sums_ref, bc_ref, run_ref, cols_ref, gains_ref,
    out_ref, dz_ref, dy_ref, grad_ref, decay_ref, rows_ref,
    cont, rstd, coef, ct,
):
    pair = pl.program_id(0)
    spans = scan_ref.shape[0] // ROWS

    @pl.when(pair == 0)
    def _():
        def masks(q):
            row = span_start(q)
            at = pl.ds(row, ROWS)
            cont[at, :] = spread(cols_ref, row, 3)
            ct[q] = jnp.concatenate(
                [
                    jnp.transpose(bc_ref[at, k * LANES : (k + 1) * LANES].astype(F32)).astype(BF16)
                    for k in (2, 3)
                ],
                axis=1,
            )
            square = jnp.broadcast_to(sums_ref[q, 0:1, :], (ROWS, LANES))
            cross = jnp.broadcast_to(sums_ref[q, 1:2, :], (ROWS, LANES))
            root = lax.rsqrt(square / inner_width + EPS)
            rstd[at, :] = jnp.transpose(root)
            coef[at, :] = jnp.transpose(root * root * root * cross / inner_width)

        loop(spans, masks)

    skip, gain = gains_ref[0:1], gains_ref[1:2]
    rows_ref[...] = jnp.zeros_like(rows_ref)

    def span(k, carry):
        leaving, decay = carry
        q = spans - 1 - k
        at = pl.ds(span_start(q), ROWS)
        x, z, dgo = x_ref[at, :], z_ref[at, :], dgo_ref[at, :]
        scanned = scan_ref[at, :] + skip * x
        gate = sigmoid(z)
        silu = z * gate
        gated = scanned * silu
        normed = gated * rstd[at, :]
        out_ref[at, :] = (normed * gain).astype(BF16)
        d_gated = rstd[at, :] * (dgo * gain) - gated * coef[at, :]
        d_scan = d_gated * silu
        dz_ref[at, :] = (d_gated * scanned * (gate * (1.0 + z * (1.0 - gate)))).astype(BF16)
        dy_ref[at, :] = d_scan
        rows_ref[0:1] += jnp.sum(dgo * normed, axis=0, keepdims=True)
        rows_ref[1:2] += jnp.sum(d_scan * x, axis=0, keepdims=True)
        run = paired(*head_cols(run_ref[at, :], pair))
        enter = jnp.exp(run) * cont[at, :]
        upper, lower = two_parts(d_scan * enter)
        turned = ct[q]
        leaving = leaving * enter[ROWS - 1 :] + dot(turned, twice(upper)) + dot(turned[:, :ROWS], lower)
        decay = decay * enter[ROWS - 1 :]
        grad_ref[q] = leaving
        decay_ref[q] = jnp.broadcast_to(decay, (8, LANES))
        return leaving, decay

    lax.fori_loop(
        0, spans, span, (jnp.zeros((LANES, LANES), F32), jnp.ones((1, LANES), F32))
    )


def backward_within_kernel(
    x_ref, dy_ref, bc_ref, step_ref, run_ref, run_t_ref, cols_ref, seg_rows_ref,
    dxw_ref, dbc_ref, mask, cross, d_cross,
):
    pair = pl.program_id(0)
    spans = x_ref.shape[0] // ROWS

    @pl.when(pair == 0)
    def _():
        span_masks(cols_ref, seg_rows_ref, mask, spans)

        def products(q):
            at = pl.ds(span_start(q), ROWS)
            cross[q] = cross_product(bc_ref, at)
            d_cross[q] = jnp.zeros((ROWS, ROWS), F32)

        loop(spans, products)

    def span(q):
        at = pl.ds(span_start(q), ROWS)
        size = paired(*head_cols(step_ref[at, :], pair))
        weighted = (x_ref[at, :] * size).astype(BF16)
        first, second = decay_pair(run_ref, run_t_ref, mask, q, pair)
        dy, dy_rest = two_parts(dy_ref[at, :])
        apart = heads_apart(dy)
        both = jnp.concatenate([apart, heads_apart(dy_rest)], axis=1)
        d_mix = dot(both, jnp.concatenate([weighted, weighted], axis=1), CONTRACT_COLS)
        d_cross[q] += first * d_mix[:ROWS] + second * d_mix[ROWS:]
        mix = jnp.concatenate([first * cross[q], second * cross[q]], axis=0).astype(BF16)
        dxw_ref[at, :] = dot(mix, apart, CONTRACT_ROWS)

    loop(spans, span)

    @pl.when(pair == pl.num_programs(0) - 1)
    def _():
        def shared(q):
            at = pl.ds(span_start(q), ROWS)
            grad = d_cross[q].astype(BF16)
            b, c = b_parts(bc_ref, at), c_parts(bc_ref, at)
            both = dot(grad, c, CONTRACT_ROWS)
            dbc_ref[at, :LANES] = both[:, :LANES] + both[:, LANES:]
            both = dot(grad, b)
            dbc_ref[at, LANES:] = both[:, :LANES] + both[:, LANES:]

        loop(spans, shared)


def conv_back(pad_ref, d_pre, same, taps, spans, store, rim_store):
    def span(q):
        at = pl.ds(span_start(q), ROWS + RIM)
        long = d_pre[at, :]
        total = taps[3:4] * long[:ROWS]
        for ahead in (1, 2, 3):
            masked = long * same[ahead - 1, at, :]
            moved = pltpu.roll(masked, ROWS + RIM - ahead, axis=0)[:ROWS]
            total = total + taps[3 - ahead : 4 - ahead] * moved
        store(q, total)

    loop(spans, span)
    head = d_pre[0:RIM, :]
    total = jnp.zeros((RIM, LANES), F32)
    for ahead in (1, 2, 3):
        masked = head * same[ahead - 1, 0:RIM, :]
        both = jnp.concatenate([jnp.zeros((RIM, LANES), F32), masked], axis=0)
        total = total + taps[3 - ahead : 4 - ahead] * pltpu.roll(both, 2 * RIM - ahead, axis=0)[:RIM]
    rim_store(total)


def tap_sums(d_pre, shifted):
    sums = [jnp.sum(d_pre * shifted[3 - k], axis=0, keepdims=True) for k in range(4)]
    sums.append(jnp.sum(d_pre, axis=0, keepdims=True))
    return jnp.concatenate(sums + [jnp.zeros((3, LANES), F32)], axis=0)


def silu_grad(pre):
    gate = sigmoid(pre)
    return gate * (1.0 + pre * (1.0 - gate))


def backward_finish_kernel(
    value_ref, ss_ref, rim_v_ref, rim_ss_ref, x_ref, dy_ref, scan_ref, dxw_ref, dbc_ref,
    state_ref, decay_ref, in_ref, grad_ref, back_ref, out_ref,
    bc_ref, step_ref, run_ref, cols_ref, conv_ref, conv_ss_ref, heads_ref, gains_ref,
    low_ref, tail_ref, rim_ref, taps_ref, low_ss_ref, tail_ss_ref, rim_ss_out_ref, taps_ss_ref, small_ref,
    pad, d_pre, same, cont, last, d_run, d_step, d_bc,
):
    pair = pl.program_id(0)
    rows = value_ref.shape[0]
    spans = rows // ROWS

    @pl.when(pair == 0)
    def _():
        def masks(q):
            row = span_start(q)
            for k in range(3):
                same[k, pl.ds(row, ROWS), :] = spread(cols_ref, row, k)
            cont[pl.ds(row, ROWS), :] = spread(cols_ref, row, 3)
            last[pl.ds(row, ROWS), :] = spread(cols_ref, row, 4)

        loop(spans, masks)
        same[:, rows:, :] = jnp.zeros((3, RIM, LANES), F32)
        d_pre[rows:, :] = jnp.zeros((RIM, LANES), F32)
        d_run[...] = jnp.zeros_like(d_run)
        d_step[...] = jnp.zeros_like(d_step)
        d_bc[...] = dbc_ref[...]

    pad[0:RIM, :] = rim_v_ref[...]
    pad[RIM:, :] = value_ref[...]
    taps, bias = conv_ref[0:4], conv_ref[4:5]
    skip = gains_ref[0:1]
    incoming, outgoing = in_ref[...], out_ref[...]
    selector = head_selector(pair)
    taps_ref[...] = jnp.zeros_like(taps_ref)
    final_row = row_ids(ROWS) == ROWS - 1

    def span(q):
        row = span_start(q)
        at = pl.ds(row, ROWS)
        x, dy = x_ref[at, :], dy_ref[at, :]
        size = paired(*head_cols(step_ref[at, :], pair))
        run = paired(*head_cols(run_ref[at, :], pair))
        enter = jnp.exp(run) * cont[at, :]
        to_end = jnp.exp(run[ROWS - 1 :] - run) * last[at, :]
        state, state_rest = two_parts(entering(state_ref, decay_ref, incoming, q, q - 1))
        after = state_ref[q] + decay_ref[q, 0:1, :] * incoming
        ahead = jnp.minimum(q + 1, spans - 1)
        grad = jnp.where(
            q + 1 < spans, grad_ref[ahead] + back_ref[ahead, 0:1, :] * outgoing, outgoing
        )
        weighted = x * size
        low_grad = grad.astype(BF16)
        d_weighted = dxw_ref[at, :] + to_end * dot(b_parts(bc_ref, at), twice(low_grad))
        entered = in_two(dy * enter)
        d_bc[at, LANES:] += dot(
            entered, jnp.concatenate([state, state], axis=1), CONTRACT_COLS
        ) + dot(entered[:, :LANES], state_rest, CONTRACT_COLS)
        d_bc[at, :LANES] += dot((weighted * to_end).astype(BF16), low_grad, CONTRACT_COLS)
        turn = dy.astype(BF16).astype(F32) * scan_ref[at, :]
        turn = turn - d_weighted * weighted.astype(BF16).astype(F32)
        turn = turn + jnp.where(final_row, jnp.sum(grad * after, axis=0, keepdims=True), 0.0)
        d_run[at, :] += split_sum(turn, selector)
        d_step[at, :] += split_sum(d_weighted * x, selector)
        pre, shifted = conv_span(pad, same, row, taps, bias)
        d_act = (d_weighted * size + skip * dy) * silu_grad(pre)
        d_pre[at, :] = d_act
        taps_ref[...] += tap_sums(d_act, shifted)

    loop(spans, span)

    def keep(q, total):
        low_ref[pl.ds(span_start(q), ROWS), :] = total.astype(BF16)

        @pl.when(q == spans - 1)
        def _():
            tail_ref[...] = total[ROWS - RIM :]

    def keep_rim(total):
        rim_ref[...] = total

    conv_back(pad, d_pre, same, taps, spans, keep, keep_rim)

    @pl.when(pair == pl.num_programs(0) - 1)
    def _():
        for part in range(2):
            lanes = slice(part * LANES, (part + 1) * LANES)
            pad[0:RIM, :] = rim_ss_ref[:, lanes]
            pad[RIM:, :] = ss_ref[:, lanes]
            part_taps, part_bias = conv_ss_ref[0:4, lanes], conv_ss_ref[4:5, lanes]
            taps_ss_ref[:, lanes] = jnp.zeros((8, LANES), F32)

            def shared(q):
                row = span_start(q)
                at = pl.ds(row, ROWS)
                pre, shifted = conv_span(pad, same, row, part_taps, part_bias)
                d_act = d_bc[at, lanes] * silu_grad(pre)
                d_pre[at, :] = d_act
                taps_ss_ref[:, lanes] += tap_sums(d_act, shifted)

            loop(spans, shared)

            def keep_ss(q, total):
                low_ss_ref[pl.ds(span_start(q), ROWS), lanes] = total.astype(BF16)

                @pl.when(q == spans - 1)
                def _():
                    tail_ss_ref[:, lanes] = total[ROWS - RIM :]

            def keep_rim_ss(total):
                rim_ss_out_ref[:, lanes] = total

            conv_back(pad, d_pre, same, part_taps, spans, keep_ss, keep_rim_ss)

        step_bias, rate = heads_ref[0:1, :], heads_ref[1:2, :]
        small_ref[...] = jnp.zeros_like(small_ref)
        tri_t = upper_ones()

        def steps(q):
            at = pl.ds(span_start(q), ROWS)
            d_decay = sum(dot(tri_t, part) for part in three_parts(d_run[at, :]))
            slope = sigmoid(ss_ref[at, 2 * LANES :] + step_bias)
            d_raw = (d_step[at, :] - d_decay * rate) * slope
            low_ss_ref[at, 2 * LANES :] = d_raw.astype(BF16)
            small_ref[0:1] += jnp.sum(d_raw, axis=0, keepdims=True)
            small_ref[1:2] -= jnp.sum(d_decay * step_ref[at, :] * rate, axis=0, keepdims=True)

        loop(spans, steps)


def whole(shape):
    return pl.BlockSpec(shape, lambda j: (0,) * len(shape))


def columns(rows, width=LANES):
    return pl.BlockSpec((rows, width), lambda j: (0, j))


def stacks(count, rows):
    return pl.BlockSpec((count, rows, LANES), lambda j: (0, 0, j))


def params():
    return pltpu.CompilerParams(vmem_limit_bytes=VMEM_BYTES, dimension_semantics=("arbitrary",))


def shaped(shape, dtype):
    return jax.ShapeDtypeStruct(shape, dtype)


def scratch(*shape, dtype=F32):
    return pltpu.VMEM(shape, dtype)


class Sizes:
    def __init__(self, rows, inner, heads):
        self.rows, self.inner, self.heads = rows, inner, heads
        self.spans, self.pairs = rows // ROWS, inner // LANES
        self.width = max(8, heads)


def forward_states(s, value_in, ss, rim_v, rim_ss, cols, conv_v, conv_ss, heads):
    return pl.pallas_call(
        forward_states_kernel,
        grid=(s.pairs,),
        in_specs=[
            columns(s.rows), whole((s.rows, 3 * LANES)), columns(RIM), whole((RIM, 3 * LANES)),
            whole((s.rows, 8)), columns(8), whole((8, 2 * LANES)), whole((8, LANES)),
        ],
        out_specs=[
            columns(s.rows), whole((s.rows, 4 * LANES)), whole((s.rows, LANES)), whole((s.rows, LANES)),
            whole((s.spans, s.width, LANES)), stacks(s.spans, LANES), stacks(s.spans, 8),
        ],
        out_shape=[
            shaped((s.rows, s.inner), F32), shaped((s.rows, 4 * LANES), BF16),
            shaped((s.rows, LANES), F32), shaped((s.rows, LANES), F32),
            shaped((s.spans, s.width, LANES), F32),
            shaped((s.spans, LANES, s.inner), F32), shaped((s.spans, 8, s.inner), F32),
        ],
        scratch_shapes=[
            scratch(s.rows + RIM, LANES), scratch(3, s.rows, LANES), scratch(s.rows, LANES),
            scratch(s.rows, LANES), scratch(s.spans, LANES, 2 * ROWS, dtype=BF16),
        ],
        compiler_params=params(),
        name="forward_states",
    )(value_in, ss, rim_v, rim_ss, cols, conv_v, conv_ss, heads)


def forward_within(s, x, bc, step, run, run_t, cols, seg_rows):
    return pl.pallas_call(
        forward_within_kernel,
        grid=(s.pairs,),
        in_specs=[
            columns(s.rows), whole((s.rows, 4 * LANES)), whole((s.rows, LANES)), whole((s.rows, LANES)),
            whole((s.spans, s.width, LANES)), whole((s.rows, 8)), whole((s.spans, 8, LANES)),
        ],
        out_specs=columns(s.rows),
        out_shape=shaped((s.rows, s.inner), F32),
        scratch_shapes=[scratch(s.spans, ROWS, ROWS), scratch(s.spans, ROWS, ROWS)],
        compiler_params=params(),
        name="forward_within",
    )(x, bc, step, run, run_t, cols, seg_rows)


def forward_finish(s, y, x, z, dgo, state, decay, incoming, bc, run, cols, gains):
    return pl.pallas_call(
        forward_finish_kernel,
        grid=(s.pairs,),
        in_specs=[
            columns(s.rows), columns(s.rows), columns(s.rows), columns(s.rows),
            stacks(s.spans, LANES), stacks(s.spans, 8), columns(LANES),
            whole((s.rows, 4 * LANES)), whole((s.rows, LANES)), whole((s.rows, 8)), columns(8),
        ],
        out_specs=[columns(s.rows), whole((s.spans, 16, LANES))],
        out_shape=[shaped((s.rows, s.inner), F32), shaped((s.spans, 16, LANES), F32)],
        scratch_shapes=[scratch(s.rows, LANES)] * 3,
        compiler_params=params(),
        name="forward_finish",
    )(y, x, z, dgo, state, decay, incoming, bc, run, cols, gains)


def gate_back(s, inner_width, scan, x, z, dgo, sums, bc, run, cols, gains):
    def kernel(*refs):
        gate_back_kernel(inner_width, *refs)

    return pl.pallas_call(
        kernel,
        grid=(s.pairs,),
        in_specs=[
            columns(s.rows), columns(s.rows), columns(s.rows), columns(s.rows),
            whole((s.spans, 8, LANES)), whole((s.rows, 4 * LANES)), whole((s.rows, LANES)),
            whole((s.rows, 8)), columns(8),
        ],
        out_specs=[
            columns(s.rows), columns(s.rows), columns(s.rows), stacks(s.spans, LANES),
            stacks(s.spans, 8), columns(8),
        ],
        out_shape=[
            shaped((s.rows, s.inner), BF16), shaped((s.rows, s.inner), BF16),
            shaped((s.rows, s.inner), F32), shaped((s.spans, LANES, s.inner), F32),
            shaped((s.spans, 8, s.inner), F32), shaped((8, s.inner), F32),
        ],
        scratch_shapes=[scratch(s.rows, LANES)] * 3 + [scratch(s.spans, LANES, 2 * ROWS, dtype=BF16)],
        compiler_params=params(),
        name="gate_back",
    )(scan, x, z, dgo, sums, bc, run, cols, gains)


def backward_within(s, x, dy, bc, step, run, run_t, cols, seg_rows):
    return pl.pallas_call(
        backward_within_kernel,
        grid=(s.pairs,),
        in_specs=[
            columns(s.rows), columns(s.rows), whole((s.rows, 4 * LANES)), whole((s.rows, LANES)),
            whole((s.rows, LANES)), whole((s.spans, s.width, LANES)), whole((s.rows, 8)),
            whole((s.spans, 8, LANES)),
        ],
        out_specs=[columns(s.rows), whole((s.rows, 2 * LANES))],
        out_shape=[shaped((s.rows, s.inner), F32), shaped((s.rows, 2 * LANES), F32)],
        scratch_shapes=[scratch(s.spans, ROWS, ROWS)] * 3,
        compiler_params=params(),
        name="backward_within",
    )(x, dy, bc, step, run, run_t, cols, seg_rows)


def backward_finish(
    s, value_in, ss, rim_v, rim_ss, x, dy, scan, dxw, dbc, state, decay, incoming, grad, back, outgoing,
    bc, step, run, cols, conv_v, conv_ss, heads, gains,
):
    return pl.pallas_call(
        backward_finish_kernel,
        grid=(s.pairs,),
        in_specs=[
            columns(s.rows), whole((s.rows, 3 * LANES)), columns(RIM), whole((RIM, 3 * LANES)),
            columns(s.rows), columns(s.rows), columns(s.rows), columns(s.rows), whole((s.rows, 2 * LANES)),
            stacks(s.spans, LANES), stacks(s.spans, 8), columns(LANES),
            stacks(s.spans, LANES), stacks(s.spans, 8), columns(LANES),
            whole((s.rows, 4 * LANES)), whole((s.rows, LANES)), whole((s.rows, LANES)), whole((s.rows, 8)),
            columns(8), whole((8, 2 * LANES)), whole((8, LANES)), columns(8),
        ],
        out_specs=[
            columns(s.rows), columns(RIM), columns(RIM), columns(8),
            whole((s.rows, 3 * LANES)), whole((RIM, 2 * LANES)), whole((RIM, 2 * LANES)),
            whole((8, 2 * LANES)), whole((8, LANES)),
        ],
        out_shape=[
            shaped((s.rows, s.inner), BF16), shaped((RIM, s.inner), F32), shaped((RIM, s.inner), F32),
            shaped((8, s.inner), F32), shaped((s.rows, 3 * LANES), BF16), shaped((RIM, 2 * LANES), F32),
            shaped((RIM, 2 * LANES), F32), shaped((8, 2 * LANES), F32), shaped((8, LANES), F32),
        ],
        scratch_shapes=[
            scratch(s.rows + RIM, LANES), scratch(s.rows + RIM, LANES), scratch(3, s.rows + RIM, LANES),
            scratch(s.rows, LANES), scratch(s.rows, LANES), scratch(s.rows, LANES), scratch(s.rows, LANES),
            scratch(s.rows, 2 * LANES),
        ],
        compiler_params=params(),
        name="backward_finish",
    )(
        value_in, ss, rim_v, rim_ss, x, dy, scan, dxw, dbc, state, decay, incoming, grad, back, outgoing,
        bc, step, run, cols, conv_v, conv_ss, heads, gains,
    )


def from_behind(value, axis, steps):
    count = lax.axis_size(axis)
    initial, last = (max(0, -steps), min(count, count - steps))
    return lax.ppermute(value, axis, [(source, source + steps) for source in range(initial, last)])


def move_tiles(rows, index):
    tile_total = index.shape[0]
    shaped_rows = rows.reshape((tile_total, rows.shape[0] // tile_total) + rows.shape[1:])
    return jnp.take(shaped_rows, index, axis=0, mode="clip").reshape(rows.shape)


def carry_weights(decays, here, reverse):
    count = decays.shape[0]
    ids = jnp.arange(count, dtype=jnp.int32)
    if reverse:
        between = (ids[None, :] < ids[:, None]) & (ids[None, :] > here)
        reached = ids > here
    else:
        between = (ids[None, :] > ids[:, None]) & (ids[None, :] < here)
        reached = ids < here
    chain = jnp.prod(jnp.where(between[:, :, None], decays[None, :, :], 1.0), axis=1)
    return jnp.where(reached[:, None], chain, 0.0)


def padded_rows(parts, rows=8):
    stacked = jnp.concatenate([part.reshape(-1, part.shape[-1]) for part in parts], axis=0)
    return jnp.pad(stacked, ((0, rows - stacked.shape[0]), (0, 0)))


def local(
    tokens,
    packing,
    segment_ids,
    norm_gain,
    gate_proj,
    value_proj,
    shared_proj,
    step_proj,
    conv_value,
    conv_value_bias,
    conv_shared,
    conv_shared_bias,
    step_bias,
    log_decay,
    skip_gain,
    gated_gain,
    out_proj,
    cotangent,
):
    own_rows = tokens.shape[0]
    head_shards = lax.axis_size("head")
    seq_shards = lax.axis_size("seq")
    head_index = lax.axis_index("head")
    seq_index = lax.axis_index("seq")
    shard_rows = own_rows * head_shards
    inner_local = gate_proj.shape[1]
    heads_local = step_proj.shape[1]
    inner_width = inner_local * head_shards
    tile_rows = own_rows // seq_shards
    tile_count = shard_rows // tile_rows
    s = Sizes(shard_rows, inner_local, heads_local)

    packed_tiles = packing.reshape(-1, tile_rows)[:, 0] // tile_rows
    own_device = seq_index * head_shards + head_index
    seq_ids = jnp.arange(seq_shards, dtype=jnp.int32)
    own_tiles = own_device * seq_shards + seq_ids
    tile_match = (own_tiles[:, None] == packed_tiles[None, :]).astype(jnp.int32)
    tile_shard = jnp.arange(packed_tiles.shape[0], dtype=jnp.int32) // tile_count
    dest_shard = jnp.sum(tile_match * tile_shard[None, :], axis=1)
    send_index = jnp.sum(
        (dest_shard[None, :] == seq_ids[:, None]).astype(jnp.int32) * seq_ids[None, :], axis=1
    )
    own_packed = lax.dynamic_slice_in_dim(packed_tiles, seq_index * tile_count, tile_count, 0)
    source_device = own_packed // seq_shards
    arrival = source_device % head_shards * seq_shards + source_device // head_shards
    slot_ids = jnp.arange(tile_count, dtype=jnp.int32)
    back_index = jnp.sum(
        (arrival[None, :] == slot_ids[:, None]).astype(jnp.int32) * slot_ids[None, :], axis=1
    )

    shard_start = seq_index * shard_rows
    around = jnp.concatenate([jnp.full((RIM,), -1, jnp.int32), segment_ids])
    around = lax.dynamic_slice_in_dim(around, shard_start, shard_rows + RIM, 0)
    seg = around[RIM:]
    span_last = around[RIM - 1 :: ROWS]
    before_span = jnp.repeat(span_last[:-1], ROWS)
    end_of_span = jnp.repeat(span_last[1:], ROWS)
    facts = [around[RIM - k : RIM - k + shard_rows] == seg for k in (1, 2, 3)]
    facts += [before_span == seg, end_of_span == seg, seg, seg, seg]
    cols = jnp.stack([fact.astype(F32) for fact in facts], axis=1)
    seg_rows = jnp.broadcast_to(seg.astype(F32).reshape(s.spans, 1, ROWS), (s.spans, 8, ROWS))

    head_pad = ((0, 0), (0, LANES - heads_local))
    heads = padded_rows([step_bias, jnp.exp(log_decay)])
    heads = jnp.pad(heads, head_pad)
    conv_v = padded_rows([conv_value, conv_value_bias])
    conv_ss = padded_rows([conv_shared, conv_shared_bias])
    gains = padded_rows([jnp.repeat(skip_gain, inner_local // heads_local), gated_gain])
    ss_proj = jnp.concatenate([shared_proj, jnp.pad(step_proj, head_pad)], axis=1)

    tok_float = tokens.astype(F32)
    tok_rstd = lax.rsqrt(jnp.mean(tok_float * tok_float, axis=1, keepdims=True) + EPS)
    normed = (tok_float * tok_rstd * norm_gain[None, :]).astype(BF16)

    def to_shard(rows):
        sent = lax.all_to_all(
            move_tiles(rows, send_index), "seq", split_axis=0, concat_axis=0, tiled=True
        )
        return move_tiles(lax.all_gather(sent, "head", axis=0, tiled=True), arrival)

    packed_normed = to_shard(normed)
    packed_cot = to_shard(cotangent)

    value_in = dot(packed_normed, value_proj)
    ss = dot(packed_normed, ss_proj)
    gate_z = dot(packed_normed, gate_proj)
    rim = from_behind(
        jnp.concatenate([value_in[shard_rows - RIM :], ss[shard_rows - RIM :]], axis=1), "seq", 1
    )
    rim_v, rim_ss = rim[:, :inner_local], rim[:, inner_local:]
    x, bc, step, run, run_t, state, decay = forward_states(
        s, value_in, ss, rim_v, rim_ss, cols, conv_v, conv_ss, heads
    )
    ends = jnp.concatenate([state[s.spans - 1], decay[s.spans - 1]], axis=0)
    ends = lax.all_gather(ends, "seq")
    decays = ends[:, LANES, :]
    incoming = jnp.sum(
        carry_weights(decays, seq_index, False)[:, None, :] * ends[:, :LANES, :], axis=0
    )
    y = forward_within(s, x, bc, step, run, run_t, cols, seg_rows)
    dgo = dot(packed_cot, out_proj, CONTRACT_COLS)
    scan, sums = forward_finish(
        s, y, x, gate_z, dgo, state, decay, incoming, bc, run, cols, gains
    )
    sums = lax.psum(jnp.stack([sums[:, 0, :], sums[:, 8, :]], axis=1), "head")
    sums = jnp.pad(sums, ((0, 0), (0, 6), (0, 0)))
    gated_low, low_gate, dy, grad, back, gate_rows = gate_back(
        s, inner_width, scan, x, gate_z, dgo, sums, bc, run, cols, gains
    )
    branch = lax.psum_scatter(
        move_tiles(dot(gated_low, out_proj).astype(BF16), back_index),
        "head",
        scatter_dimension=0,
        tiled=True,
    ).astype(F32)
    grad_out_proj = lax.psum_scatter(
        dot(gated_low, packed_cot, CONTRACT_ROWS).astype(BF16), "seq", scatter_dimension=0, tiled=True
    ).astype(F32)
    starts = lax.all_gather(grad[0], "seq")
    outgoing = jnp.sum(carry_weights(decays, seq_index, True)[:, None, :] * starts, axis=0)
    dxw, dbc = backward_within(s, x, dy, bc, step, run, run_t, cols, seg_rows)
    low_value, tail, rim_out, taps_v, low_ss, tail_ss, rim_ss_out, taps_ss, small = backward_finish(
        s, value_in, ss, rim_v, rim_ss, x, dy, scan, dxw, dbc, state, decay, incoming, grad, back,
        outgoing, bc, step, run, cols, conv_v, conv_ss, heads, gains,
    )
    rim_back = from_behind(jnp.concatenate([rim_out, rim_ss_out], axis=1), "seq", -1)
    tail = (jnp.concatenate([tail, tail_ss], axis=1) + rim_back).astype(BF16)
    low_value = lax.dynamic_update_slice(low_value, tail[:, :inner_local], (shard_rows - RIM, 0))
    low_ss = lax.dynamic_update_slice(low_ss, tail[:, inner_local:], (shard_rows - RIM, 0))

    d_normed = (
        dot(low_gate, gate_proj, CONTRACT_COLS)
        + dot(low_value, value_proj, CONTRACT_COLS)
        + dot(low_ss, ss_proj, CONTRACT_COLS)
    )
    d_normed = lax.psum_scatter(
        move_tiles(d_normed.astype(BF16), back_index), "head", scatter_dimension=0, tiled=True
    ).astype(F32)
    gate_grads = dot(packed_normed, low_gate, CONTRACT_ROWS)
    value_grads = dot(packed_normed, low_value, CONTRACT_ROWS)
    ss_grads = dot(packed_normed, low_ss, CONTRACT_ROWS)
    grad_norm_rows = (
        jnp.sum(gate_grads * gate_proj.astype(F32), axis=1)
        + jnp.sum(value_grads * value_proj.astype(F32), axis=1)
        + jnp.sum(ss_grads * ss_proj.astype(F32), axis=1)
    )

    def over_seq(grads):
        return lax.psum_scatter(
            grads.astype(BF16), "seq", scatter_dimension=0, tiled=True
        ).astype(F32)

    grad_gate = over_seq(gate_grads)
    grad_value = over_seq(value_grads)
    grad_ss = lax.psum_scatter(ss_grads, "seq", scatter_dimension=0, tiled=True)
    grad_step_proj = grad_ss[:, 2 * LANES : 2 * LANES + heads_local]
    grad_shared = lax.psum(grad_ss[:, : 2 * LANES], "head")
    grad_shared = lax.all_gather(grad_shared.astype(BF16), "seq", axis=0, tiled=True).astype(F32)

    branch_back = lax.all_to_all(branch.astype(BF16), "seq", split_axis=0, concat_axis=0, tiled=True)
    normed_back = lax.all_to_all(d_normed.astype(BF16), "seq", split_axis=0, concat_axis=0, tiled=True)
    branch_given = move_tiles(branch_back, dest_shard).astype(F32)
    d_normed_given = move_tiles(normed_back, dest_shard).astype(F32)
    mixed_rows = (tok_float + branch_given).astype(BF16)
    scaled = d_normed_given * norm_gain[None, :]
    row_dot = jnp.sum(scaled * tok_float, axis=1, keepdims=True) / tokens.shape[1]
    d_tok = tok_rstd * scaled - tok_float * (tok_rstd * tok_rstd * tok_rstd * row_dot)
    grad_tokens = (cotangent.astype(F32) + d_tok).astype(BF16)

    per_head = [jnp.sum(gate_rows[1].reshape(heads_local, -1), axis=1)]
    per_head += [small[0, :heads_local], small[1, :heads_local]]
    pieces = [taps_v[:5].reshape(-1), gate_rows[0]] + per_head
    own_size = sum(piece.shape[0] for piece in pieces)
    shared_pieces = [taps_ss[:5].reshape(-1), grad_norm_rows]
    everything = lax.psum(jnp.concatenate(pieces + shared_pieces), "seq")
    shared_sums = lax.psum(everything[own_size:], "head")
    own_taps = everything[: 5 * inner_local].reshape(5, inner_local)
    rest = everything[5 * inner_local : own_size]
    grad_gated = rest[:inner_local]
    rest = rest[inner_local:]
    grad_skip = rest[:heads_local]
    grad_step_bias = rest[heads_local : 2 * heads_local]
    grad_log_decay = rest[2 * heads_local :]
    shared_taps = shared_sums[: 10 * LANES].reshape(5, 2 * LANES)
    grad_norm_gain = shared_sums[10 * LANES :] / norm_gain
    return (
        mixed_rows,
        grad_tokens,
        grad_norm_gain,
        grad_gate,
        grad_value,
        grad_shared,
        grad_step_proj,
        own_taps[:4],
        own_taps[4],
        shared_taps[:4],
        shared_taps[4],
        grad_step_bias,
        grad_log_decay,
        grad_skip,
        grad_gated,
        grad_out_proj,
    )


def solution(mesh):
    placed = (
        P(("seq", "head"), None),
        P(),
        P(),
        P(),
        P(None, "head"),
        P(None, "head"),
        P(),
        P(None, "head"),
        P(None, "head"),
        P("head"),
        P(),
        P(),
        P("head"),
        P("head"),
        P("head"),
        P("head"),
        P("head", None),
        P(("seq", "head"), None),
    )
    return jax.shard_map(
        local,
        mesh=mesh,
        in_specs=placed,
        out_specs=(
            P(("seq", "head"), None),
            P(("seq", "head"), None),
            P(),
            P("seq", "head"),
            P("seq", "head"),
            P(),
            P("seq", "head"),
            P(None, "head"),
            P("head"),
            P(),
            P(),
            P("head"),
            P("head"),
            P("head"),
            P("head"),
            P(("head", "seq"), None),
        ),
        check_vma=False,
    )
```

```python
import jax
import jax.numpy as jnp
from jax import lax
from jax.experimental import pallas as pl
from jax.experimental.pallas import tpu as pltpu
from jax.sharding import PartitionSpec as P

EPS = 1e-05
ROWS = 128
LANES = 128
HALF = 64
RIM = 8
FAR = -1e30
UNROLL = 8
F32 = jnp.float32
BF16 = jnp.bfloat16
VMEM_BYTES = 56 * 1024 * 1024
CONTRACT_ROWS = (((0,), (0,)), ((), ()))
CONTRACT_COLS = (((1,), (1,)), ((), ()))


def dot(a, b, dims=(((1,), (0,)), ((), ()))):
    return lax.dot_general(a, b, dims, preferred_element_type=F32)


def two_parts(x):
    upper = x.astype(BF16)
    return upper, (x - upper.astype(F32)).astype(BF16)


def three_parts(x):
    upper, rest = x.astype(BF16), x
    rest = x - upper.astype(F32)
    middle = rest.astype(BF16)
    return upper, middle, (rest - middle.astype(F32)).astype(BF16)


def in_two(x):
    return jnp.concatenate(two_parts(x), axis=1)


def twice(x):
    return jnp.concatenate([x, x], axis=0)


def b_parts(bc_ref, at):
    return bc_ref[at, : 2 * LANES]


def c_parts(bc_ref, at):
    return bc_ref[at, 2 * LANES :]


def cross_product(bc_ref, at):
    b, c = b_parts(bc_ref, at), c_parts(bc_ref, at)
    upper = jnp.concatenate([b[:, :LANES], b[:, :LANES]], axis=1)
    return dot(c, upper, CONTRACT_COLS) + dot(c[:, :LANES], b[:, LANES:], CONTRACT_COLS)


def lane_ids(rows):
    return lax.broadcasted_iota(jnp.int32, (rows, LANES), 1)


def row_ids(rows):
    return lax.broadcasted_iota(jnp.int32, (rows, LANES), 0)


def head_cols(block, pair):
    shift = lax.rem(LANES - 2 * pair, LANES)
    turned = pltpu.roll(block, shift, axis=1)
    first = jnp.broadcast_to(turned[:, 0:1], block.shape)
    second = jnp.broadcast_to(turned[:, 1:2], block.shape)
    return first, second


def paired(first, second):
    return jnp.where(lane_ids(first.shape[0]) < HALF, first, second)


def head_selector(pair):
    lane = row_ids(LANES)
    head = 2 * pair + jnp.where(lane < HALF, 0, 1)
    return (lane_ids(LANES) == head).astype(F32).astype(BF16)


def split_sum(x, selector):
    upper, lower = two_parts(x)
    stacked = jnp.concatenate([upper, lower], axis=1)
    return dot(stacked, jnp.concatenate([selector, selector], axis=0))


def lower_ones():
    return (row_ids(ROWS) >= lane_ids(ROWS)).astype(F32).astype(BF16)


def upper_ones():
    return (row_ids(ROWS) <= lane_ids(ROWS)).astype(F32).astype(BF16)


def spread(ref, row, col):
    return jnp.broadcast_to(ref[pl.ds(row, ROWS), col : col + 1], (ROWS, LANES))


def softplus(x):
    return jnp.maximum(x, 0.0) + jnp.log1p(jnp.exp(-jnp.abs(x)))


def sigmoid(x):
    return 1.0 / (1.0 + jnp.exp(-x))


def span_start(q):
    return pl.multiple_of(q * ROWS, ROWS)


def loop(count, body):
    def step(q, carry):
        body(q)
        return carry

    lax.fori_loop(0, count, step, 0, unroll=UNROLL)


def conv_span(pad_ref, same_ref, row, taps, bias):
    long = pad_ref[pl.ds(row, ROWS + RIM), :]
    total = bias + taps[3:4] * long[RIM:]
    shifted = []
    for back in (1, 2, 3):
        moved = pltpu.roll(long, back, axis=0)[RIM:]
        moved = moved * same_ref[back - 1, pl.ds(row, ROWS), :]
        shifted.append(moved)
        total = total + taps[3 - back : 4 - back] * moved
    return total, [long[RIM:]] + shifted


def forward_states_kernel(
    value_ref, ss_ref, rim_v_ref, rim_ss_ref, cols_ref, conv_ref, conv_ss_ref, heads_ref,
    x_ref, bc_ref, step_ref, run_ref, run_t_ref, state_ref, decay_ref,
    pad, same, cont, last, bt,
):
    pair = pl.program_id(0)
    rows = value_ref.shape[0]
    spans = rows // ROWS
    width = run_t_ref.shape[1]

    @pl.when(pair == 0)
    def _():
        def masks(q):
            row = span_start(q)
            for k in range(3):
                same[k, pl.ds(row, ROWS), :] = spread(cols_ref, row, k)
            cont[pl.ds(row, ROWS), :] = spread(cols_ref, row, 3)
            last[pl.ds(row, ROWS), :] = spread(cols_ref, row, 4)

        loop(spans, masks)
        for part in range(2):
            lanes = slice(part * LANES, (part + 1) * LANES)
            pad[0:RIM, :] = rim_ss_ref[:, lanes]
            pad[RIM:, :] = ss_ref[:, lanes]
            taps, bias = conv_ss_ref[0:4, lanes], conv_ss_ref[4:5, lanes]

            def shared(q):
                row = span_start(q)
                pre, _ = conv_span(pad, same, row, taps, bias)
                act = pre * sigmoid(pre)
                bc_ref[pl.ds(row, ROWS), 2 * part * LANES : 2 * (part + 1) * LANES] = in_two(act)
                if part == 0:
                    bt[q] = in_two(jnp.transpose(act))

            loop(spans, shared)

        bias, rate = heads_ref[0:1, :], heads_ref[1:2, :]
        tri, tri_t = lower_ones(), upper_ones()

        def steps(q):
            row = span_start(q)
            size = softplus(ss_ref[pl.ds(row, ROWS), 2 * LANES :] + bias)
            step_ref[pl.ds(row, ROWS), :] = size
            parts = three_parts(-size * rate)
            run_ref[pl.ds(row, ROWS), :] = sum(dot(tri, part) for part in parts)
            turned = sum(dot(part, tri_t, CONTRACT_ROWS) for part in parts)
            run_t_ref[q] = turned[:width]

        loop(spans, steps)

    pad[0:RIM, :] = rim_v_ref[...]
    pad[RIM:, :] = value_ref[...]
    taps, bias = conv_ref[0:4], conv_ref[4:5]

    def span(q, carry):
        state, decay = carry
        row = span_start(q)
        at = pl.ds(row, ROWS)
        pre, _ = conv_span(pad, same, row, taps, bias)
        x = pre * sigmoid(pre)
        x_ref[at, :] = x
        size = paired(*head_cols(step_ref[at, :], pair))
        run = paired(*head_cols(run_ref[at, :], pair))
        enter = jnp.exp(run[ROWS - 1 :]) * cont[pl.ds(row + ROWS - 8, 8), :][7:8]
        to_end = jnp.exp(run[ROWS - 1 :] - run) * last[at, :]
        state = state * enter + dot(bt[q], twice((x * size * to_end).astype(BF16)))
        decay = decay * enter
        state_ref[q] = state
        decay_ref[q] = jnp.broadcast_to(decay, (8, LANES))
        return state, decay

    lax.fori_loop(
        0, spans, span, (jnp.zeros((LANES, LANES), F32), jnp.ones((1, LANES), F32)),
        unroll=UNROLL,
    )


def span_masks(cols_ref, seg_rows_ref, bias_ref, spans):
    causal = row_ids(ROWS) >= lane_ids(ROWS)

    def mask(q):
        own = spread(cols_ref, span_start(q), 5)
        other = jnp.broadcast_to(seg_rows_ref[q, 0:1, :], (ROWS, ROWS))
        bias_ref[q] = jnp.where(causal & (own == other), 0.0, FAR)

    loop(spans, mask)


def decay_pair(run_ref, run_t_ref, mask_ref, q, pair):
    first, second = head_cols(run_ref[pl.ds(span_start(q), ROWS), :], pair)
    rows = run_t_ref[q, pl.ds(2 * pair, 2), :]
    mask = mask_ref[q]
    return jnp.exp(first - rows[0:1] + mask), jnp.exp(second - rows[1:2] + mask)


def heads_apart(x):
    lane = lane_ids(x.shape[0])
    zero = jnp.zeros_like(x)
    return jnp.concatenate([jnp.where(lane < HALF, x, zero), jnp.where(lane < HALF, zero, x)], axis=0)


def forward_within_kernel(
    x_ref, bc_ref, step_ref, run_ref, run_t_ref, cols_ref, seg_rows_ref, y_ref, mask, cross
):
    pair = pl.program_id(0)
    spans = x_ref.shape[0] // ROWS

    @pl.when(pair == 0)
    def _():
        span_masks(cols_ref, seg_rows_ref, mask, spans)

        def products(q):
            at = pl.ds(span_start(q), ROWS)
            cross[q] = cross_product(bc_ref, at)

        loop(spans, products)

    def span(q):
        at = pl.ds(span_start(q), ROWS)
        size = paired(*head_cols(step_ref[at, :], pair))
        weighted = x_ref[at, :] * size
        first, second = decay_pair(run_ref, run_t_ref, mask, q, pair)
        mix = jnp.concatenate([first * cross[q], second * cross[q]], axis=1).astype(BF16)
        y_ref[at, :] = dot(mix, heads_apart(weighted).astype(BF16))

    loop(spans, span)


def entering(state_ref, decay_ref, incoming, q, before):
    at = jnp.maximum(before, 0)
    local = state_ref[at] + decay_ref[at, 0:1, :] * incoming
    return jnp.where(before >= 0, local, incoming)


def row_sums(acc_ref, out_ref, base, spans):
    ones = jnp.ones((8, LANES), BF16)

    def total(q):
        parts = three_parts(acc_ref[pl.ds(span_start(q), ROWS), :])
        out_ref[q, base : base + 8, :] = sum(dot(ones, part, CONTRACT_COLS) for part in parts)

    loop(spans, total)


def forward_finish_kernel(
    y_ref, x_ref, z_ref, dgo_ref, state_ref, decay_ref, in_ref, bc_ref, run_ref, cols_ref, gains_ref,
    scan_ref, sums_ref, cont, squares, inner,
):
    pair = pl.program_id(0)
    spans = y_ref.shape[0] // ROWS

    @pl.when(pair == 0)
    def _():
        def masks(q):
            row = span_start(q)
            cont[pl.ds(row, ROWS), :] = spread(cols_ref, row, 3)

        loop(spans, masks)
        squares[...] = jnp.zeros_like(squares)
        inner[...] = jnp.zeros_like(inner)

    incoming = in_ref[...]
    skip, gain = gains_ref[0:1], gains_ref[1:2]

    def span(q):
        at = pl.ds(span_start(q), ROWS)
        run = paired(*head_cols(run_ref[at, :], pair))
        state = entering(state_ref, decay_ref, incoming, q, q - 1)
        upper, lower = two_parts(state)
        c = c_parts(bc_ref, at)
        carried = dot(c, twice(upper)) + dot(c[:, :LANES], lower)
        scan = y_ref[at, :] + carried * (jnp.exp(run) * cont[at, :])
        scan_ref[at, :] = scan
        z = z_ref[at, :]
        gated = (scan + skip * x_ref[at, :]) * (z * sigmoid(z))
        squares[at, :] += gated * gated
        inner[at, :] += gain * dgo_ref[at, :] * gated

    loop(spans, span)

    @pl.when(pair == pl.num_programs(0) - 1)
    def _():
        row_sums(squares, sums_ref, 0, spans)
        row_sums(inner, sums_ref, 8, spans)


def gate_back_kernel(
    inner_width,
    scan_ref, x_ref, z_ref, dgo_ref, sums_ref, bc_ref, run_ref, cols_ref, gains_ref,
    out_ref, dz_ref, dy_ref, grad_ref, decay_ref, rows_ref,
    cont, rstd, coef, ct,
):
    pair = pl.program_id(0)
    spans = scan_ref.shape[0] // ROWS

    @pl.when(pair == 0)
    def _():
        def masks(q):
            row = span_start(q)
            at = pl.ds(row, ROWS)
            cont[at, :] = spread(cols_ref, row, 3)
            ct[q] = jnp.concatenate(
                [
                    jnp.transpose(bc_ref[at, k * LANES : (k + 1) * LANES].astype(F32)).astype(BF16)
                    for k in (2, 3)
                ],
                axis=1,
            )
            square = jnp.broadcast_to(sums_ref[q, 0:1, :], (ROWS, LANES))
            cross = jnp.broadcast_to(sums_ref[q, 1:2, :], (ROWS, LANES))
            root = lax.rsqrt(square / inner_width + EPS)
            rstd[at, :] = jnp.transpose(root)
            coef[at, :] = jnp.transpose(root * root * root * cross / inner_width)

        loop(spans, masks)

    skip, gain = gains_ref[0:1], gains_ref[1:2]
    rows_ref[...] = jnp.zeros_like(rows_ref)

    def span(k, carry):
        leaving, decay = carry
        q = spans - 1 - k
        at = pl.ds(span_start(q), ROWS)
        x, z, dgo = x_ref[at, :], z_ref[at, :], dgo_ref[at, :]
        scanned = scan_ref[at, :] + skip * x
        gate = sigmoid(z)
        silu = z * gate
        gated = scanned * silu
        normed = gated * rstd[at, :]
        out_ref[at, :] = (normed * gain).astype(BF16)
        d_gated = rstd[at, :] * (dgo * gain) - gated * coef[at, :]
        d_scan = d_gated * silu
        dz_ref[at, :] = (d_gated * scanned * (gate * (1.0 + z * (1.0 - gate)))).astype(BF16)
        dy_ref[at, :] = d_scan
        rows_ref[0:1] += jnp.sum(dgo * normed, axis=0, keepdims=True)
        rows_ref[1:2] += jnp.sum(d_scan * x, axis=0, keepdims=True)
        run = paired(*head_cols(run_ref[at, :], pair))
        enter = jnp.exp(run) * cont[at, :]
        upper, lower = two_parts(d_scan * enter)
        turned = ct[q]
        leaving = leaving * enter[ROWS - 1 :] + dot(turned, twice(upper)) + dot(turned[:, :ROWS], lower)
        decay = decay * enter[ROWS - 1 :]
        grad_ref[q] = leaving
        decay_ref[q] = jnp.broadcast_to(decay, (8, LANES))
        return leaving, decay

    lax.fori_loop(
        0, spans, span, (jnp.zeros((LANES, LANES), F32), jnp.ones((1, LANES), F32)),
        unroll=UNROLL,
    )


def backward_within_kernel(
    x_ref, dy_ref, bc_ref, step_ref, run_ref, run_t_ref, cols_ref, seg_rows_ref,
    dxw_ref, dbc_ref, mask, cross, d_cross,
):
    pair = pl.program_id(0)
    spans = x_ref.shape[0] // ROWS

    @pl.when(pair == 0)
    def _():
        span_masks(cols_ref, seg_rows_ref, mask, spans)

        def products(q):
            at = pl.ds(span_start(q), ROWS)
            cross[q] = cross_product(bc_ref, at)
            d_cross[q] = jnp.zeros((ROWS, ROWS), F32)

        loop(spans, products)

    def span(q):
        at = pl.ds(span_start(q), ROWS)
        size = paired(*head_cols(step_ref[at, :], pair))
        weighted = (x_ref[at, :] * size).astype(BF16)
        first, second = decay_pair(run_ref, run_t_ref, mask, q, pair)
        dy, dy_rest = two_parts(dy_ref[at, :])
        apart = heads_apart(dy)
        both = jnp.concatenate([apart, heads_apart(dy_rest)], axis=1)
        d_mix = dot(both, jnp.concatenate([weighted, weighted], axis=1), CONTRACT_COLS)
        d_cross[q] += first * d_mix[:ROWS] + second * d_mix[ROWS:]
        mix = jnp.concatenate([first * cross[q], second * cross[q]], axis=0).astype(BF16)
        dxw_ref[at, :] = dot(mix, apart, CONTRACT_ROWS)

    loop(spans, span)

    @pl.when(pair == pl.num_programs(0) - 1)
    def _():
        def shared(q):
            at = pl.ds(span_start(q), ROWS)
            grad = d_cross[q].astype(BF16)
            b, c = b_parts(bc_ref, at), c_parts(bc_ref, at)
            both = dot(grad, c, CONTRACT_ROWS)
            dbc_ref[at, :LANES] = both[:, :LANES] + both[:, LANES:]
            both = dot(grad, b)
            dbc_ref[at, LANES:] = both[:, :LANES] + both[:, LANES:]

        loop(spans, shared)


def conv_back(pad_ref, d_pre, same, taps, spans, store, rim_store):
    def span(q):
        at = pl.ds(span_start(q), ROWS + RIM)
        long = d_pre[at, :]
        total = taps[3:4] * long[:ROWS]
        for ahead in (1, 2, 3):
            masked = long * same[ahead - 1, at, :]
            moved = pltpu.roll(masked, ROWS + RIM - ahead, axis=0)[:ROWS]
            total = total + taps[3 - ahead : 4 - ahead] * moved
        store(q, total)

    loop(spans, span)
    head = d_pre[0:RIM, :]
    total = jnp.zeros((RIM, LANES), F32)
    for ahead in (1, 2, 3):
        masked = head * same[ahead - 1, 0:RIM, :]
        both = jnp.concatenate([jnp.zeros((RIM, LANES), F32), masked], axis=0)
        total = total + taps[3 - ahead : 4 - ahead] * pltpu.roll(both, 2 * RIM - ahead, axis=0)[:RIM]
    rim_store(total)


def tap_sums(d_pre, shifted):
    sums = [jnp.sum(d_pre * shifted[3 - k], axis=0, keepdims=True) for k in range(4)]
    sums.append(jnp.sum(d_pre, axis=0, keepdims=True))
    return jnp.concatenate(sums + [jnp.zeros((3, LANES), F32)], axis=0)


def silu_grad(pre):
    gate = sigmoid(pre)
    return gate * (1.0 + pre * (1.0 - gate))


def backward_finish_kernel(
    value_ref, ss_ref, rim_v_ref, rim_ss_ref, x_ref, dy_ref, scan_ref, dxw_ref, dbc_ref,
    state_ref, decay_ref, in_ref, grad_ref, back_ref, out_ref,
    bc_ref, step_ref, run_ref, cols_ref, conv_ref, conv_ss_ref, heads_ref, gains_ref,
    low_ref, tail_ref, rim_ref, taps_ref, low_ss_ref, tail_ss_ref, rim_ss_out_ref, taps_ss_ref, small_ref,
    pad, d_pre, same, cont, last, d_run, d_step, d_bc,
):
    pair = pl.program_id(0)
    rows = value_ref.shape[0]
    spans = rows // ROWS

    @pl.when(pair == 0)
    def _():
        def masks(q):
            row = span_start(q)
            for k in range(3):
                same[k, pl.ds(row, ROWS), :] = spread(cols_ref, row, k)
            cont[pl.ds(row, ROWS), :] = spread(cols_ref, row, 3)
            last[pl.ds(row, ROWS), :] = spread(cols_ref, row, 4)

        loop(spans, masks)
        same[:, rows:, :] = jnp.zeros((3, RIM, LANES), F32)
        d_pre[rows:, :] = jnp.zeros((RIM, LANES), F32)
        d_run[...] = jnp.zeros_like(d_run)
        d_step[...] = jnp.zeros_like(d_step)
        d_bc[...] = dbc_ref[...]

    pad[0:RIM, :] = rim_v_ref[...]
    pad[RIM:, :] = value_ref[...]
    taps, bias = conv_ref[0:4], conv_ref[4:5]
    skip = gains_ref[0:1]
    incoming, outgoing = in_ref[...], out_ref[...]
    selector = head_selector(pair)
    taps_ref[...] = jnp.zeros_like(taps_ref)
    final_row = row_ids(ROWS) == ROWS - 1

    def span(q):
        row = span_start(q)
        at = pl.ds(row, ROWS)
        x, dy = x_ref[at, :], dy_ref[at, :]
        size = paired(*head_cols(step_ref[at, :], pair))
        run = paired(*head_cols(run_ref[at, :], pair))
        enter = jnp.exp(run) * cont[at, :]
        to_end = jnp.exp(run[ROWS - 1 :] - run) * last[at, :]
        state, state_rest = two_parts(entering(state_ref, decay_ref, incoming, q, q - 1))
        after = state_ref[q] + decay_ref[q, 0:1, :] * incoming
        ahead = jnp.minimum(q + 1, spans - 1)
        grad = jnp.where(
            q + 1 < spans, grad_ref[ahead] + back_ref[ahead, 0:1, :] * outgoing, outgoing
        )
        weighted = x * size
        low_grad = grad.astype(BF16)
        d_weighted = dxw_ref[at, :] + to_end * dot(b_parts(bc_ref, at), twice(low_grad))
        entered = in_two(dy * enter)
        d_bc[at, LANES:] += dot(
            entered, jnp.concatenate([state, state], axis=1), CONTRACT_COLS
        ) + dot(entered[:, :LANES], state_rest, CONTRACT_COLS)
        d_bc[at, :LANES] += dot((weighted * to_end).astype(BF16), low_grad, CONTRACT_COLS)
        turn = dy.astype(BF16).astype(F32) * scan_ref[at, :]
        turn = turn - d_weighted * weighted.astype(BF16).astype(F32)
        turn = turn + jnp.where(final_row, jnp.sum(grad * after, axis=0, keepdims=True), 0.0)
        d_run[at, :] += split_sum(turn, selector)
        d_step[at, :] += split_sum(d_weighted * x, selector)
        pre, shifted = conv_span(pad, same, row, taps, bias)
        d_act = (d_weighted * size + skip * dy) * silu_grad(pre)
        d_pre[at, :] = d_act
        taps_ref[...] += tap_sums(d_act, shifted)

    loop(spans, span)

    def keep(q, total):
        low_ref[pl.ds(span_start(q), ROWS), :] = total.astype(BF16)

        @pl.when(q == spans - 1)
        def _():
            tail_ref[...] = total[ROWS - RIM :]

    def keep_rim(total):
        rim_ref[...] = total

    conv_back(pad, d_pre, same, taps, spans, keep, keep_rim)

    @pl.when(pair == pl.num_programs(0) - 1)
    def _():
        for part in range(2):
            lanes = slice(part * LANES, (part + 1) * LANES)
            pad[0:RIM, :] = rim_ss_ref[:, lanes]
            pad[RIM:, :] = ss_ref[:, lanes]
            part_taps, part_bias = conv_ss_ref[0:4, lanes], conv_ss_ref[4:5, lanes]
            taps_ss_ref[:, lanes] = jnp.zeros((8, LANES), F32)

            def shared(q):
                row = span_start(q)
                at = pl.ds(row, ROWS)
                pre, shifted = conv_span(pad, same, row, part_taps, part_bias)
                d_act = d_bc[at, lanes] * silu_grad(pre)
                d_pre[at, :] = d_act
                taps_ss_ref[:, lanes] += tap_sums(d_act, shifted)

            loop(spans, shared)

            def keep_ss(q, total):
                low_ss_ref[pl.ds(span_start(q), ROWS), lanes] = total.astype(BF16)

                @pl.when(q == spans - 1)
                def _():
                    tail_ss_ref[:, lanes] = total[ROWS - RIM :]

            def keep_rim_ss(total):
                rim_ss_out_ref[:, lanes] = total

            conv_back(pad, d_pre, same, part_taps, spans, keep_ss, keep_rim_ss)

        step_bias, rate = heads_ref[0:1, :], heads_ref[1:2, :]
        small_ref[...] = jnp.zeros_like(small_ref)
        tri_t = upper_ones()

        def steps(q):
            at = pl.ds(span_start(q), ROWS)
            d_decay = sum(dot(tri_t, part) for part in three_parts(d_run[at, :]))
            slope = sigmoid(ss_ref[at, 2 * LANES :] + step_bias)
            d_raw = (d_step[at, :] - d_decay * rate) * slope
            low_ss_ref[at, 2 * LANES :] = d_raw.astype(BF16)
            small_ref[0:1] += jnp.sum(d_raw, axis=0, keepdims=True)
            small_ref[1:2] -= jnp.sum(d_decay * step_ref[at, :] * rate, axis=0, keepdims=True)

        loop(spans, steps)


def store_tiles(slots_ref, out_ref, value, scatter):
    if not scatter:
        out_ref[...] = value
        return
    tile = value.shape[0] // slots_ref.shape[0]
    for k in range(slots_ref.shape[0]):
        start = pl.multiple_of(slots_ref[k] * tile, tile)
        out_ref[pl.ds(start, tile), :] = value[k * tile : (k + 1) * tile]


def branch_kernel(scatter, slots_ref, rows_ref, weight_ref, out_ref):
    store_tiles(slots_ref, out_ref, dot(rows_ref[...], weight_ref[...]).astype(BF16), scatter)


def normed_grad_kernel(
    scatter, slots_ref, gate_ref, value_ref, ss_ref, gate_w, value_w, ss_w, normed_ref, out_ref, diag_ref
):
    total = dot(gate_ref[...], gate_w[...], CONTRACT_COLS)
    total = total + dot(value_ref[...], value_w[...], CONTRACT_COLS)
    total = total + dot(ss_ref[...], ss_w[...], CONTRACT_COLS)
    store_tiles(slots_ref, out_ref, total.astype(BF16), scatter)
    sums = jnp.sum(total * normed_ref[...].astype(F32), axis=0, keepdims=True)
    diag_ref[...] = jnp.broadcast_to(sums, diag_ref.shape)


def whole(shape):
    return pl.BlockSpec(shape, lambda j: (0,) * len(shape))


def columns(rows, width=LANES):
    return pl.BlockSpec((rows, width), lambda j: (0, j))


def stacks(count, rows):
    return pl.BlockSpec((count, rows, LANES), lambda j: (0, 0, j))


def params():
    return pltpu.CompilerParams(vmem_limit_bytes=VMEM_BYTES, dimension_semantics=("arbitrary",))


def shaped(shape, dtype):
    return jax.ShapeDtypeStruct(shape, dtype)


def scratch(*shape, dtype=F32):
    return pltpu.VMEM(shape, dtype)


class Sizes:
    def __init__(self, rows, inner, heads):
        self.rows, self.inner, self.heads = rows, inner, heads
        self.spans, self.pairs = rows // ROWS, inner // LANES
        self.width = max(8, heads)

    def cost(self):
        cells = self.rows * self.inner
        return pl.CostEstimate(flops=20000 * cells, bytes_accessed=16 * cells, transcendentals=cells)


def forward_states(s, value_in, ss, rim_v, rim_ss, cols, conv_v, conv_ss, heads):
    return pl.pallas_call(
        forward_states_kernel,
        grid=(s.pairs,),
        in_specs=[
            columns(s.rows), whole((s.rows, 3 * LANES)), columns(RIM), whole((RIM, 3 * LANES)),
            whole((s.rows, 8)), columns(8), whole((8, 2 * LANES)), whole((8, LANES)),
        ],
        out_specs=[
            columns(s.rows), whole((s.rows, 4 * LANES)), whole((s.rows, LANES)), whole((s.rows, LANES)),
            whole((s.spans, s.width, LANES)), stacks(s.spans, LANES), stacks(s.spans, 8),
        ],
        out_shape=[
            shaped((s.rows, s.inner), F32), shaped((s.rows, 4 * LANES), BF16),
            shaped((s.rows, LANES), F32), shaped((s.rows, LANES), F32),
            shaped((s.spans, s.width, LANES), F32),
            shaped((s.spans, LANES, s.inner), F32), shaped((s.spans, 8, s.inner), F32),
        ],
        scratch_shapes=[
            scratch(s.rows + RIM, LANES), scratch(3, s.rows, LANES), scratch(s.rows, LANES),
            scratch(s.rows, LANES), scratch(s.spans, LANES, 2 * ROWS, dtype=BF16),
        ],
        compiler_params=params(),
        cost_estimate=s.cost(),
        name="forward_states",
    )(value_in, ss, rim_v, rim_ss, cols, conv_v, conv_ss, heads)


def forward_within(s, x, bc, step, run, run_t, cols, seg_rows):
    return pl.pallas_call(
        forward_within_kernel,
        grid=(s.pairs,),
        in_specs=[
            columns(s.rows), whole((s.rows, 4 * LANES)), whole((s.rows, LANES)), whole((s.rows, LANES)),
            whole((s.spans, s.width, LANES)), whole((s.rows, 8)), whole((s.spans, 8, LANES)),
        ],
        out_specs=columns(s.rows),
        out_shape=shaped((s.rows, s.inner), F32),
        scratch_shapes=[scratch(s.spans, ROWS, ROWS), scratch(s.spans, ROWS, ROWS)],
        compiler_params=params(),
        cost_estimate=s.cost(),
        name="forward_within",
    )(x, bc, step, run, run_t, cols, seg_rows)


def forward_finish(s, y, x, z, dgo, state, decay, incoming, bc, run, cols, gains):
    return pl.pallas_call(
        forward_finish_kernel,
        grid=(s.pairs,),
        in_specs=[
            columns(s.rows), columns(s.rows), columns(s.rows), columns(s.rows),
            stacks(s.spans, LANES), stacks(s.spans, 8), columns(LANES),
            whole((s.rows, 4 * LANES)), whole((s.rows, LANES)), whole((s.rows, 8)), columns(8),
        ],
        out_specs=[columns(s.rows), whole((s.spans, 16, LANES))],
        out_shape=[shaped((s.rows, s.inner), F32), shaped((s.spans, 16, LANES), F32)],
        scratch_shapes=[scratch(s.rows, LANES)] * 3,
        compiler_params=params(),
        cost_estimate=s.cost(),
        name="forward_finish",
    )(y, x, z, dgo, state, decay, incoming, bc, run, cols, gains)


def gate_back(s, inner_width, scan, x, z, dgo, sums, bc, run, cols, gains):
    def kernel(*refs):
        gate_back_kernel(inner_width, *refs)

    return pl.pallas_call(
        kernel,
        grid=(s.pairs,),
        in_specs=[
            columns(s.rows), columns(s.rows), columns(s.rows), columns(s.rows),
            whole((s.spans, 8, LANES)), whole((s.rows, 4 * LANES)), whole((s.rows, LANES)),
            whole((s.rows, 8)), columns(8),
        ],
        out_specs=[
            columns(s.rows), columns(s.rows), columns(s.rows), stacks(s.spans, LANES),
            stacks(s.spans, 8), columns(8),
        ],
        out_shape=[
            shaped((s.rows, s.inner), BF16), shaped((s.rows, s.inner), BF16),
            shaped((s.rows, s.inner), F32), shaped((s.spans, LANES, s.inner), F32),
            shaped((s.spans, 8, s.inner), F32), shaped((8, s.inner), F32),
        ],
        scratch_shapes=[scratch(s.rows, LANES)] * 3 + [scratch(s.spans, LANES, 2 * ROWS, dtype=BF16)],
        compiler_params=params(),
        cost_estimate=s.cost(),
        name="gate_back",
    )(scan, x, z, dgo, sums, bc, run, cols, gains)


def backward_within(s, x, dy, bc, step, run, run_t, cols, seg_rows):
    return pl.pallas_call(
        backward_within_kernel,
        grid=(s.pairs,),
        in_specs=[
            columns(s.rows), columns(s.rows), whole((s.rows, 4 * LANES)), whole((s.rows, LANES)),
            whole((s.rows, LANES)), whole((s.spans, s.width, LANES)), whole((s.rows, 8)),
            whole((s.spans, 8, LANES)),
        ],
        out_specs=[columns(s.rows), whole((s.rows, 2 * LANES))],
        out_shape=[shaped((s.rows, s.inner), F32), shaped((s.rows, 2 * LANES), F32)],
        scratch_shapes=[scratch(s.spans, ROWS, ROWS)] * 3,
        compiler_params=params(),
        cost_estimate=s.cost(),
        name="backward_within",
    )(x, dy, bc, step, run, run_t, cols, seg_rows)


def backward_finish(
    s, value_in, ss, rim_v, rim_ss, x, dy, scan, dxw, dbc, state, decay, incoming, grad, back, outgoing,
    bc, step, run, cols, conv_v, conv_ss, heads, gains,
):
    return pl.pallas_call(
        backward_finish_kernel,
        grid=(s.pairs,),
        in_specs=[
            columns(s.rows), whole((s.rows, 3 * LANES)), columns(RIM), whole((RIM, 3 * LANES)),
            columns(s.rows), columns(s.rows), columns(s.rows), columns(s.rows), whole((s.rows, 2 * LANES)),
            stacks(s.spans, LANES), stacks(s.spans, 8), columns(LANES),
            stacks(s.spans, LANES), stacks(s.spans, 8), columns(LANES),
            whole((s.rows, 4 * LANES)), whole((s.rows, LANES)), whole((s.rows, LANES)), whole((s.rows, 8)),
            columns(8), whole((8, 2 * LANES)), whole((8, LANES)), columns(8),
        ],
        out_specs=[
            columns(s.rows), columns(RIM), columns(RIM), columns(8),
            whole((s.rows, 3 * LANES)), whole((RIM, 2 * LANES)), whole((RIM, 2 * LANES)),
            whole((8, 2 * LANES)), whole((8, LANES)),
        ],
        out_shape=[
            shaped((s.rows, s.inner), BF16), shaped((RIM, s.inner), F32), shaped((RIM, s.inner), F32),
            shaped((8, s.inner), F32), shaped((s.rows, 3 * LANES), BF16), shaped((RIM, 2 * LANES), F32),
            shaped((RIM, 2 * LANES), F32), shaped((8, 2 * LANES), F32), shaped((8, LANES), F32),
        ],
        scratch_shapes=[
            scratch(s.rows + RIM, LANES), scratch(s.rows + RIM, LANES), scratch(3, s.rows + RIM, LANES),
            scratch(s.rows, LANES), scratch(s.rows, LANES), scratch(s.rows, LANES), scratch(s.rows, LANES),
            scratch(s.rows, 2 * LANES),
        ],
        compiler_params=params(),
        cost_estimate=s.cost(),
        name="backward_finish",
    )(
        value_in, ss, rim_v, rim_ss, x, dy, scan, dxw, dbc, state, decay, incoming, grad, back, outgoing,
        bc, step, run, cols, conv_v, conv_ss, heads, gains,
    )


WIDE = 256


def tile_product(kernel, slots, operands, specs, outs, out_specs, blocks, flops):
    rows = operands[0].shape[0]
    scatter = (rows // slots.shape[0]) % 16 == 0

    def body(*refs):
        kernel(scatter, *refs)

    results = pl.pallas_call(
        body,
        grid_spec=pltpu.PrefetchScalarGridSpec(
            num_scalar_prefetch=1, grid=(blocks,), in_specs=specs, out_specs=out_specs
        ),
        out_shape=outs,
        compiler_params=params(),
        cost_estimate=pl.CostEstimate(flops=flops, bytes_accessed=8 * rows * WIDE * blocks, transcendentals=0),
        name=kernel.__name__,
    )(slots, *operands)
    return results, scatter


def fixed(shape):
    return pl.BlockSpec(shape, lambda j, slots: (0,) * len(shape))


def branch_rows(slots, back_index, gated_low, out_proj):
    rows, inner = gated_low.shape
    width = out_proj.shape[1]
    [out], scatter = tile_product(
        branch_kernel,
        slots,
        (gated_low, out_proj),
        [fixed((rows, inner)), pl.BlockSpec((inner, WIDE), lambda j, slots: (0, j))],
        [shaped((rows, width), BF16)],
        [pl.BlockSpec((rows, WIDE), lambda j, slots: (0, j))],
        width // WIDE,
        2 * rows * inner * width,
    )
    return out if scatter else move_tiles(out, back_index)


def normed_grad(slots, back_index, lows, weights, normed):
    rows, width = normed.shape
    (out, diag), scatter = tile_product(
        normed_grad_kernel,
        slots,
        (*lows, *weights, normed),
        [fixed(low.shape) for low in lows]
        + [pl.BlockSpec((WIDE, w.shape[1]), lambda j, slots: (j, 0)) for w in weights]
        + [pl.BlockSpec((rows, WIDE), lambda j, slots: (0, j))],
        [shaped((rows, width), BF16), shaped((8, width), F32)],
        [pl.BlockSpec((rows, WIDE), lambda j, slots: (0, j)), pl.BlockSpec((8, WIDE), lambda j, slots: (0, j))],
        width // WIDE,
        2 * rows * width * sum(low.shape[1] for low in lows),
    )
    return (out if scatter else move_tiles(out, back_index)), diag[0]


def swapped(value, axis, bit):
    count = lax.axis_size(axis)
    return lax.ppermute(value, axis, [(k, k ^ (1 << bit)) for k in range(count)])


def axis_bits(axis):
    return lax.axis_size(axis).bit_length() - 1


class RowsOverSeq:
    def __init__(self, grads, seq_index, backwards):
        bits, count = axis_bits("seq"), lax.axis_size("seq")
        self.here = seq_index
        self.total = grads.reshape((2,) * bits + (grads.shape[0] // count, grads.shape[1]))
        self.left = list(range(bits))[::-1]
        self.order = [0] + (list(range(1, bits))[::-1] if backwards else list(range(1, bits)))

    def swap(self):
        bit = self.order.pop(0)
        at, own = self.left.index(bit), (self.here >> bit) & 1
        self.left.pop(at)
        self.keep = lax.dynamic_index_in_dim(self.total, own, at, keepdims=False)
        self.send = lax.dynamic_index_in_dim(self.total, 1 - own, at, keepdims=False).astype(BF16)
        return swapped(self.send, "seq", bit)

    def join(self, got):
        total = self.keep.astype(F32) + got.astype(F32)
        self.total = total.astype(self.total.dtype) if self.order else total


class SumByPairs:
    def __init__(self, value, axis):
        self.size, self.axis = value.shape[0], axis
        padded = jnp.pad(value, (0, -self.size % (8 * LANES)))
        self.total, self.order = padded.reshape(-1, LANES), list(range(axis_bits(axis)))

    def swap(self):
        self.keep = self.send = self.total
        return swapped(self.send, self.axis, self.order.pop(0))

    def join(self, got):
        self.total = self.keep + got
        if not self.order:
            self.total = self.total.reshape(-1)[: self.size]


class SumByHalves:
    def __init__(self, value, axis):
        self.total, self.axis, self.here = value, axis, lax.axis_index(axis)
        bits = list(range(axis_bits(axis)))
        self.order = [(bit, True) for bit in bits[::-1]] + [(bit, False) for bit in bits]

    def swap(self):
        bit, self.adds = self.order.pop(0)
        self.own = (self.here >> bit) & 1
        if self.adds:
            half = self.total.shape[0] // 2
            self.keep = lax.dynamic_slice_in_dim(self.total, self.own * half, half, 0)
            self.send = lax.dynamic_slice_in_dim(self.total, (1 - self.own) * half, half, 0)
        else:
            self.keep = self.send = self.total
        self.send = self.send.astype(BF16)
        return swapped(self.send, self.axis, bit)

    def join(self, got):
        if self.adds:
            self.total = self.keep.astype(F32) + got.astype(F32)
            return
        mine, upper = self.keep.astype(BF16), self.own == 1
        self.total = jnp.concatenate(
            [jnp.where(upper, got, mine), jnp.where(upper, mine, got)], axis=0
        )


def swap_all(parts):
    return [(part, part.swap()) for part in parts if part.order]


def join_all(parts, got, *tokens):
    if not got:
        return
    arrived = lax.optimization_barrier((tuple(piece for _, piece in got), *tokens))[0]
    for (part, _), piece in zip(got, arrived):
        part.join(piece)


def finish_all(parts):
    while any(part.order for part in parts):
        join_all(parts, swap_all(parts))


def carried_states(states, decay, reverse, *covers):
    count = lax.axis_size("seq")
    sign = -1 if reverse else 1
    both = jnp.concatenate([states, decay], axis=0)
    results = []

    def cover(reach, got):
        if len(results) == len(covers):
            return got
        result, token = covers[len(results)](reach)
        results.append(result)
        return after(got, token)

    def joined(near, far):
        through = near[LANES : LANES + 1]
        return jnp.concatenate([near[:LANES], jnp.zeros_like(near[LANES:])], axis=0) + through * far

    near, far = (from_behind(both, "seq", sign * k) for k in (1, 2))
    near, far = cover(both, (near, far))
    reach, width = joined(near, far), 2
    while width < count - 1:
        reach = joined(reach, cover(reach, from_behind(reach, "seq", sign * width)))
        width *= 2
    while len(results) < len(covers):
        cover(reach, reach)
    return reach[:LANES], results


def after(value, *tokens):
    return lax.optimization_barrier((value, *tokens))[0]


def from_behind(value, axis, steps):
    count = lax.axis_size(axis)
    initial, last = (max(0, -steps), min(count, count - steps))
    return lax.ppermute(value, axis, [(source, source + steps) for source in range(initial, last)])


def move_tiles(rows, index):
    tile_total = index.shape[0]
    shaped_rows = rows.reshape((tile_total, rows.shape[0] // tile_total) + rows.shape[1:])
    return jnp.take(shaped_rows, index, axis=0, mode="clip").reshape(rows.shape)


def carry_weights(decays, here, reverse):
    count = decays.shape[0]
    ids = jnp.arange(count, dtype=jnp.int32)
    if reverse:
        between = (ids[None, :] < ids[:, None]) & (ids[None, :] > here)
        reached = ids > here
    else:
        between = (ids[None, :] > ids[:, None]) & (ids[None, :] < here)
        reached = ids < here
    chain = jnp.prod(jnp.where(between[:, :, None], decays[None, :, :], 1.0), axis=1)
    return jnp.where(reached[:, None], chain, 0.0)


def padded_rows(parts, rows=8):
    stacked = jnp.concatenate([part.reshape(-1, part.shape[-1]) for part in parts], axis=0)
    return jnp.pad(stacked, ((0, rows - stacked.shape[0]), (0, 0)))


def local(
    tokens,
    packing,
    segment_ids,
    norm_gain,
    gate_proj,
    value_proj,
    shared_proj,
    step_proj,
    conv_value,
    conv_value_bias,
    conv_shared,
    conv_shared_bias,
    step_bias,
    log_decay,
    skip_gain,
    gated_gain,
    out_proj,
    cotangent,
):
    own_rows = tokens.shape[0]
    head_shards = lax.axis_size("head")
    seq_shards = lax.axis_size("seq")
    head_index = lax.axis_index("head")
    seq_index = lax.axis_index("seq")
    shard_rows = own_rows * head_shards
    inner_local = gate_proj.shape[1]
    heads_local = step_proj.shape[1]
    inner_width = inner_local * head_shards
    tile_rows = own_rows // seq_shards
    tile_count = shard_rows // tile_rows
    s = Sizes(shard_rows, inner_local, heads_local)

    packed_tiles = packing.reshape(-1, tile_rows)[:, 0] // tile_rows
    own_device = seq_index * head_shards + head_index
    seq_ids = jnp.arange(seq_shards, dtype=jnp.int32)
    own_tiles = own_device * seq_shards + seq_ids
    tile_match = (own_tiles[:, None] == packed_tiles[None, :]).astype(jnp.int32)
    tile_shard = jnp.arange(packed_tiles.shape[0], dtype=jnp.int32) // tile_count
    dest_shard = jnp.sum(tile_match * tile_shard[None, :], axis=1)
    send_index = jnp.sum(
        (dest_shard[None, :] == seq_ids[:, None]).astype(jnp.int32) * seq_ids[None, :], axis=1
    )
    own_packed = lax.dynamic_slice_in_dim(packed_tiles, seq_index * tile_count, tile_count, 0)
    source_device = own_packed // seq_shards
    arrival = source_device % head_shards * seq_shards + source_device // head_shards
    slot_ids = jnp.arange(tile_count, dtype=jnp.int32)
    back_index = jnp.sum(
        (arrival[None, :] == slot_ids[:, None]).astype(jnp.int32) * slot_ids[None, :], axis=1
    )

    shard_start = seq_index * shard_rows
    around = jnp.concatenate([jnp.full((RIM,), -1, jnp.int32), segment_ids])
    around = lax.dynamic_slice_in_dim(around, shard_start, shard_rows + RIM, 0)
    seg = around[RIM:]
    span_last = around[RIM - 1 :: ROWS]
    before_span = jnp.repeat(span_last[:-1], ROWS)
    end_of_span = jnp.repeat(span_last[1:], ROWS)
    facts = [around[RIM - k : RIM - k + shard_rows] == seg for k in (1, 2, 3)]
    facts += [before_span == seg, end_of_span == seg, seg, seg, seg]
    cols = jnp.stack([fact.astype(F32) for fact in facts], axis=1)
    seg_rows = jnp.broadcast_to(seg.astype(F32).reshape(s.spans, 1, ROWS), (s.spans, 8, ROWS))

    head_pad = ((0, 0), (0, LANES - heads_local))
    heads = padded_rows([step_bias, jnp.exp(log_decay)])
    heads = jnp.pad(heads, head_pad)
    conv_v = padded_rows([conv_value, conv_value_bias])
    conv_ss = padded_rows([conv_shared, conv_shared_bias])
    gains = padded_rows([jnp.repeat(skip_gain, inner_local // heads_local), gated_gain])
    ss_proj = jnp.concatenate([shared_proj, jnp.pad(step_proj, head_pad)], axis=1)

    tok_float = tokens.astype(F32)
    tok_rstd = lax.rsqrt(jnp.mean(tok_float * tok_float, axis=1, keepdims=True) + EPS)
    normed = (tok_float * tok_rstd * norm_gain[None, :]).astype(BF16)

    def to_shard(rows):
        sent = lax.all_to_all(
            move_tiles(rows, send_index), "seq", split_axis=0, concat_axis=0, tiled=True
        )
        return lax.all_gather(sent, "head", axis=0, tiled=True)

    packed_normed = move_tiles(to_shard(normed), arrival)
    arrived_cot = to_shard(cotangent)

    value_in = dot(packed_normed, value_proj)
    ss = dot(packed_normed, ss_proj)
    rim = from_behind(
        jnp.concatenate([value_in[shard_rows - RIM :], ss[shard_rows - RIM :]], axis=1), "seq", 1
    )
    rim_v, rim_ss = rim[:, :inner_local], rim[:, inner_local:]
    x, bc, step, run, run_t, state, decay = forward_states(
        s, value_in, ss, rim_v, rim_ss, cols, conv_v, conv_ss, heads
    )

    def project_gate(reach):
        z = dot(after(packed_normed, reach), gate_proj)
        return z, z

    def within(reach):
        y = forward_within(s, after(x, reach), bc, step, run, run_t, cols, seg_rows)
        return y, y

    def cot_products(reach):
        cot = move_tiles(arrived_cot, after(arrival, reach))
        dgo = dot(cot, out_proj, CONTRACT_COLS)
        return (cot, dgo), dgo

    incoming, (gate_z, y, (packed_cot, dgo)) = carried_states(
        state[s.spans - 1], decay[s.spans - 1], False, project_gate, within, cot_products
    )
    scan, sums = forward_finish(
        s, y, x, gate_z, dgo, state, decay, incoming, bc, run, cols, gains
    )
    sums = lax.psum(jnp.stack([sums[:, 0, :], sums[:, 8, :]], axis=1), "head")
    sums = jnp.pad(sums, ((0, 0), (0, 6), (0, 0)))
    gated_low, low_gate, dy, grad, back, gate_rows = gate_back(
        s, inner_width, scan, x, gate_z, dgo, sums, bc, run, cols, gains
    )

    starts = lax.all_gather(jnp.concatenate([grad[0], decay[s.spans - 1]], axis=0), "seq")
    branch = branch_rows(arrival, back_index, gated_low, out_proj)
    out_grads = dot(after(gated_low, branch), packed_cot, CONTRACT_ROWS).astype(BF16)
    gate_grads = dot(after(packed_normed, out_grads), low_gate, CONTRACT_ROWS).astype(BF16)
    branch = lax.psum_scatter(
        after(branch, starts, gate_grads), "head", scatter_dimension=0, tiled=True
    )
    early = [RowsOverSeq(out_grads, seq_index, True)]
    got = swap_all(early)
    dxw, dbc = backward_within(s, x, after(dy, gate_grads), bc, step, run, run_t, cols, seg_rows)
    join_all(early, got, dbc)
    decays = starts[:, LANES, :]
    outgoing = jnp.sum(
        carry_weights(decays, seq_index, True)[:, None, :] * starts[:, :LANES, :], axis=0
    )
    got = swap_all(early)
    dy = after(dy, *[part.keep for part in early], *[part.send for part in early])
    low_value, tail, rim_out, taps_v, low_ss, tail_ss, rim_ss_out, taps_ss, small = backward_finish(
        s, value_in, ss, rim_v, rim_ss, x, dy, scan, dxw, dbc, state, decay, incoming, grad, back,
        outgoing, bc, step, run, cols, conv_v, conv_ss, heads, gains,
    )
    join_all(early, got, small)
    rim_out = after(rim_out, *[part.total for part in early])
    got = swap_all(early)
    rim_back = from_behind(jnp.concatenate([rim_out, rim_ss_out], axis=1), "seq", -1)
    tail = (jnp.concatenate([tail, tail_ss], axis=1) + rim_back).astype(BF16)
    low_value = lax.dynamic_update_slice(low_value, tail[:, :inner_local], (shard_rows - RIM, 0))
    low_ss = lax.dynamic_update_slice(low_ss, tail[:, inner_local:], (shard_rows - RIM, 0))

    low_gate = after(low_gate, branch, *[part.keep for part in early], *[part.send for part in early])
    d_normed, grad_norm_rows = normed_grad(
        arrival,
        back_index,
        (low_gate, low_value, low_ss),
        (gate_proj, value_proj, ss_proj),
        packed_normed,
    )
    late_normed = after(packed_normed, d_normed)
    d_normed = lax.psum_scatter(
        after(d_normed, *[piece for _, piece in got]), "head", scatter_dimension=0, tiled=True
    )
    join_all(early, got, low_gate)
    branch_back = lax.all_to_all(branch, "seq", split_axis=0, concat_axis=0, tiled=True)
    ss_grads = dot(late_normed, low_ss, CONTRACT_ROWS)
    value_grads = dot(after(late_normed, ss_grads), low_value, CONTRACT_ROWS).astype(BF16)

    per_head = [jnp.sum(gate_rows[1].reshape(heads_local, -1), axis=1)]
    per_head += [small[0, :heads_local], small[1, :heads_local]]
    pieces = [taps_v[:5].reshape(-1), gate_rows[0]] + per_head
    own_size = sum(piece.shape[0] for piece in pieces)
    shared_pieces = [taps_ss[:5].reshape(-1), grad_norm_rows]
    ss_sum = RowsOverSeq(ss_grads, seq_index, True)
    flat_sum = SumByPairs(jnp.concatenate(pieces + shared_pieces), "seq")
    join_all(None, swap_all([ss_sum, flat_sum]))
    gate_grads, value_grads = after((gate_grads, value_grads), ss_sum.total)
    large = [RowsOverSeq(gate_grads, seq_index, False), RowsOverSeq(value_grads, seq_index, True)]
    pending, age = [], 0

    def step(parts):
        nonlocal pending, age
        got = swap_all(parts)
        if not pending:
            pending, age = swap_all(large), 0
        join_all(parts, got)
        age += 1
        if age == 2 and pending:
            join_all(large, pending, *[part.total for part in parts])
            pending = []

    while ss_sum.order or flat_sum.order:
        step([ss_sum, flat_sum])
    grad_ss, everything = ss_sum.total, flat_sum.total
    shared_sum = SumByHalves(grad_ss[:, : 2 * LANES], "head")
    flat_sum = SumByPairs(everything[own_size:], "head")
    while shared_sum.order or flat_sum.order:
        step([shared_sum, flat_sum])
    normed_back = lax.all_to_all(d_normed, "seq", split_axis=0, concat_axis=0, tiled=True)
    join_all(large, pending, shared_sum.total, normed_back)
    finish_all(large + early)
    grad_shared, shared_sums = shared_sum.total, flat_sum.total
    grad_gate, grad_value = [part.total for part in large]
    grad_out_proj = early[0].total
    grad_step_proj = grad_ss[:, 2 * LANES : 2 * LANES + heads_local]
    grad_shared = lax.all_gather(grad_shared, "seq", axis=0, tiled=True).astype(F32)

    branch_given = move_tiles(branch_back, dest_shard).astype(F32)
    d_normed_given = move_tiles(normed_back, dest_shard).astype(F32)
    mixed_rows = (tok_float + branch_given).astype(BF16)
    scaled = d_normed_given * norm_gain[None, :]
    row_dot = jnp.sum(scaled * tok_float, axis=1, keepdims=True) / tokens.shape[1]
    d_tok = tok_rstd * scaled - tok_float * (tok_rstd * tok_rstd * tok_rstd * row_dot)
    grad_tokens = (cotangent.astype(F32) + d_tok).astype(BF16)

    own_taps = everything[: 5 * inner_local].reshape(5, inner_local)
    rest = everything[5 * inner_local : own_size]
    grad_gated = rest[:inner_local]
    rest = rest[inner_local:]
    grad_skip = rest[:heads_local]
    grad_step_bias = rest[heads_local : 2 * heads_local]
    grad_log_decay = rest[2 * heads_local :]
    shared_taps = shared_sums[: 10 * LANES].reshape(5, 2 * LANES)
    grad_norm_gain = shared_sums[10 * LANES : 10 * LANES + norm_gain.shape[0]] / norm_gain
    return (
        mixed_rows,
        grad_tokens,
        grad_norm_gain,
        grad_gate,
        grad_value,
        grad_shared,
        grad_step_proj,
        own_taps[:4],
        own_taps[4],
        shared_taps[:4],
        shared_taps[4],
        grad_step_bias,
        grad_log_decay,
        grad_skip,
        grad_gated,
        grad_out_proj,
    )


def solution(mesh):
    placed = (
        P(("seq", "head"), None),
        P(),
        P(),
        P(),
        P(None, "head"),
        P(None, "head"),
        P(),
        P(None, "head"),
        P(None, "head"),
        P("head"),
        P(),
        P(),
        P("head"),
        P("head"),
        P("head"),
        P("head"),
        P("head", None),
        P(("seq", "head"), None),
    )
    return jax.shard_map(
        local,
        mesh=mesh,
        in_specs=placed,
        out_specs=(
            P(("seq", "head"), None),
            P(("seq", "head"), None),
            P(),
            P("seq", "head"),
            P("seq", "head"),
            P(),
            P("seq", "head"),
            P(None, "head"),
            P("head"),
            P(),
            P(),
            P("head"),
            P("head"),
            P("head"),
            P("head"),
            P(("head", "seq"), None),
        ),
        check_vma=False,
    )
```

```python
import jax
import jax.numpy as jnp
from jax import lax
from jax.experimental import pallas as pl
from jax.experimental.pallas import tpu as pltpu
from jax.sharding import PartitionSpec as P

EPS = 1e-05
ROWS = 128
LANES = 128
HALF = 64
RIM = 8
FAR = -1e30
UNROLL = 8
F32 = jnp.float32
BF16 = jnp.bfloat16
VMEM_BYTES = 56 * 1024 * 1024
CONTRACT_ROWS = (((0,), (0,)), ((), ()))
CONTRACT_COLS = (((1,), (1,)), ((), ()))


def dot(a, b, dims=(((1,), (0,)), ((), ()))):
    return lax.dot_general(a, b, dims, preferred_element_type=F32)


def two_parts(x):
    upper = x.astype(BF16)
    return upper, (x - upper.astype(F32)).astype(BF16)


def three_parts(x):
    upper, rest = x.astype(BF16), x
    rest = x - upper.astype(F32)
    middle = rest.astype(BF16)
    return upper, middle, (rest - middle.astype(F32)).astype(BF16)


def in_two(x):
    return jnp.concatenate(two_parts(x), axis=1)


def twice(x):
    return jnp.concatenate([x, x], axis=0)


def b_parts(bc_ref, at):
    return bc_ref[at, : 2 * LANES]


def c_parts(bc_ref, at):
    return bc_ref[at, 2 * LANES :]


def cross_product(bc_ref, at):
    b, c = b_parts(bc_ref, at), c_parts(bc_ref, at)
    upper = jnp.concatenate([b[:, :LANES], b[:, :LANES]], axis=1)
    return dot(c, upper, CONTRACT_COLS) + dot(c[:, :LANES], b[:, LANES:], CONTRACT_COLS)


def lane_ids(rows):
    return lax.broadcasted_iota(jnp.int32, (rows, LANES), 1)


def row_ids(rows):
    return lax.broadcasted_iota(jnp.int32, (rows, LANES), 0)


def head_cols(block, pair):
    shift = lax.rem(LANES - 2 * pair, LANES)
    turned = pltpu.roll(block, shift, axis=1)
    first = jnp.broadcast_to(turned[:, 0:1], block.shape)
    second = jnp.broadcast_to(turned[:, 1:2], block.shape)
    return first, second


def paired(first, second):
    return jnp.where(lane_ids(first.shape[0]) < HALF, first, second)


def head_selector(pair):
    lane = row_ids(LANES)
    head = 2 * pair + jnp.where(lane < HALF, 0, 1)
    return (lane_ids(LANES) == head).astype(F32).astype(BF16)


def split_sum(x, selector):
    upper, lower = two_parts(x)
    stacked = jnp.concatenate([upper, lower], axis=1)
    return dot(stacked, jnp.concatenate([selector, selector], axis=0))


def lower_ones():
    return (row_ids(ROWS) >= lane_ids(ROWS)).astype(F32).astype(BF16)


def upper_ones():
    return (row_ids(ROWS) <= lane_ids(ROWS)).astype(F32).astype(BF16)


def spread(ref, row, col):
    return jnp.broadcast_to(ref[pl.ds(row, ROWS), col : col + 1], (ROWS, LANES))


def softplus(x):
    return jnp.maximum(x, 0.0) + jnp.log1p(jnp.exp(-jnp.abs(x)))


def sigmoid(x):
    return 1.0 / (1.0 + jnp.exp(-x))


def span_start(q):
    return pl.multiple_of(q * ROWS, ROWS)


def loop(count, body):
    def step(q, carry):
        body(q)
        return carry

    lax.fori_loop(0, count, step, 0, unroll=UNROLL)


def conv_span(pad_ref, same_ref, row, taps, bias):
    long = pad_ref[pl.ds(row, ROWS + RIM), :]
    total = bias + taps[3:4] * long[RIM:]
    shifted = []
    for back in (1, 2, 3):
        moved = pltpu.roll(long, back, axis=0)[RIM:]
        moved = moved * same_ref[back - 1, pl.ds(row, ROWS), :]
        shifted.append(moved)
        total = total + taps[3 - back : 4 - back] * moved
    return total, [long[RIM:]] + shifted


def forward_states_kernel(
    value_ref, ss_ref, rim_v_ref, rim_ss_ref, cols_ref, conv_ref, conv_ss_ref, heads_ref,
    x_ref, bc_ref, step_ref, run_ref, run_t_ref, state_ref, decay_ref,
    pad, same, cont, last, bt,
):
    pair = pl.program_id(0)
    rows = value_ref.shape[0]
    spans = rows // ROWS
    width = run_t_ref.shape[1]

    @pl.when(pair == 0)
    def _():
        def masks(q):
            row = span_start(q)
            for k in range(3):
                same[k, pl.ds(row, ROWS), :] = spread(cols_ref, row, k)
            cont[pl.ds(row, ROWS), :] = spread(cols_ref, row, 3)
            last[pl.ds(row, ROWS), :] = spread(cols_ref, row, 4)

        loop(spans, masks)
        for part in range(2):
            lanes = slice(part * LANES, (part + 1) * LANES)
            pad[0:RIM, :] = rim_ss_ref[:, lanes]
            pad[RIM:, :] = ss_ref[:, lanes]
            taps, bias = conv_ss_ref[0:4, lanes], conv_ss_ref[4:5, lanes]

            def shared(q):
                row = span_start(q)
                pre, _ = conv_span(pad, same, row, taps, bias)
                act = pre * sigmoid(pre)
                bc_ref[pl.ds(row, ROWS), 2 * part * LANES : 2 * (part + 1) * LANES] = in_two(act)
                if part == 0:
                    bt[q] = in_two(jnp.transpose(act))

            loop(spans, shared)

        bias, rate = heads_ref[0:1, :], heads_ref[1:2, :]
        tri, tri_t = lower_ones(), upper_ones()

        def steps(q):
            row = span_start(q)
            size = softplus(ss_ref[pl.ds(row, ROWS), 2 * LANES :] + bias)
            step_ref[pl.ds(row, ROWS), :] = size
            parts = three_parts(-size * rate)
            run_ref[pl.ds(row, ROWS), :] = sum(dot(tri, part) for part in parts)
            turned = sum(dot(part, tri_t, CONTRACT_ROWS) for part in parts)
            run_t_ref[q] = turned[:width]

        loop(spans, steps)

    pad[0:RIM, :] = rim_v_ref[...]
    pad[RIM:, :] = value_ref[...]
    taps, bias = conv_ref[0:4], conv_ref[4:5]

    def span(q, carry):
        state, decay = carry
        row = span_start(q)
        at = pl.ds(row, ROWS)
        pre, _ = conv_span(pad, same, row, taps, bias)
        x = pre * sigmoid(pre)
        x_ref[at, :] = x
        size = paired(*head_cols(step_ref[at, :], pair))
        run = paired(*head_cols(run_ref[at, :], pair))
        enter = jnp.exp(run[ROWS - 1 :]) * cont[pl.ds(row + ROWS - 8, 8), :][7:8]
        to_end = jnp.exp(run[ROWS - 1 :] - run) * last[at, :]
        state = state * enter + dot(bt[q], twice((x * size * to_end).astype(BF16)))
        decay = decay * enter
        state_ref[q] = state
        decay_ref[q] = jnp.broadcast_to(decay, (8, LANES))
        return state, decay

    lax.fori_loop(
        0, spans, span, (jnp.zeros((LANES, LANES), F32), jnp.ones((1, LANES), F32)),
        unroll=UNROLL,
    )


def span_masks(cols_ref, seg_rows_ref, bias_ref, spans):
    causal = row_ids(ROWS) >= lane_ids(ROWS)

    def mask(q):
        own = spread(cols_ref, span_start(q), 5)
        other = jnp.broadcast_to(seg_rows_ref[q, 0:1, :], (ROWS, ROWS))
        bias_ref[q] = jnp.where(causal & (own == other), 0.0, FAR)

    loop(spans, mask)


def decay_pair(run_ref, run_t_ref, mask_ref, q, pair):
    first, second = head_cols(run_ref[pl.ds(span_start(q), ROWS), :], pair)
    rows = run_t_ref[q, pl.ds(2 * pair, 2), :]
    mask = mask_ref[q]
    return jnp.exp(first - rows[0:1] + mask), jnp.exp(second - rows[1:2] + mask)


def heads_apart(x):
    lane = lane_ids(x.shape[0])
    zero = jnp.zeros_like(x)
    return jnp.concatenate([jnp.where(lane < HALF, x, zero), jnp.where(lane < HALF, zero, x)], axis=0)


def forward_within_kernel(
    x_ref, bc_ref, step_ref, run_ref, run_t_ref, cols_ref, seg_rows_ref, y_ref, mask, cross
):
    pair = pl.program_id(0)
    spans = x_ref.shape[0] // ROWS

    @pl.when(pair == 0)
    def _():
        span_masks(cols_ref, seg_rows_ref, mask, spans)

        def products(q):
            at = pl.ds(span_start(q), ROWS)
            cross[q] = cross_product(bc_ref, at)

        loop(spans, products)

    def span(q):
        at = pl.ds(span_start(q), ROWS)
        size = paired(*head_cols(step_ref[at, :], pair))
        weighted = x_ref[at, :] * size
        first, second = decay_pair(run_ref, run_t_ref, mask, q, pair)
        mix = jnp.concatenate([first * cross[q], second * cross[q]], axis=1).astype(BF16)
        y_ref[at, :] = dot(mix, heads_apart(weighted).astype(BF16))

    loop(spans, span)


def entering(state_ref, decay_ref, incoming, q, before):
    at = jnp.maximum(before, 0)
    local = state_ref[at] + decay_ref[at, 0:1, :] * incoming
    return jnp.where(before >= 0, local, incoming)


def row_sums(acc_ref, out_ref, base, spans):
    ones = jnp.ones((8, LANES), BF16)

    def total(q):
        parts = three_parts(acc_ref[pl.ds(span_start(q), ROWS), :])
        out_ref[q, base : base + 8, :] = sum(dot(ones, part, CONTRACT_COLS) for part in parts)

    loop(spans, total)


def forward_finish_kernel(
    y_ref, x_ref, z_ref, dgo_ref, state_ref, decay_ref, in_ref, bc_ref, run_ref, cols_ref, gains_ref,
    scan_ref, sums_ref, cont, squares, inner,
):
    pair = pl.program_id(0)
    spans = y_ref.shape[0] // ROWS

    @pl.when(pair == 0)
    def _():
        def masks(q):
            row = span_start(q)
            cont[pl.ds(row, ROWS), :] = spread(cols_ref, row, 3)

        loop(spans, masks)
        squares[...] = jnp.zeros_like(squares)
        inner[...] = jnp.zeros_like(inner)

    incoming = in_ref[...]
    skip, gain = gains_ref[0:1], gains_ref[1:2]

    def span(q):
        at = pl.ds(span_start(q), ROWS)
        run = paired(*head_cols(run_ref[at, :], pair))
        state = entering(state_ref, decay_ref, incoming, q, q - 1)
        upper, lower = two_parts(state)
        c = c_parts(bc_ref, at)
        carried = dot(c, twice(upper)) + dot(c[:, :LANES], lower)
        scan = y_ref[at, :] + carried * (jnp.exp(run) * cont[at, :])
        scan_ref[at, :] = scan
        z = z_ref[at, :]
        gated = (scan + skip * x_ref[at, :]) * (z * sigmoid(z))
        squares[at, :] += gated * gated
        inner[at, :] += gain * dgo_ref[at, :] * gated

    loop(spans, span)

    @pl.when(pair == pl.num_programs(0) - 1)
    def _():
        row_sums(squares, sums_ref, 0, spans)
        row_sums(inner, sums_ref, 8, spans)


def gate_back_kernel(
    inner_width,
    scan_ref, x_ref, z_ref, dgo_ref, sums_ref, bc_ref, run_ref, cols_ref, gains_ref,
    out_ref, dz_ref, dy_ref, grad_ref, decay_ref, rows_ref,
    cont, rstd, coef, ct,
):
    pair = pl.program_id(0)
    spans = scan_ref.shape[0] // ROWS

    @pl.when(pair == 0)
    def _():
        def masks(q):
            row = span_start(q)
            at = pl.ds(row, ROWS)
            cont[at, :] = spread(cols_ref, row, 3)
            ct[q] = jnp.concatenate(
                [
                    jnp.transpose(bc_ref[at, k * LANES : (k + 1) * LANES].astype(F32)).astype(BF16)
                    for k in (2, 3)
                ],
                axis=1,
            )
            square = jnp.broadcast_to(sums_ref[q, 0:1, :], (ROWS, LANES))
            cross = jnp.broadcast_to(sums_ref[q, 1:2, :], (ROWS, LANES))
            root = lax.rsqrt(square / inner_width + EPS)
            rstd[at, :] = jnp.transpose(root)
            coef[at, :] = jnp.transpose(root * root * root * cross / inner_width)

        loop(spans, masks)

    skip, gain = gains_ref[0:1], gains_ref[1:2]
    rows_ref[...] = jnp.zeros_like(rows_ref)

    def span(k, carry):
        leaving, decay = carry
        q = spans - 1 - k
        at = pl.ds(span_start(q), ROWS)
        x, z, dgo = x_ref[at, :], z_ref[at, :], dgo_ref[at, :]
        scanned = scan_ref[at, :] + skip * x
        gate = sigmoid(z)
        silu = z * gate
        gated = scanned * silu
        normed = gated * rstd[at, :]
        out_ref[at, :] = (normed * gain).astype(BF16)
        d_gated = rstd[at, :] * (dgo * gain) - gated * coef[at, :]
        d_scan = d_gated * silu
        dz_ref[at, :] = (d_gated * scanned * (gate * (1.0 + z * (1.0 - gate)))).astype(BF16)
        dy_ref[at, :] = d_scan
        rows_ref[0:1] += jnp.sum(dgo * normed, axis=0, keepdims=True)
        rows_ref[1:2] += jnp.sum(d_scan * x, axis=0, keepdims=True)
        run = paired(*head_cols(run_ref[at, :], pair))
        enter = jnp.exp(run) * cont[at, :]
        upper, lower = two_parts(d_scan * enter)
        turned = ct[q]
        leaving = leaving * enter[ROWS - 1 :] + dot(turned, twice(upper)) + dot(turned[:, :ROWS], lower)
        decay = decay * enter[ROWS - 1 :]
        grad_ref[q] = leaving
        decay_ref[q] = jnp.broadcast_to(decay, (8, LANES))
        return leaving, decay

    lax.fori_loop(
        0, spans, span, (jnp.zeros((LANES, LANES), F32), jnp.ones((1, LANES), F32)),
        unroll=UNROLL,
    )


def backward_within_kernel(
    x_ref, dy_ref, bc_ref, step_ref, run_ref, run_t_ref, cols_ref, seg_rows_ref,
    dxw_ref, dbc_ref, mask, cross, d_cross,
):
    pair = pl.program_id(0)
    spans = x_ref.shape[0] // ROWS

    @pl.when(pair == 0)
    def _():
        span_masks(cols_ref, seg_rows_ref, mask, spans)

        def products(q):
            at = pl.ds(span_start(q), ROWS)
            cross[q] = cross_product(bc_ref, at)
            d_cross[q] = jnp.zeros((ROWS, ROWS), F32)

        loop(spans, products)

    def span(q):
        at = pl.ds(span_start(q), ROWS)
        size = paired(*head_cols(step_ref[at, :], pair))
        weighted = (x_ref[at, :] * size).astype(BF16)
        first, second = decay_pair(run_ref, run_t_ref, mask, q, pair)
        dy, dy_rest = two_parts(dy_ref[at, :])
        apart = heads_apart(dy)
        both = jnp.concatenate([apart, heads_apart(dy_rest)], axis=1)
        d_mix = dot(both, jnp.concatenate([weighted, weighted], axis=1), CONTRACT_COLS)
        d_cross[q] += first * d_mix[:ROWS] + second * d_mix[ROWS:]
        mix = jnp.concatenate([first * cross[q], second * cross[q]], axis=0).astype(BF16)
        dxw_ref[at, :] = dot(mix, apart, CONTRACT_ROWS)

    loop(spans, span)

    @pl.when(pair == pl.num_programs(0) - 1)
    def _():
        def shared(q):
            at = pl.ds(span_start(q), ROWS)
            grad = d_cross[q].astype(BF16)
            b, c = b_parts(bc_ref, at), c_parts(bc_ref, at)
            both = dot(grad, c, CONTRACT_ROWS)
            dbc_ref[at, :LANES] = both[:, :LANES] + both[:, LANES:]
            both = dot(grad, b)
            dbc_ref[at, LANES:] = both[:, :LANES] + both[:, LANES:]

        loop(spans, shared)


def conv_back(pad_ref, d_pre, same, taps, spans, store, rim_store):
    def span(q):
        at = pl.ds(span_start(q), ROWS + RIM)
        long = d_pre[at, :]
        total = taps[3:4] * long[:ROWS]
        for ahead in (1, 2, 3):
            masked = long * same[ahead - 1, at, :]
            moved = pltpu.roll(masked, ROWS + RIM - ahead, axis=0)[:ROWS]
            total = total + taps[3 - ahead : 4 - ahead] * moved
        store(q, total)

    loop(spans, span)
    head = d_pre[0:RIM, :]
    total = jnp.zeros((RIM, LANES), F32)
    for ahead in (1, 2, 3):
        masked = head * same[ahead - 1, 0:RIM, :]
        both = jnp.concatenate([jnp.zeros((RIM, LANES), F32), masked], axis=0)
        total = total + taps[3 - ahead : 4 - ahead] * pltpu.roll(both, 2 * RIM - ahead, axis=0)[:RIM]
    rim_store(total)


def tap_sums(d_pre, shifted):
    sums = [jnp.sum(d_pre * shifted[3 - k], axis=0, keepdims=True) for k in range(4)]
    sums.append(jnp.sum(d_pre, axis=0, keepdims=True))
    return jnp.concatenate(sums + [jnp.zeros((3, LANES), F32)], axis=0)


def silu_grad(pre):
    gate = sigmoid(pre)
    return gate * (1.0 + pre * (1.0 - gate))


def backward_finish_kernel(
    value_ref, ss_ref, rim_v_ref, rim_ss_ref, x_ref, dy_ref, scan_ref, dxw_ref, dbc_ref,
    state_ref, decay_ref, in_ref, grad_ref, back_ref, out_ref,
    bc_ref, step_ref, run_ref, cols_ref, conv_ref, conv_ss_ref, heads_ref, gains_ref,
    low_ref, tail_ref, rim_ref, taps_ref, low_ss_ref, tail_ss_ref, rim_ss_out_ref, taps_ss_ref, small_ref,
    pad, d_pre, same, cont, last, d_run, d_step, d_bc,
):
    pair = pl.program_id(0)
    rows = value_ref.shape[0]
    spans = rows // ROWS

    @pl.when(pair == 0)
    def _():
        def masks(q):
            row = span_start(q)
            for k in range(3):
                same[k, pl.ds(row, ROWS), :] = spread(cols_ref, row, k)
            cont[pl.ds(row, ROWS), :] = spread(cols_ref, row, 3)
            last[pl.ds(row, ROWS), :] = spread(cols_ref, row, 4)

        loop(spans, masks)
        same[:, rows:, :] = jnp.zeros((3, RIM, LANES), F32)
        d_pre[rows:, :] = jnp.zeros((RIM, LANES), F32)
        d_run[...] = jnp.zeros_like(d_run)
        d_step[...] = jnp.zeros_like(d_step)
        d_bc[...] = dbc_ref[...]

    pad[0:RIM, :] = rim_v_ref[...]
    pad[RIM:, :] = value_ref[...]
    taps, bias = conv_ref[0:4], conv_ref[4:5]
    skip = gains_ref[0:1]
    incoming, outgoing = in_ref[...], out_ref[...]
    selector = head_selector(pair)
    taps_ref[...] = jnp.zeros_like(taps_ref)
    final_row = row_ids(ROWS) == ROWS - 1

    def span(q):
        row = span_start(q)
        at = pl.ds(row, ROWS)
        x, dy = x_ref[at, :], dy_ref[at, :]
        size = paired(*head_cols(step_ref[at, :], pair))
        run = paired(*head_cols(run_ref[at, :], pair))
        enter = jnp.exp(run) * cont[at, :]
        to_end = jnp.exp(run[ROWS - 1 :] - run) * last[at, :]
        state, state_rest = two_parts(entering(state_ref, decay_ref, incoming, q, q - 1))
        after = state_ref[q] + decay_ref[q, 0:1, :] * incoming
        ahead = jnp.minimum(q + 1, spans - 1)
        grad = jnp.where(
            q + 1 < spans, grad_ref[ahead] + back_ref[ahead, 0:1, :] * outgoing, outgoing
        )
        weighted = x * size
        low_grad = grad.astype(BF16)
        d_weighted = dxw_ref[at, :] + to_end * dot(b_parts(bc_ref, at), twice(low_grad))
        entered = in_two(dy * enter)
        d_bc[at, LANES:] += dot(
            entered, jnp.concatenate([state, state], axis=1), CONTRACT_COLS
        ) + dot(entered[:, :LANES], state_rest, CONTRACT_COLS)
        d_bc[at, :LANES] += dot((weighted * to_end).astype(BF16), low_grad, CONTRACT_COLS)
        turn = dy.astype(BF16).astype(F32) * scan_ref[at, :]
        turn = turn - d_weighted * weighted.astype(BF16).astype(F32)
        turn = turn + jnp.where(final_row, jnp.sum(grad * after, axis=0, keepdims=True), 0.0)
        d_run[at, :] += split_sum(turn, selector)
        d_step[at, :] += split_sum(d_weighted * x, selector)
        pre, shifted = conv_span(pad, same, row, taps, bias)
        d_act = (d_weighted * size + skip * dy) * silu_grad(pre)
        d_pre[at, :] = d_act
        taps_ref[...] += tap_sums(d_act, shifted)

    loop(spans, span)

    def keep(q, total):
        low_ref[pl.ds(span_start(q), ROWS), :] = total.astype(BF16)

        @pl.when(q == spans - 1)
        def _():
            tail_ref[...] = total[ROWS - RIM :]

    def keep_rim(total):
        rim_ref[...] = total

    conv_back(pad, d_pre, same, taps, spans, keep, keep_rim)

    @pl.when(pair == pl.num_programs(0) - 1)
    def _():
        for part in range(2):
            lanes = slice(part * LANES, (part + 1) * LANES)
            pad[0:RIM, :] = rim_ss_ref[:, lanes]
            pad[RIM:, :] = ss_ref[:, lanes]
            part_taps, part_bias = conv_ss_ref[0:4, lanes], conv_ss_ref[4:5, lanes]
            taps_ss_ref[:, lanes] = jnp.zeros((8, LANES), F32)

            def shared(q):
                row = span_start(q)
                at = pl.ds(row, ROWS)
                pre, shifted = conv_span(pad, same, row, part_taps, part_bias)
                d_act = d_bc[at, lanes] * silu_grad(pre)
                d_pre[at, :] = d_act
                taps_ss_ref[:, lanes] += tap_sums(d_act, shifted)

            loop(spans, shared)

            def keep_ss(q, total):
                low_ss_ref[pl.ds(span_start(q), ROWS), lanes] = total.astype(BF16)

                @pl.when(q == spans - 1)
                def _():
                    tail_ss_ref[:, lanes] = total[ROWS - RIM :]

            def keep_rim_ss(total):
                rim_ss_out_ref[:, lanes] = total

            conv_back(pad, d_pre, same, part_taps, spans, keep_ss, keep_rim_ss)

        step_bias, rate = heads_ref[0:1, :], heads_ref[1:2, :]
        small_ref[...] = jnp.zeros_like(small_ref)
        tri_t = upper_ones()

        def steps(q):
            at = pl.ds(span_start(q), ROWS)
            d_decay = sum(dot(tri_t, part) for part in three_parts(d_run[at, :]))
            slope = sigmoid(ss_ref[at, 2 * LANES :] + step_bias)
            d_raw = (d_step[at, :] - d_decay * rate) * slope
            low_ss_ref[at, 2 * LANES :] = d_raw.astype(BF16)
            small_ref[0:1] += jnp.sum(d_raw, axis=0, keepdims=True)
            small_ref[1:2] -= jnp.sum(d_decay * step_ref[at, :] * rate, axis=0, keepdims=True)

        loop(spans, steps)


def store_tiles(slots_ref, out_ref, value, scatter):
    if not scatter:
        out_ref[...] = value
        return
    tile = value.shape[0] // slots_ref.shape[0]
    for k in range(slots_ref.shape[0]):
        start = pl.multiple_of(slots_ref[k] * tile, tile)
        out_ref[pl.ds(start, tile), :] = value[k * tile : (k + 1) * tile]


def branch_kernel(scatter, slots_ref, rows_ref, weight_ref, out_ref):
    store_tiles(slots_ref, out_ref, dot(rows_ref[...], weight_ref[...]).astype(BF16), scatter)


def normed_grad_kernel(
    scatter, slots_ref, gate_ref, value_ref, ss_ref, gate_w, value_w, ss_w, normed_ref, out_ref, diag_ref
):
    total = dot(gate_ref[...], gate_w[...], CONTRACT_COLS)
    total = total + dot(value_ref[...], value_w[...], CONTRACT_COLS)
    total = total + dot(ss_ref[...], ss_w[...], CONTRACT_COLS)
    store_tiles(slots_ref, out_ref, total.astype(BF16), scatter)
    sums = jnp.sum(total * normed_ref[...].astype(F32), axis=0, keepdims=True)
    diag_ref[...] = jnp.broadcast_to(sums, diag_ref.shape)


def whole(shape):
    return pl.BlockSpec(shape, lambda j: (0,) * len(shape))


def columns(rows, width=LANES):
    return pl.BlockSpec((rows, width), lambda j: (0, j))


def value_columns(rows):
    return pl.BlockSpec((rows, LANES), lambda j: (0, j + 3))


def stacks(count, rows):
    return pl.BlockSpec((count, rows, LANES), lambda j: (0, 0, j))


def params():
    return pltpu.CompilerParams(vmem_limit_bytes=VMEM_BYTES, dimension_semantics=("arbitrary",))


def shaped(shape, dtype):
    return jax.ShapeDtypeStruct(shape, dtype)


def scratch(*shape, dtype=F32):
    return pltpu.VMEM(shape, dtype)


class Sizes:
    def __init__(self, rows, inner, heads):
        self.rows, self.inner, self.heads = rows, inner, heads
        self.spans, self.pairs = rows // ROWS, inner // LANES
        self.width = max(8, heads)

    def cost(self):
        cells = self.rows * self.inner
        return pl.CostEstimate(flops=1, bytes_accessed=1, transcendentals=0)


def forward_states(s, both, rim, cols, conv_v, conv_ss, heads):
    return pl.pallas_call(
        forward_states_kernel,
        grid=(s.pairs,),
        in_specs=[
            value_columns(s.rows), whole((s.rows, 3 * LANES)), value_columns(RIM), whole((RIM, 3 * LANES)),
            whole((s.rows, 8)), columns(8), whole((8, 2 * LANES)), whole((8, LANES)),
        ],
        out_specs=[
            columns(s.rows), whole((s.rows, 4 * LANES)), whole((s.rows, LANES)), whole((s.rows, LANES)),
            whole((s.spans, s.width, LANES)), stacks(s.spans, LANES), stacks(s.spans, 8),
        ],
        out_shape=[
            shaped((s.rows, s.inner), F32), shaped((s.rows, 4 * LANES), BF16),
            shaped((s.rows, LANES), F32), shaped((s.rows, LANES), F32),
            shaped((s.spans, s.width, LANES), F32),
            shaped((s.spans, LANES, s.inner), F32), shaped((s.spans, 8, s.inner), F32),
        ],
        scratch_shapes=[
            scratch(s.rows + RIM, LANES), scratch(3, s.rows, LANES), scratch(s.rows, LANES),
            scratch(s.rows, LANES), scratch(s.spans, LANES, 2 * ROWS, dtype=BF16),
        ],
        compiler_params=params(),
        cost_estimate=s.cost(),
        name="forward_states",
    )(both, both, rim, rim, cols, conv_v, conv_ss, heads)


def forward_within(s, x, bc, step, run, run_t, cols, seg_rows):
    return pl.pallas_call(
        forward_within_kernel,
        grid=(s.pairs,),
        in_specs=[
            columns(s.rows), whole((s.rows, 4 * LANES)), whole((s.rows, LANES)), whole((s.rows, LANES)),
            whole((s.spans, s.width, LANES)), whole((s.rows, 8)), whole((s.spans, 8, LANES)),
        ],
        out_specs=columns(s.rows),
        out_shape=shaped((s.rows, s.inner), F32),
        scratch_shapes=[scratch(s.spans, ROWS, ROWS), scratch(s.spans, ROWS, ROWS)],
        compiler_params=params(),
        cost_estimate=s.cost(),
        name="forward_within",
    )(x, bc, step, run, run_t, cols, seg_rows)


def forward_finish(s, y, x, z, dgo, state, decay, incoming, bc, run, cols, gains):
    return pl.pallas_call(
        forward_finish_kernel,
        grid=(s.pairs,),
        in_specs=[
            columns(s.rows), columns(s.rows), columns(s.rows), columns(s.rows),
            stacks(s.spans, LANES), stacks(s.spans, 8), columns(LANES),
            whole((s.rows, 4 * LANES)), whole((s.rows, LANES)), whole((s.rows, 8)), columns(8),
        ],
        out_specs=[columns(s.rows), whole((s.spans, 16, LANES))],
        out_shape=[shaped((s.rows, s.inner), F32), shaped((s.spans, 16, LANES), F32)],
        scratch_shapes=[scratch(s.rows, LANES)] * 3,
        compiler_params=params(),
        cost_estimate=s.cost(),
        name="forward_finish",
    )(y, x, z, dgo, state, decay, incoming, bc, run, cols, gains)


def gate_back(s, inner_width, scan, x, z, dgo, sums, bc, run, cols, gains):
    def kernel(*refs):
        gate_back_kernel(inner_width, *refs)

    return pl.pallas_call(
        kernel,
        grid=(s.pairs,),
        in_specs=[
            columns(s.rows), columns(s.rows), columns(s.rows), columns(s.rows),
            whole((s.spans, 8, LANES)), whole((s.rows, 4 * LANES)), whole((s.rows, LANES)),
            whole((s.rows, 8)), columns(8),
        ],
        out_specs=[
            columns(s.rows), columns(s.rows), columns(s.rows), stacks(s.spans, LANES),
            stacks(s.spans, 8), columns(8),
        ],
        out_shape=[
            shaped((s.rows, s.inner), BF16), shaped((s.rows, s.inner), BF16),
            shaped((s.rows, s.inner), F32), shaped((s.spans, LANES, s.inner), F32),
            shaped((s.spans, 8, s.inner), F32), shaped((8, s.inner), F32),
        ],
        scratch_shapes=[scratch(s.rows, LANES)] * 3 + [scratch(s.spans, LANES, 2 * ROWS, dtype=BF16)],
        compiler_params=params(),
        cost_estimate=s.cost(),
        name="gate_back",
    )(scan, x, z, dgo, sums, bc, run, cols, gains)


def backward_within(s, x, dy, bc, step, run, run_t, cols, seg_rows):
    return pl.pallas_call(
        backward_within_kernel,
        grid=(s.pairs,),
        in_specs=[
            columns(s.rows), columns(s.rows), whole((s.rows, 4 * LANES)), whole((s.rows, LANES)),
            whole((s.rows, LANES)), whole((s.spans, s.width, LANES)), whole((s.rows, 8)),
            whole((s.spans, 8, LANES)),
        ],
        out_specs=[columns(s.rows), whole((s.rows, 2 * LANES))],
        out_shape=[shaped((s.rows, s.inner), F32), shaped((s.rows, 2 * LANES), F32)],
        scratch_shapes=[scratch(s.spans, ROWS, ROWS)] * 3,
        compiler_params=params(),
        cost_estimate=s.cost(),
        name="backward_within",
    )(x, dy, bc, step, run, run_t, cols, seg_rows)


def backward_finish(
    s, both, rim, x, dy, scan, dxw, dbc, state, decay, incoming, grad, back, outgoing,
    bc, step, run, cols, conv_v, conv_ss, heads, gains,
):
    return pl.pallas_call(
        backward_finish_kernel,
        grid=(s.pairs,),
        in_specs=[
            value_columns(s.rows), whole((s.rows, 3 * LANES)), value_columns(RIM), whole((RIM, 3 * LANES)),
            columns(s.rows), columns(s.rows), columns(s.rows), columns(s.rows), whole((s.rows, 2 * LANES)),
            stacks(s.spans, LANES), stacks(s.spans, 8), columns(LANES),
            stacks(s.spans, LANES), stacks(s.spans, 8), columns(LANES),
            whole((s.rows, 4 * LANES)), whole((s.rows, LANES)), whole((s.rows, LANES)), whole((s.rows, 8)),
            columns(8), whole((8, 2 * LANES)), whole((8, LANES)), columns(8),
        ],
        out_specs=[
            columns(s.rows), columns(RIM), columns(RIM), columns(8),
            whole((s.rows, 3 * LANES)), whole((RIM, 2 * LANES)), whole((RIM, 2 * LANES)),
            whole((8, 2 * LANES)), whole((8, LANES)),
        ],
        out_shape=[
            shaped((s.rows, s.inner), BF16), shaped((RIM, s.inner), F32), shaped((RIM, s.inner), F32),
            shaped((8, s.inner), F32), shaped((s.rows, 3 * LANES), BF16), shaped((RIM, 2 * LANES), F32),
            shaped((RIM, 2 * LANES), F32), shaped((8, 2 * LANES), F32), shaped((8, LANES), F32),
        ],
        scratch_shapes=[
            scratch(s.rows + RIM, LANES), scratch(s.rows + RIM, LANES), scratch(3, s.rows + RIM, LANES),
            scratch(s.rows, LANES), scratch(s.rows, LANES), scratch(s.rows, LANES), scratch(s.rows, LANES),
            scratch(s.rows, 2 * LANES),
        ],
        compiler_params=params(),
        cost_estimate=s.cost(),
        name="backward_finish",
    )(
        both, both, rim, rim, x, dy, scan, dxw, dbc, state, decay, incoming, grad, back, outgoing,
        bc, step, run, cols, conv_v, conv_ss, heads, gains,
    )


WIDE = 256


def tile_product(kernel, slots, operands, specs, outs, out_specs, blocks, flops):
    rows = operands[0].shape[0]
    scatter = (rows // slots.shape[0]) % 16 == 0

    def body(*refs):
        kernel(scatter, *refs)

    results = pl.pallas_call(
        body,
        grid_spec=pltpu.PrefetchScalarGridSpec(
            num_scalar_prefetch=1, grid=(blocks,), in_specs=specs, out_specs=out_specs
        ),
        out_shape=outs,
        compiler_params=params(),
        cost_estimate=pl.CostEstimate(flops=1, bytes_accessed=1, transcendentals=0),
        name=kernel.__name__,
    )(slots, *operands)
    return results, scatter


def fixed(shape):
    return pl.BlockSpec(shape, lambda j, slots: (0,) * len(shape))


def branch_rows(slots, back_index, gated_low, out_proj):
    rows, inner = gated_low.shape
    width = out_proj.shape[1]
    [out], scatter = tile_product(
        branch_kernel,
        slots,
        (gated_low, out_proj),
        [fixed((rows, inner)), pl.BlockSpec((inner, WIDE), lambda j, slots: (0, j))],
        [shaped((rows, width), BF16)],
        [pl.BlockSpec((rows, WIDE), lambda j, slots: (0, j))],
        width // WIDE,
        2 * rows * inner * width,
    )
    return out if scatter else move_tiles(out, back_index)


def normed_grad(slots, back_index, lows, weights, normed):
    rows, width = normed.shape
    (out, diag), scatter = tile_product(
        normed_grad_kernel,
        slots,
        (*lows, *weights, normed),
        [fixed(low.shape) for low in lows]
        + [pl.BlockSpec((WIDE, w.shape[1]), lambda j, slots: (j, 0)) for w in weights]
        + [pl.BlockSpec((rows, WIDE), lambda j, slots: (0, j))],
        [shaped((rows, width), BF16), shaped((8, width), F32)],
        [pl.BlockSpec((rows, WIDE), lambda j, slots: (0, j)), pl.BlockSpec((8, WIDE), lambda j, slots: (0, j))],
        width // WIDE,
        2 * rows * width * sum(low.shape[1] for low in lows),
    )
    return (out if scatter else move_tiles(out, back_index)), diag[0]


def swapped(value, axis, bit):
    count = lax.axis_size(axis)
    return lax.ppermute(value, axis, [(k, k ^ (1 << bit)) for k in range(count)])


def axis_bits(axis):
    return lax.axis_size(axis).bit_length() - 1


class RowsOverSeq:
    def __init__(self, grads, seq_index, backwards):
        bits, count = axis_bits("seq"), lax.axis_size("seq")
        self.here = seq_index
        self.total = grads.reshape((2,) * bits + (grads.shape[0] // count, grads.shape[1]))
        self.left = list(range(bits))[::-1]
        self.order = [0] + (list(range(1, bits))[::-1] if backwards else list(range(1, bits)))

    def swap(self):
        bit = self.order.pop(0)
        at, own = self.left.index(bit), (self.here >> bit) & 1
        self.left.pop(at)
        self.keep = lax.dynamic_index_in_dim(self.total, own, at, keepdims=False)
        self.send = lax.dynamic_index_in_dim(self.total, 1 - own, at, keepdims=False)
        return swapped(self.send, "seq", bit)

    def join(self, got):
        total = self.keep.astype(F32) + got.astype(F32)
        self.total = total.astype(self.total.dtype) if self.order else total


class SumByPairs:
    def __init__(self, value, axis):
        self.size, self.axis = value.shape[0], axis
        padded = jnp.pad(value, (0, -self.size % (8 * LANES)))
        self.total, self.order = padded.reshape(-1, LANES), list(range(axis_bits(axis)))

    def swap(self):
        self.keep = self.send = self.total
        return swapped(self.send, self.axis, self.order.pop(0))

    def join(self, got):
        self.total = self.keep + got
        if not self.order:
            self.total = self.total.reshape(-1)[: self.size]


class SumByHalves:
    def __init__(self, value, axis):
        self.total, self.axis, self.here = value, axis, lax.axis_index(axis)
        bits = list(range(axis_bits(axis)))
        self.order = [(bit, True) for bit in bits[::-1]] + [(bit, False) for bit in bits]

    def swap(self):
        bit, self.adds = self.order.pop(0)
        self.own = (self.here >> bit) & 1
        if self.adds:
            half = self.total.shape[0] // 2
            self.keep = lax.dynamic_slice_in_dim(self.total, self.own * half, half, 0)
            self.send = lax.dynamic_slice_in_dim(self.total, (1 - self.own) * half, half, 0)
        else:
            self.keep = self.send = self.total.astype(BF16)
        return swapped(self.send, self.axis, bit)

    def join(self, got):
        if self.adds:
            self.total = self.keep.astype(F32) + got.astype(F32)
            return
        mine, upper = self.keep, self.own == 1
        self.total = jnp.concatenate(
            [jnp.where(upper, got, mine), jnp.where(upper, mine, got)], axis=0
        )


class Chain:
    def __init__(self, part, *makers):
        self.part, self.makers, self.totals = part, list(makers), []

    @property
    def order(self):
        while not self.part.order and self.makers:
            self.totals.append(self.part.total)
            self.part = self.makers.pop(0)(self.part.total)
        return self.part.order

    @property
    def total(self):
        return self.part.total

    def swap(self):
        return self.part.swap()

    def join(self, got):
        self.part.join(got)


def swap_all(parts):
    return [(part, part.swap()) for part in parts if part.order]


def join_all(parts, got, *tokens):
    if not got:
        return
    arrived = lax.optimization_barrier((tuple(piece for _, piece in got), *tokens))[0]
    for (part, _), piece in zip(got, arrived):
        part.join(piece)


def finish_all(parts):
    while any(part.order for part in parts):
        join_all(parts, swap_all(parts))


def carried_states(states, decay, reverse, *covers, results=None):
    count = lax.axis_size("seq")
    sign = -1 if reverse else 1
    both = jnp.concatenate([states, decay], axis=0)
    results = [] if results is None else results

    def cover(reach, got):
        if len(results) == len(covers):
            return got
        result, token = covers[len(results)](reach)
        results.append(result)
        return after(got, token)

    def joined(near, far):
        through = near[LANES : LANES + 1]
        return jnp.concatenate([near[:LANES], jnp.zeros_like(near[LANES:])], axis=0) + through * far

    near, far = (from_behind(both, "seq", sign * k) for k in (1, 2))
    near, far = cover(both, (near, far))
    reach, width = joined(near, far), 2
    while width < count - 1:
        reach = joined(reach, cover(reach, from_behind(reach, "seq", sign * width)))
        width *= 2
    while len(results) < len(covers):
        cover(reach, reach)
    return reach[:LANES], results


def after(value, *tokens):
    return lax.optimization_barrier((value, *tokens))[0]


def from_behind(value, axis, steps):
    count = lax.axis_size(axis)
    initial, last = (max(0, -steps), min(count, count - steps))
    return lax.ppermute(value, axis, [(source, source + steps) for source in range(initial, last)])


def move_tiles(rows, index):
    tile_total = index.shape[0]
    shaped_rows = rows.reshape((tile_total, rows.shape[0] // tile_total) + rows.shape[1:])
    return jnp.take(shaped_rows, index, axis=0, mode="clip").reshape(rows.shape)


def carry_weights(decays, here, reverse):
    count = decays.shape[0]
    ids = jnp.arange(count, dtype=jnp.int32)
    if reverse:
        between = (ids[None, :] < ids[:, None]) & (ids[None, :] > here)
        reached = ids > here
    else:
        between = (ids[None, :] > ids[:, None]) & (ids[None, :] < here)
        reached = ids < here
    chain = jnp.prod(jnp.where(between[:, :, None], decays[None, :, :], 1.0), axis=1)
    return jnp.where(reached[:, None], chain, 0.0)


def padded_rows(parts, rows=8):
    stacked = jnp.concatenate([part.reshape(-1, part.shape[-1]) for part in parts], axis=0)
    return jnp.pad(stacked, ((0, rows - stacked.shape[0]), (0, 0)))


def local(
    tokens,
    packing,
    segment_ids,
    norm_gain,
    gate_proj,
    value_proj,
    shared_proj,
    step_proj,
    conv_value,
    conv_value_bias,
    conv_shared,
    conv_shared_bias,
    step_bias,
    log_decay,
    skip_gain,
    gated_gain,
    out_proj,
    cotangent,
):
    own_rows = tokens.shape[0]
    head_shards = lax.axis_size("head")
    seq_shards = lax.axis_size("seq")
    head_index = lax.axis_index("head")
    seq_index = lax.axis_index("seq")
    shard_rows = own_rows * head_shards
    inner_local = gate_proj.shape[1]
    heads_local = step_proj.shape[1]
    inner_width = inner_local * head_shards
    tile_rows = own_rows // seq_shards
    tile_count = shard_rows // tile_rows
    s = Sizes(shard_rows, inner_local, heads_local)

    packed_tiles = packing.reshape(-1, tile_rows)[:, 0] // tile_rows
    own_device = seq_index * head_shards + head_index
    seq_ids = jnp.arange(seq_shards, dtype=jnp.int32)
    own_tiles = own_device * seq_shards + seq_ids
    tile_match = (own_tiles[:, None] == packed_tiles[None, :]).astype(jnp.int32)
    tile_shard = jnp.arange(packed_tiles.shape[0], dtype=jnp.int32) // tile_count
    dest_shard = jnp.sum(tile_match * tile_shard[None, :], axis=1)
    send_index = jnp.sum(
        (dest_shard[None, :] == seq_ids[:, None]).astype(jnp.int32) * seq_ids[None, :], axis=1
    )
    own_packed = lax.dynamic_slice_in_dim(packed_tiles, seq_index * tile_count, tile_count, 0)
    source_device = own_packed // seq_shards
    arrival = source_device % head_shards * seq_shards + source_device // head_shards
    slot_ids = jnp.arange(tile_count, dtype=jnp.int32)
    back_index = jnp.sum(
        (arrival[None, :] == slot_ids[:, None]).astype(jnp.int32) * slot_ids[None, :], axis=1
    )

    shard_start = seq_index * shard_rows
    around = jnp.concatenate([jnp.full((RIM,), -1, jnp.int32), segment_ids])
    around = lax.dynamic_slice_in_dim(around, shard_start, shard_rows + RIM, 0)
    seg = around[RIM:]
    span_last = around[RIM - 1 :: ROWS]
    before_span = jnp.repeat(span_last[:-1], ROWS)
    end_of_span = jnp.repeat(span_last[1:], ROWS)
    facts = [around[RIM - k : RIM - k + shard_rows] == seg for k in (1, 2, 3)]
    facts += [before_span == seg, end_of_span == seg, seg, seg, seg]
    cols = jnp.stack([fact.astype(F32) for fact in facts], axis=1)
    seg_rows = jnp.broadcast_to(seg.astype(F32).reshape(s.spans, 1, ROWS), (s.spans, 8, ROWS))

    head_pad = ((0, 0), (0, LANES - heads_local))
    heads = padded_rows([step_bias, jnp.exp(log_decay)])
    heads = jnp.pad(heads, head_pad)
    conv_v = padded_rows([conv_value, conv_value_bias])
    conv_ss = padded_rows([conv_shared, conv_shared_bias])
    gains = padded_rows([jnp.repeat(skip_gain, inner_local // heads_local), gated_gain])
    ss_proj = jnp.concatenate([shared_proj, jnp.pad(step_proj, head_pad)], axis=1)

    tok_float = tokens.astype(F32)
    tok_rstd = lax.rsqrt(jnp.mean(tok_float * tok_float, axis=1, keepdims=True) + EPS)
    normed = (tok_float * tok_rstd * norm_gain[None, :]).astype(BF16)

    def to_shard(rows):
        sent = lax.all_to_all(
            move_tiles(rows, send_index), "seq", split_axis=0, concat_axis=0, tiled=True
        )
        return lax.all_gather(sent, "head", axis=0, tiled=True)

    packed_normed = move_tiles(to_shard(normed), arrival)
    arrived_cot = to_shard(cotangent)

    both = dot(packed_normed, jnp.concatenate([ss_proj, value_proj], axis=1))
    rim = from_behind(both[shard_rows - RIM :], "seq", 1)
    x, bc, step, run, run_t, state, decay = forward_states(
        s, both, rim, cols, conv_v, conv_ss, heads
    )

    def project_gate(reach):
        z = dot(after(packed_normed, reach), gate_proj)
        return z, z

    def within(reach):
        y = forward_within(s, after(x, reach), bc, step, run, run_t, cols, seg_rows)
        return y, y

    def cot_products(reach):
        cot = move_tiles(arrived_cot, after(arrival, reach))
        dgo = dot(cot, out_proj, CONTRACT_COLS)
        return (cot, dgo), dgo

    incoming, (gate_z, y, (packed_cot, dgo)) = carried_states(
        state[s.spans - 1], decay[s.spans - 1], False, project_gate, within, cot_products
    )
    scan, sums = forward_finish(
        s, y, x, gate_z, dgo, state, decay, incoming, bc, run, cols, gains
    )
    sums = lax.psum(jnp.stack([sums[:, 0, :], sums[:, 8, :]], axis=1), "head")
    sums = jnp.pad(sums, ((0, 0), (0, 6), (0, 0)))
    gated_low, low_gate, dy, grad, back, gate_rows = gate_back(
        s, inner_width, scan, x, gate_z, dgo, sums, bc, run, cols, gains
    )

    starts = lax.all_gather(jnp.concatenate([grad[0], decay[s.spans - 1]], axis=0), "seq")
    branch = branch_rows(arrival, back_index, gated_low, out_proj)
    dxw, dbc = backward_within(s, x, after(dy, branch), bc, step, run, run_t, cols, seg_rows)
    out_grads = dot(after(gated_low, dbc), packed_cot, CONTRACT_ROWS).astype(BF16)
    gate_grads = dot(after(packed_normed, out_grads), low_gate, CONTRACT_ROWS).astype(BF16)
    branch = lax.psum_scatter(branch, "head", scatter_dimension=0, tiled=True)
    out_sum = RowsOverSeq(out_grads, seq_index, True)
    gate_sum = RowsOverSeq(gate_grads, seq_index, False)
    early = [out_sum, gate_sum]
    got = swap_all(early)
    decays = starts[:, LANES, :]
    outgoing = jnp.sum(
        carry_weights(decays, seq_index, True)[:, None, :] * starts[:, :LANES, :], axis=0
    )
    dy = after(dy, gate_grads, *[part.keep for part in early], *[part.send for part in early])
    low_value, tail, rim_out, taps_v, low_ss, tail_ss, rim_ss_out, taps_ss, small = backward_finish(
        s, both, rim, x, dy, scan, dxw, dbc, state, decay, incoming, grad, back,
        outgoing, bc, step, run, cols, conv_v, conv_ss, heads, gains,
    )
    join_all(early, got, small)
    got = swap_all(early)
    rim_out = after(rim_out, *[part.send for part in early])
    rim_back = from_behind(jnp.concatenate([rim_out, rim_ss_out], axis=1), "seq", -1)
    tail = (jnp.concatenate([tail, tail_ss], axis=1) + rim_back).astype(BF16)
    low_value = lax.dynamic_update_slice(low_value, tail[:, :inner_local], (shard_rows - RIM, 0))
    low_ss = lax.dynamic_update_slice(low_ss, tail[:, inner_local:], (shard_rows - RIM, 0))

    ss_grads = dot(packed_normed, low_ss, CONTRACT_ROWS)
    shared_sum = Chain(
        RowsOverSeq(ss_grads[:, : 2 * LANES], seq_index, False), lambda total: SumByHalves(total, "head")
    )
    step_rows = RowsOverSeq(ss_grads[:, 2 * LANES :].astype(BF16), seq_index, False)
    got += swap_all([shared_sum, step_rows])
    low_gate = after(low_gate, ss_grads)
    d_normed, grad_norm_rows = normed_grad(
        arrival,
        back_index,
        (low_gate, low_value, low_ss),
        (gate_proj, value_proj, ss_proj),
        packed_normed,
    )
    gate_rows, small, taps_v, taps_ss = after((gate_rows, small, taps_v, taps_ss), d_normed)
    arrived, low_value = lax.optimization_barrier(
        (tuple(piece for _, piece in got), after(low_value, d_normed))
    )
    d_normed = lax.psum_scatter(
        after(d_normed, branch), "head", scatter_dimension=0, tiled=True
    )
    for (part, _), piece in zip(got, arrived):
        part.join(piece)
    value_grads = dot(packed_normed, low_value, CONTRACT_ROWS).astype(BF16)

    per_head = [jnp.sum(gate_rows[1].reshape(heads_local, -1), axis=1)]
    per_head += [small[0, :heads_local], small[1, :heads_local]]
    pieces = [taps_v[:5].reshape(-1), gate_rows[0]] + per_head
    own_size = sum(piece.shape[0] for piece in pieces)
    shared_pieces = [taps_ss[:5].reshape(-1), grad_norm_rows]
    flat_sum = Chain(
        SumByPairs(jnp.concatenate(pieces + shared_pieces), "seq"),
        lambda total: SumByPairs(total[own_size:], "head"),
    )
    half = inner_local // 2
    short = [shared_sum, flat_sum, step_rows]
    got = swap_all(short)
    arrived, value_grads = lax.optimization_barrier((tuple(piece for _, piece in got), value_grads))
    for (part, _), piece in zip(got, arrived):
        part.join(piece)
    values = [
        RowsOverSeq(value_grads[:, :half], seq_index, False),
        RowsOverSeq(value_grads[:, half:], seq_index, True),
    ]
    beside = [values, [], values, [], values]
    while any(part.order for part in short):
        got = swap_all(short + (beside.pop(0) if beside else []))
        if len(beside) == 1:
            arrived, branch_back = lax.optimization_barrier(
                (tuple(piece for _, piece in got), branch_back)
            )
            got = [(part, piece) for (part, _), piece in zip(got, arrived)]
        join_all(None, got)
        if len(beside) == 3:
            branch = after(branch, shared_sum.total)
            branch_back = lax.all_to_all(branch, "seq", split_axis=0, concat_axis=0, tiled=True)
    last = swap_all(early)
    normed_back = lax.all_to_all(d_normed, "seq", split_axis=0, concat_axis=0, tiled=True)
    arrived, normed_back = lax.optimization_barrier(
        (tuple(piece for _, piece in last), normed_back)
    )
    for (part, _), piece in zip(last, arrived):
        part.join(piece)
    finish_all(values + early)
    everything, grad_shared, shared_sums = flat_sum.totals[0], shared_sum.total, flat_sum.total
    grad_out_proj, grad_gate = out_sum.total, gate_sum.total
    grad_value = jnp.concatenate([part.total for part in values], axis=1)
    grad_step_proj = step_rows.total[:, :heads_local]
    grad_shared = lax.all_gather(grad_shared, "seq", axis=0, tiled=True).astype(F32)

    branch_given = move_tiles(branch_back, dest_shard).astype(F32)
    d_normed_given = move_tiles(normed_back, dest_shard).astype(F32)
    mixed_rows = (tok_float + branch_given).astype(BF16)
    scaled = d_normed_given * norm_gain[None, :]
    row_dot = jnp.sum(scaled * tok_float, axis=1, keepdims=True) / tokens.shape[1]
    d_tok = tok_rstd * scaled - tok_float * (tok_rstd * tok_rstd * tok_rstd * row_dot)
    grad_tokens = (cotangent.astype(F32) + d_tok).astype(BF16)

    own_taps = everything[: 5 * inner_local].reshape(5, inner_local)
    rest = everything[5 * inner_local : own_size]
    grad_gated = rest[:inner_local]
    rest = rest[inner_local:]
    grad_skip = rest[:heads_local]
    grad_step_bias = rest[heads_local : 2 * heads_local]
    grad_log_decay = rest[2 * heads_local :]
    shared_taps = shared_sums[: 10 * LANES].reshape(5, 2 * LANES)
    grad_norm_gain = shared_sums[10 * LANES : 10 * LANES + norm_gain.shape[0]] / norm_gain
    return (
        mixed_rows,
        grad_tokens,
        grad_norm_gain,
        grad_gate,
        grad_value,
        grad_shared,
        grad_step_proj,
        own_taps[:4],
        own_taps[4],
        shared_taps[:4],
        shared_taps[4],
        grad_step_bias,
        grad_log_decay,
        grad_skip,
        grad_gated,
        grad_out_proj,
    )


def solution(mesh):
    placed = (
        P(("seq", "head"), None),
        P(),
        P(),
        P(),
        P(None, "head"),
        P(None, "head"),
        P(),
        P(None, "head"),
        P(None, "head"),
        P("head"),
        P(),
        P(),
        P("head"),
        P("head"),
        P("head"),
        P("head"),
        P("head", None),
        P(("seq", "head"), None),
    )
    return jax.shard_map(
        local,
        mesh=mesh,
        in_specs=placed,
        out_specs=(
            P(("seq", "head"), None),
            P(("seq", "head"), None),
            P(),
            P("seq", "head"),
            P("seq", "head"),
            P(),
            P("seq", "head"),
            P(None, "head"),
            P("head"),
            P(),
            P(),
            P("head"),
            P("head"),
            P("head"),
            P("head"),
            P(("head", "seq"), None),
        ),
        check_vma=False,
    )
```

```python
import jax
import jax.numpy as jnp
from jax import lax
from jax.experimental import pallas as pl
from jax.experimental.pallas import tpu as pltpu
from jax.sharding import PartitionSpec as P

EPS = 1e-05
ROWS = 128
LANES = 128
HALF = 64
RIM = 8
FAR = -1e30
UNROLL = 8
F32 = jnp.float32
BF16 = jnp.bfloat16
VMEM_BYTES = 56 * 1024 * 1024
CONTRACT_ROWS = (((0,), (0,)), ((), ()))
CONTRACT_COLS = (((1,), (1,)), ((), ()))


def dot(a, b, dims=(((1,), (0,)), ((), ()))):
    return lax.dot_general(a, b, dims, preferred_element_type=F32)


def two_parts(x):
    upper = x.astype(BF16)
    return upper, (x - upper.astype(F32)).astype(BF16)


def three_parts(x):
    upper, rest = x.astype(BF16), x
    rest = x - upper.astype(F32)
    middle = rest.astype(BF16)
    return upper, middle, (rest - middle.astype(F32)).astype(BF16)


def in_two(x):
    return jnp.concatenate(two_parts(x), axis=1)


def twice(x):
    return jnp.concatenate([x, x], axis=0)


def b_parts(bc_ref, at):
    return bc_ref[at, : 2 * LANES]


def c_parts(bc_ref, at):
    return bc_ref[at, 2 * LANES :]


def cross_product(bc_ref, at):
    b, c = b_parts(bc_ref, at), c_parts(bc_ref, at)
    upper = jnp.concatenate([b[:, :LANES], b[:, :LANES]], axis=1)
    return dot(c, upper, CONTRACT_COLS) + dot(c[:, :LANES], b[:, LANES:], CONTRACT_COLS)


def lane_ids(rows):
    return lax.broadcasted_iota(jnp.int32, (rows, LANES), 1)


def row_ids(rows):
    return lax.broadcasted_iota(jnp.int32, (rows, LANES), 0)


def from_head(block, head):
    index = head + jnp.zeros(block.shape, jnp.int32)
    return jnp.take_along_axis(block, index, axis=1)


def head_cols(block, pair):
    return from_head(block, 2 * pair), from_head(block, 2 * pair + 1)


def head_pair(block, pair):
    return from_head(block, 2 * pair + jnp.where(lane_ids(block.shape[0]) < HALF, 0, 1))


def head_selector(pair):
    lane = row_ids(LANES)
    head = 2 * pair + jnp.where(lane < HALF, 0, 1)
    return (lane_ids(LANES) == head).astype(F32).astype(BF16)


def split_sum(x, selector):
    upper, lower = two_parts(x)
    stacked = jnp.concatenate([upper, lower], axis=1)
    return dot(stacked, jnp.concatenate([selector, selector], axis=0))


def lower_ones():
    return (row_ids(ROWS) >= lane_ids(ROWS)).astype(F32).astype(BF16)


def upper_ones():
    return (row_ids(ROWS) <= lane_ids(ROWS)).astype(F32).astype(BF16)


def spread(ref, row, col):
    return jnp.broadcast_to(ref[pl.ds(row, ROWS), col : col + 1], (ROWS, LANES))


def softplus(x):
    return jnp.maximum(x, 0.0) + jnp.log1p(jnp.exp(-jnp.abs(x)))


def sigmoid(x):
    return 1.0 / (1.0 + jnp.exp(-x))


def span_start(q):
    return pl.multiple_of(q * ROWS, ROWS)


def loop(count, body):
    def step(q, carry):
        body(q)
        return carry

    lax.fori_loop(0, count, step, 0, unroll=UNROLL)


def conv_span(pad_ref, same_ref, row, taps, bias):
    long = pad_ref[pl.ds(row, ROWS + RIM), :]
    total = bias + taps[3:4] * long[RIM:]
    shifted = []
    for back in (1, 2, 3):
        moved = pad_ref[pl.ds(row + RIM - back, ROWS), :]
        moved = moved * same_ref[back - 1, pl.ds(row, ROWS), :]
        shifted.append(moved)
        total = total + taps[3 - back : 4 - back] * moved
    return total, [long[RIM:]] + shifted


def forward_states_kernel(
    value_ref, ss_ref, rim_v_ref, rim_ss_ref, cols_ref, conv_ref, conv_ss_ref, heads_ref,
    x_ref, bc_ref, step_ref, run_ref, run_t_ref, state_ref, decay_ref,
    pad, same, cont, last, bt,
):
    pair = pl.program_id(0)
    rows = value_ref.shape[0]
    spans = rows // ROWS
    width = run_t_ref.shape[1]

    @pl.when(pair == 0)
    def _():
        def masks(q):
            row = span_start(q)
            for k in range(3):
                same[k, pl.ds(row, ROWS), :] = spread(cols_ref, row, k)
            cont[pl.ds(row, ROWS), :] = spread(cols_ref, row, 3)
            last[pl.ds(row, ROWS), :] = spread(cols_ref, row, 4)

        loop(spans, masks)
        for part in range(2):
            lanes = slice(part * LANES, (part + 1) * LANES)
            pad[0:RIM, :] = rim_ss_ref[:, lanes]
            pad[RIM:, :] = ss_ref[:, lanes]
            taps, bias = conv_ss_ref[0:4, lanes], conv_ss_ref[4:5, lanes]

            def shared(q):
                row = span_start(q)
                pre, _ = conv_span(pad, same, row, taps, bias)
                act = pre * sigmoid(pre)
                bc_ref[pl.ds(row, ROWS), 2 * part * LANES : 2 * (part + 1) * LANES] = in_two(act)
                if part == 0:
                    bt[q] = in_two(jnp.transpose(act))

            loop(spans, shared)

        bias, rate = heads_ref[0:1, :], heads_ref[1:2, :]
        tri, tri_t = lower_ones(), upper_ones()

        def steps(q):
            row = span_start(q)
            size = softplus(ss_ref[pl.ds(row, ROWS), 2 * LANES :] + bias)
            step_ref[pl.ds(row, ROWS), :] = size
            parts = three_parts(-size * rate)
            run_ref[pl.ds(row, ROWS), :] = sum(dot(tri, part) for part in parts)
            turned = sum(dot(part, tri_t, CONTRACT_ROWS) for part in parts)
            run_t_ref[q] = turned[:width]

        loop(spans, steps)

    pad[0:RIM, :] = rim_v_ref[...]
    pad[RIM:, :] = value_ref[...]
    taps, bias = conv_ref[0:4], conv_ref[4:5]

    def span(q, carry):
        state, decay = carry
        row = span_start(q)
        at = pl.ds(row, ROWS)
        pre, _ = conv_span(pad, same, row, taps, bias)
        x = pre * sigmoid(pre)
        x_ref[at, :] = x
        size = head_pair(step_ref[at, :], pair)
        run = head_pair(run_ref[at, :], pair)
        enter = jnp.exp(run[ROWS - 1 :]) * cont[pl.ds(row + ROWS - 8, 8), :][7:8]
        to_end = jnp.exp(run[ROWS - 1 :] - run) * last[at, :]
        state = state * enter + dot(bt[q], twice((x * size * to_end).astype(BF16)))
        decay = decay * enter
        state_ref[q] = state
        decay_ref[q] = jnp.broadcast_to(decay, (8, LANES))
        return state, decay

    lax.fori_loop(
        0, spans, span, (jnp.zeros((LANES, LANES), F32), jnp.ones((1, LANES), F32)),
        unroll=UNROLL,
    )


def span_masks(cols_ref, seg_rows_ref, bias_ref, spans):
    causal = row_ids(ROWS) >= lane_ids(ROWS)

    def mask(q):
        own = spread(cols_ref, span_start(q), 5)
        other = jnp.broadcast_to(seg_rows_ref[q, 0:1, :], (ROWS, ROWS))
        bias_ref[q] = jnp.where(causal & (own == other), 0.0, FAR)

    loop(spans, mask)


def decay_pair(run_ref, run_t_ref, mask_ref, q, pair):
    first, second = head_cols(run_ref[pl.ds(span_start(q), ROWS), :], pair)
    rows = run_t_ref[q, pl.ds(2 * pair, 2), :]
    mask = mask_ref[q]
    return jnp.exp(first - rows[0:1] + mask), jnp.exp(second - rows[1:2] + mask)


def heads_apart(x):
    lane = lane_ids(x.shape[0])
    zero = jnp.zeros_like(x)
    return jnp.concatenate([jnp.where(lane < HALF, x, zero), jnp.where(lane < HALF, zero, x)], axis=0)


def forward_within_kernel(
    x_ref, bc_ref, step_ref, run_ref, run_t_ref, cols_ref, seg_rows_ref, y_ref, mask, cross
):
    pair = pl.program_id(0)
    spans = x_ref.shape[0] // ROWS

    @pl.when(pair == 0)
    def _():
        span_masks(cols_ref, seg_rows_ref, mask, spans)

        def products(q):
            at = pl.ds(span_start(q), ROWS)
            cross[q] = cross_product(bc_ref, at)

        loop(spans, products)

    def span(q):
        at = pl.ds(span_start(q), ROWS)
        size = head_pair(step_ref[at, :], pair)
        weighted = x_ref[at, :] * size
        first, second = decay_pair(run_ref, run_t_ref, mask, q, pair)
        mix = jnp.concatenate([first * cross[q], second * cross[q]], axis=1).astype(BF16)
        y_ref[at, :] = dot(mix, heads_apart(weighted).astype(BF16))

    loop(spans, span)


def entering(state_ref, decay_ref, incoming, q, before):
    at = jnp.maximum(before, 0)
    local = state_ref[at] + decay_ref[at, 0:1, :] * incoming
    return jnp.where(before >= 0, local, incoming)


def row_sums(acc_ref, out_ref, base, spans):
    ones = jnp.ones((8, LANES), BF16)

    def total(q):
        parts = three_parts(acc_ref[pl.ds(span_start(q), ROWS), :])
        out_ref[q, base : base + 8, :] = sum(dot(ones, part, CONTRACT_COLS) for part in parts)

    loop(spans, total)


def forward_finish_kernel(
    y_ref, x_ref, z_ref, dgo_ref, state_ref, decay_ref, in_ref, bc_ref, run_ref, cols_ref, gains_ref,
    scan_ref, sums_ref, cont, squares, inner,
):
    pair = pl.program_id(0)
    spans = y_ref.shape[0] // ROWS

    @pl.when(pair == 0)
    def _():
        def masks(q):
            row = span_start(q)
            cont[pl.ds(row, ROWS), :] = spread(cols_ref, row, 3)

        loop(spans, masks)
        squares[...] = jnp.zeros_like(squares)
        inner[...] = jnp.zeros_like(inner)

    incoming = in_ref[...]
    skip, gain = gains_ref[0:1], gains_ref[1:2]

    def span(q):
        at = pl.ds(span_start(q), ROWS)
        run = head_pair(run_ref[at, :], pair)
        state = entering(state_ref, decay_ref, incoming, q, q - 1)
        upper, lower = two_parts(state)
        c = c_parts(bc_ref, at)
        carried = dot(c, twice(upper)) + dot(c[:, :LANES], lower)
        scan = y_ref[at, :] + carried * (jnp.exp(run) * cont[at, :])
        scan_ref[at, :] = scan
        z = z_ref[at, :]
        gated = (scan + skip * x_ref[at, :]) * (z * sigmoid(z))
        squares[at, :] += gated * gated
        inner[at, :] += gain * dgo_ref[at, :] * gated

    loop(spans, span)

    @pl.when(pair == pl.num_programs(0) - 1)
    def _():
        row_sums(squares, sums_ref, 0, spans)
        row_sums(inner, sums_ref, 8, spans)


def gate_back_kernel(
    inner_width,
    scan_ref, x_ref, z_ref, dgo_ref, sums_ref, bc_ref, run_ref, cols_ref, gains_ref,
    out_ref, dz_ref, dy_ref, grad_ref, decay_ref, rows_ref,
    cont, rstd, coef, ct,
):
    pair = pl.program_id(0)
    spans = scan_ref.shape[0] // ROWS

    @pl.when(pair == 0)
    def _():
        def masks(q):
            row = span_start(q)
            at = pl.ds(row, ROWS)
            cont[at, :] = spread(cols_ref, row, 3)
            ct[q] = jnp.concatenate(
                [
                    jnp.transpose(bc_ref[at, k * LANES : (k + 1) * LANES].astype(F32)).astype(BF16)
                    for k in (2, 3)
                ],
                axis=1,
            )
            square = jnp.broadcast_to(sums_ref[q, 0:1, :], (ROWS, LANES))
            cross = jnp.broadcast_to(sums_ref[q, 1:2, :], (ROWS, LANES))
            root = lax.rsqrt(square / inner_width + EPS)
            rstd[at, :] = jnp.transpose(root)
            coef[at, :] = jnp.transpose(root * root * root * cross / inner_width)

        loop(spans, masks)

    skip, gain = gains_ref[0:1], gains_ref[1:2]
    rows_ref[...] = jnp.zeros_like(rows_ref)

    def span(k, carry):
        leaving, decay = carry
        q = spans - 1 - k
        at = pl.ds(span_start(q), ROWS)
        x, z, dgo = x_ref[at, :], z_ref[at, :], dgo_ref[at, :]
        scanned = scan_ref[at, :] + skip * x
        gate = sigmoid(z)
        silu = z * gate
        gated = scanned * silu
        normed = gated * rstd[at, :]
        out_ref[at, :] = (normed * gain).astype(BF16)
        d_gated = rstd[at, :] * (dgo * gain) - gated * coef[at, :]
        d_scan = d_gated * silu
        dz_ref[at, :] = (d_gated * scanned * (gate * (1.0 + z * (1.0 - gate)))).astype(BF16)
        dy_ref[at, :] = d_scan
        rows_ref[0:1] += jnp.sum(dgo * normed, axis=0, keepdims=True)
        rows_ref[1:2] += jnp.sum(d_scan * x, axis=0, keepdims=True)
        run = head_pair(run_ref[at, :], pair)
        enter = jnp.exp(run) * cont[at, :]
        upper, lower = two_parts(d_scan * enter)
        turned = ct[q]
        leaving = leaving * enter[ROWS - 1 :] + dot(turned, twice(upper)) + dot(turned[:, :ROWS], lower)
        decay = decay * enter[ROWS - 1 :]
        grad_ref[q] = leaving
        decay_ref[q] = jnp.broadcast_to(decay, (8, LANES))
        return leaving, decay

    lax.fori_loop(
        0, spans, span, (jnp.zeros((LANES, LANES), F32), jnp.ones((1, LANES), F32)),
        unroll=UNROLL,
    )


def backward_within_kernel(
    x_ref, dy_ref, bc_ref, step_ref, run_ref, run_t_ref, cols_ref, seg_rows_ref,
    dxw_ref, dbc_ref, mask, cross, d_cross,
):
    pair = pl.program_id(0)
    spans = x_ref.shape[0] // ROWS

    @pl.when(pair == 0)
    def _():
        span_masks(cols_ref, seg_rows_ref, mask, spans)

        def products(q):
            at = pl.ds(span_start(q), ROWS)
            cross[q] = cross_product(bc_ref, at)
            d_cross[q] = jnp.zeros((ROWS, ROWS), F32)

        loop(spans, products)

    def span(q):
        at = pl.ds(span_start(q), ROWS)
        size = head_pair(step_ref[at, :], pair)
        weighted = (x_ref[at, :] * size).astype(BF16)
        first, second = decay_pair(run_ref, run_t_ref, mask, q, pair)
        dy, dy_rest = two_parts(dy_ref[at, :])
        apart = heads_apart(dy)
        both = jnp.concatenate([apart, heads_apart(dy_rest)], axis=1)
        d_mix = dot(both, jnp.concatenate([weighted, weighted], axis=1), CONTRACT_COLS)
        d_cross[q] += first * d_mix[:ROWS] + second * d_mix[ROWS:]
        mix = jnp.concatenate([first * cross[q], second * cross[q]], axis=0).astype(BF16)
        dxw_ref[at, :] = dot(mix, apart, CONTRACT_ROWS)

    loop(spans, span)

    @pl.when(pair == pl.num_programs(0) - 1)
    def _():
        def shared(q):
            at = pl.ds(span_start(q), ROWS)
            grad = d_cross[q].astype(BF16)
            b, c = b_parts(bc_ref, at), c_parts(bc_ref, at)
            both = dot(grad, c, CONTRACT_ROWS)
            dbc_ref[at, :LANES] = both[:, :LANES] + both[:, LANES:]
            both = dot(grad, b)
            dbc_ref[at, LANES:] = both[:, :LANES] + both[:, LANES:]

        loop(spans, shared)


def conv_back(pad_ref, d_pre, same, taps, spans, store, rim_store):
    def span(q):
        at = pl.ds(span_start(q), ROWS + RIM)
        long = d_pre[at, :]
        total = taps[3:4] * long[:ROWS]
        for ahead in (1, 2, 3):
            start = span_start(q) + ahead
            moved = d_pre[pl.ds(start, ROWS), :] * same[ahead - 1, pl.ds(start, ROWS), :]
            total = total + taps[3 - ahead : 4 - ahead] * moved
        store(q, total)

    loop(spans, span)
    head = d_pre[0:RIM, :]
    total = jnp.zeros((RIM, LANES), F32)
    for ahead in (1, 2, 3):
        masked = head * same[ahead - 1, 0:RIM, :]
        both = jnp.concatenate([jnp.zeros((RIM, LANES), F32), masked], axis=0)
        total = total + taps[3 - ahead : 4 - ahead] * pltpu.roll(both, 2 * RIM - ahead, axis=0)[:RIM]
    rim_store(total)


def tap_sums(d_pre, shifted):
    sums = [jnp.sum(d_pre * shifted[3 - k], axis=0, keepdims=True) for k in range(4)]
    sums.append(jnp.sum(d_pre, axis=0, keepdims=True))
    return jnp.concatenate(sums + [jnp.zeros((3, LANES), F32)], axis=0)


def silu_grad(pre):
    gate = sigmoid(pre)
    return gate * (1.0 + pre * (1.0 - gate))


def backward_finish_kernel(
    value_ref, ss_ref, rim_v_ref, rim_ss_ref, x_ref, dy_ref, scan_ref, dxw_ref, dbc_ref,
    state_ref, decay_ref, in_ref, grad_ref, back_ref, out_ref,
    bc_ref, step_ref, run_ref, cols_ref, conv_ref, conv_ss_ref, heads_ref, gains_ref,
    low_ref, tail_ref, rim_ref, taps_ref, low_ss_ref, tail_ss_ref, rim_ss_out_ref, taps_ss_ref, small_ref,
    pad, d_pre, same, cont, last, d_run, d_step, d_bc,
):
    pair = pl.program_id(0)
    rows = value_ref.shape[0]
    spans = rows // ROWS

    @pl.when(pair == 0)
    def _():
        def masks(q):
            row = span_start(q)
            for k in range(3):
                same[k, pl.ds(row, ROWS), :] = spread(cols_ref, row, k)
            cont[pl.ds(row, ROWS), :] = spread(cols_ref, row, 3)
            last[pl.ds(row, ROWS), :] = spread(cols_ref, row, 4)

        loop(spans, masks)
        same[:, rows:, :] = jnp.zeros((3, RIM, LANES), F32)
        d_pre[rows:, :] = jnp.zeros((RIM, LANES), F32)
        d_run[...] = jnp.zeros_like(d_run)
        d_step[...] = jnp.zeros_like(d_step)
        d_bc[...] = dbc_ref[...]

    pad[0:RIM, :] = rim_v_ref[...]
    pad[RIM:, :] = value_ref[...]
    taps, bias = conv_ref[0:4], conv_ref[4:5]
    skip = gains_ref[0:1]
    incoming, outgoing = in_ref[...], out_ref[...]
    selector = head_selector(pair)
    taps_ref[...] = jnp.zeros_like(taps_ref)
    final_row = row_ids(ROWS) == ROWS - 1

    def span(q):
        row = span_start(q)
        at = pl.ds(row, ROWS)
        x, dy = x_ref[at, :], dy_ref[at, :]
        size = head_pair(step_ref[at, :], pair)
        run = head_pair(run_ref[at, :], pair)
        enter = jnp.exp(run) * cont[at, :]
        to_end = jnp.exp(run[ROWS - 1 :] - run) * last[at, :]
        state, state_rest = two_parts(entering(state_ref, decay_ref, incoming, q, q - 1))
        after = state_ref[q] + decay_ref[q, 0:1, :] * incoming
        ahead = jnp.minimum(q + 1, spans - 1)
        grad = jnp.where(
            q + 1 < spans, grad_ref[ahead] + back_ref[ahead, 0:1, :] * outgoing, outgoing
        )
        weighted = x * size
        low_grad = grad.astype(BF16)
        d_weighted = dxw_ref[at, :] + to_end * dot(b_parts(bc_ref, at), twice(low_grad))
        entered = in_two(dy * enter)
        d_bc[at, LANES:] += dot(
            entered, jnp.concatenate([state, state], axis=1), CONTRACT_COLS
        ) + dot(entered[:, :LANES], state_rest, CONTRACT_COLS)
        d_bc[at, :LANES] += dot((weighted * to_end).astype(BF16), low_grad, CONTRACT_COLS)
        turn = dy.astype(BF16).astype(F32) * scan_ref[at, :]
        turn = turn - d_weighted * weighted.astype(BF16).astype(F32)
        turn = turn + jnp.where(final_row, jnp.sum(grad * after, axis=0, keepdims=True), 0.0)
        d_run[at, :] += split_sum(turn, selector)
        d_step[at, :] += split_sum(d_weighted * x, selector)
        pre, shifted = conv_span(pad, same, row, taps, bias)
        d_act = (d_weighted * size + skip * dy) * silu_grad(pre)
        d_pre[at, :] = d_act
        taps_ref[...] += tap_sums(d_act, shifted)

    loop(spans, span)

    def keep(q, total):
        low_ref[pl.ds(span_start(q), ROWS), :] = total.astype(BF16)

        @pl.when(q == spans - 1)
        def _():
            tail_ref[...] = total[ROWS - RIM :]

    def keep_rim(total):
        rim_ref[...] = total

    conv_back(pad, d_pre, same, taps, spans, keep, keep_rim)

    @pl.when(pair == pl.num_programs(0) - 1)
    def _():
        for part in range(2):
            lanes = slice(part * LANES, (part + 1) * LANES)
            pad[0:RIM, :] = rim_ss_ref[:, lanes]
            pad[RIM:, :] = ss_ref[:, lanes]
            part_taps, part_bias = conv_ss_ref[0:4, lanes], conv_ss_ref[4:5, lanes]
            taps_ss_ref[:, lanes] = jnp.zeros((8, LANES), F32)

            def shared(q):
                row = span_start(q)
                at = pl.ds(row, ROWS)
                pre, shifted = conv_span(pad, same, row, part_taps, part_bias)
                d_act = d_bc[at, lanes] * silu_grad(pre)
                d_pre[at, :] = d_act
                taps_ss_ref[:, lanes] += tap_sums(d_act, shifted)

            loop(spans, shared)

            def keep_ss(q, total):
                low_ss_ref[pl.ds(span_start(q), ROWS), lanes] = total.astype(BF16)

                @pl.when(q == spans - 1)
                def _():
                    tail_ss_ref[:, lanes] = total[ROWS - RIM :]

            def keep_rim_ss(total):
                rim_ss_out_ref[:, lanes] = total

            conv_back(pad, d_pre, same, part_taps, spans, keep_ss, keep_rim_ss)

        step_bias, rate = heads_ref[0:1, :], heads_ref[1:2, :]
        small_ref[...] = jnp.zeros_like(small_ref)
        tri_t = upper_ones()

        def steps(q):
            at = pl.ds(span_start(q), ROWS)
            d_decay = sum(dot(tri_t, part) for part in three_parts(d_run[at, :]))
            slope = sigmoid(ss_ref[at, 2 * LANES :] + step_bias)
            d_raw = (d_step[at, :] - d_decay * rate) * slope
            low_ss_ref[at, 2 * LANES :] = d_raw.astype(BF16)
            small_ref[0:1] += jnp.sum(d_raw, axis=0, keepdims=True)
            small_ref[1:2] -= jnp.sum(d_decay * step_ref[at, :] * rate, axis=0, keepdims=True)

        loop(spans, steps)


def store_tiles(slots_ref, out_ref, value, scatter):
    if not scatter:
        out_ref[...] = value
        return
    tile = value.shape[0] // slots_ref.shape[0]
    for k in range(slots_ref.shape[0]):
        start = pl.multiple_of(slots_ref[k] * tile, tile)
        out_ref[pl.ds(start, tile), :] = value[k * tile : (k + 1) * tile]


def branch_kernel(scatter, slots_ref, rows_ref, weight_ref, out_ref):
    store_tiles(slots_ref, out_ref, dot(rows_ref[...], weight_ref[...]).astype(BF16), scatter)


def normed_grad_kernel(
    scatter, slots_ref, gate_ref, value_ref, ss_ref, gate_w, value_w, ss_w, normed_ref, out_ref, diag_ref
):
    total = dot(gate_ref[...], gate_w[...], CONTRACT_COLS)
    total = total + dot(value_ref[...], value_w[...], CONTRACT_COLS)
    total = total + dot(ss_ref[...], ss_w[...], CONTRACT_COLS)
    store_tiles(slots_ref, out_ref, total.astype(BF16), scatter)
    sums = jnp.sum(total * normed_ref[...].astype(F32), axis=0, keepdims=True)
    diag_ref[...] = jnp.broadcast_to(sums, diag_ref.shape)


def whole(shape):
    return pl.BlockSpec(shape, lambda j: (0,) * len(shape))


def columns(rows, width=LANES):
    return pl.BlockSpec((rows, width), lambda j: (0, j))


def value_columns(rows):
    return pl.BlockSpec((rows, LANES), lambda j: (0, j + 3))


def stacks(count, rows):
    return pl.BlockSpec((count, rows, LANES), lambda j: (0, 0, j))


def params():
    return pltpu.CompilerParams(vmem_limit_bytes=VMEM_BYTES, dimension_semantics=("arbitrary",))


def shaped(shape, dtype):
    return jax.ShapeDtypeStruct(shape, dtype)


def scratch(*shape, dtype=F32):
    return pltpu.VMEM(shape, dtype)


class Sizes:
    def __init__(self, rows, inner, heads):
        self.rows, self.inner, self.heads = rows, inner, heads
        self.spans, self.pairs = rows // ROWS, inner // LANES
        self.width = max(8, heads)

    def cost(self):
        cells = self.rows * self.inner
        return pl.CostEstimate(flops=1, bytes_accessed=1, transcendentals=0)


def forward_states(s, both, rim, cols, conv_v, conv_ss, heads):
    return pl.pallas_call(
        forward_states_kernel,
        grid=(s.pairs,),
        in_specs=[
            value_columns(s.rows), whole((s.rows, 3 * LANES)), value_columns(RIM), whole((RIM, 3 * LANES)),
            whole((s.rows, 8)), columns(8), whole((8, 2 * LANES)), whole((8, LANES)),
        ],
        out_specs=[
            columns(s.rows), whole((s.rows, 4 * LANES)), whole((s.rows, LANES)), whole((s.rows, LANES)),
            whole((s.spans, s.width, LANES)), stacks(s.spans, LANES), stacks(s.spans, 8),
        ],
        out_shape=[
            shaped((s.rows, s.inner), F32), shaped((s.rows, 4 * LANES), BF16),
            shaped((s.rows, LANES), F32), shaped((s.rows, LANES), F32),
            shaped((s.spans, s.width, LANES), F32),
            shaped((s.spans, LANES, s.inner), F32), shaped((s.spans, 8, s.inner), F32),
        ],
        scratch_shapes=[
            scratch(s.rows + RIM, LANES), scratch(3, s.rows, LANES), scratch(s.rows, LANES),
            scratch(s.rows, LANES), scratch(s.spans, LANES, 2 * ROWS, dtype=BF16),
        ],
        compiler_params=params(),
        cost_estimate=s.cost(),
        name="forward_states",
    )(both, both, rim, rim, cols, conv_v, conv_ss, heads)


def forward_within(s, x, bc, step, run, run_t, cols, seg_rows):
    return pl.pallas_call(
        forward_within_kernel,
        grid=(s.pairs,),
        in_specs=[
            columns(s.rows), whole((s.rows, 4 * LANES)), whole((s.rows, LANES)), whole((s.rows, LANES)),
            whole((s.spans, s.width, LANES)), whole((s.rows, 8)), whole((s.spans, 8, LANES)),
        ],
        out_specs=columns(s.rows),
        out_shape=shaped((s.rows, s.inner), F32),
        scratch_shapes=[scratch(s.spans, ROWS, ROWS), scratch(s.spans, ROWS, ROWS)],
        compiler_params=params(),
        cost_estimate=s.cost(),
        name="forward_within",
    )(x, bc, step, run, run_t, cols, seg_rows)


def forward_finish(s, y, x, z, dgo, state, decay, incoming, bc, run, cols, gains):
    return pl.pallas_call(
        forward_finish_kernel,
        grid=(s.pairs,),
        in_specs=[
            columns(s.rows), columns(s.rows), columns(s.rows), columns(s.rows),
            stacks(s.spans, LANES), stacks(s.spans, 8), columns(LANES),
            whole((s.rows, 4 * LANES)), whole((s.rows, LANES)), whole((s.rows, 8)), columns(8),
        ],
        out_specs=[columns(s.rows), whole((s.spans, 16, LANES))],
        out_shape=[shaped((s.rows, s.inner), F32), shaped((s.spans, 16, LANES), F32)],
        scratch_shapes=[scratch(s.rows, LANES)] * 3,
        compiler_params=params(),
        cost_estimate=s.cost(),
        name="forward_finish",
    )(y, x, z, dgo, state, decay, incoming, bc, run, cols, gains)


def gate_back(s, inner_width, scan, x, z, dgo, sums, bc, run, cols, gains):
    def kernel(*refs):
        gate_back_kernel(inner_width, *refs)

    return pl.pallas_call(
        kernel,
        grid=(s.pairs,),
        in_specs=[
            columns(s.rows), columns(s.rows), columns(s.rows), columns(s.rows),
            whole((s.spans, 8, LANES)), whole((s.rows, 4 * LANES)), whole((s.rows, LANES)),
            whole((s.rows, 8)), columns(8),
        ],
        out_specs=[
            columns(s.rows), columns(s.rows), columns(s.rows), stacks(s.spans, LANES),
            stacks(s.spans, 8), columns(8),
        ],
        out_shape=[
            shaped((s.rows, s.inner), BF16), shaped((s.rows, s.inner), BF16),
            shaped((s.rows, s.inner), F32), shaped((s.spans, LANES, s.inner), F32),
            shaped((s.spans, 8, s.inner), F32), shaped((8, s.inner), F32),
        ],
        scratch_shapes=[scratch(s.rows, LANES)] * 3 + [scratch(s.spans, LANES, 2 * ROWS, dtype=BF16)],
        compiler_params=params(),
        cost_estimate=s.cost(),
        name="gate_back",
    )(scan, x, z, dgo, sums, bc, run, cols, gains)


def backward_within(s, x, dy, bc, step, run, run_t, cols, seg_rows):
    return pl.pallas_call(
        backward_within_kernel,
        grid=(s.pairs,),
        in_specs=[
            columns(s.rows), columns(s.rows), whole((s.rows, 4 * LANES)), whole((s.rows, LANES)),
            whole((s.rows, LANES)), whole((s.spans, s.width, LANES)), whole((s.rows, 8)),
            whole((s.spans, 8, LANES)),
        ],
        out_specs=[columns(s.rows), whole((s.rows, 2 * LANES))],
        out_shape=[shaped((s.rows, s.inner), F32), shaped((s.rows, 2 * LANES), F32)],
        scratch_shapes=[scratch(s.spans, ROWS, ROWS)] * 3,
        compiler_params=params(),
        cost_estimate=s.cost(),
        name="backward_within",
    )(x, dy, bc, step, run, run_t, cols, seg_rows)


def backward_finish(
    s, both, rim, x, dy, scan, dxw, dbc, state, decay, incoming, grad, back, outgoing,
    bc, step, run, cols, conv_v, conv_ss, heads, gains,
):
    return pl.pallas_call(
        backward_finish_kernel,
        grid=(s.pairs,),
        in_specs=[
            value_columns(s.rows), whole((s.rows, 3 * LANES)), value_columns(RIM), whole((RIM, 3 * LANES)),
            columns(s.rows), columns(s.rows), columns(s.rows), columns(s.rows), whole((s.rows, 2 * LANES)),
            stacks(s.spans, LANES), stacks(s.spans, 8), columns(LANES),
            stacks(s.spans, LANES), stacks(s.spans, 8), columns(LANES),
            whole((s.rows, 4 * LANES)), whole((s.rows, LANES)), whole((s.rows, LANES)), whole((s.rows, 8)),
            columns(8), whole((8, 2 * LANES)), whole((8, LANES)), columns(8),
        ],
        out_specs=[
            columns(s.rows), columns(RIM), columns(RIM), columns(8),
            whole((s.rows, 3 * LANES)), whole((RIM, 2 * LANES)), whole((RIM, 2 * LANES)),
            whole((8, 2 * LANES)), whole((8, LANES)),
        ],
        out_shape=[
            shaped((s.rows, s.inner), BF16), shaped((RIM, s.inner), F32), shaped((RIM, s.inner), F32),
            shaped((8, s.inner), F32), shaped((s.rows, 3 * LANES), BF16), shaped((RIM, 2 * LANES), F32),
            shaped((RIM, 2 * LANES), F32), shaped((8, 2 * LANES), F32), shaped((8, LANES), F32),
        ],
        scratch_shapes=[
            scratch(s.rows + RIM, LANES), scratch(s.rows + RIM, LANES), scratch(3, s.rows + RIM, LANES),
            scratch(s.rows, LANES), scratch(s.rows, LANES), scratch(s.rows, LANES), scratch(s.rows, LANES),
            scratch(s.rows, 2 * LANES),
        ],
        compiler_params=params(),
        cost_estimate=s.cost(),
        name="backward_finish",
    )(
        both, both, rim, rim, x, dy, scan, dxw, dbc, state, decay, incoming, grad, back, outgoing,
        bc, step, run, cols, conv_v, conv_ss, heads, gains,
    )


WIDE = 256


def tile_product(kernel, slots, operands, specs, outs, out_specs, blocks, flops):
    rows = operands[0].shape[0]
    scatter = (rows // slots.shape[0]) % 16 == 0

    def body(*refs):
        kernel(scatter, *refs)

    results = pl.pallas_call(
        body,
        grid_spec=pltpu.PrefetchScalarGridSpec(
            num_scalar_prefetch=1, grid=(blocks,), in_specs=specs, out_specs=out_specs
        ),
        out_shape=outs,
        compiler_params=params(),
        cost_estimate=pl.CostEstimate(flops=1, bytes_accessed=1, transcendentals=0),
        name=kernel.__name__,
    )(slots, *operands)
    return results, scatter


def fixed(shape):
    return pl.BlockSpec(shape, lambda j, slots: (0,) * len(shape))


def branch_rows(slots, back_index, gated_low, out_proj):
    rows, inner = gated_low.shape
    width = out_proj.shape[1]
    [out], scatter = tile_product(
        branch_kernel,
        slots,
        (gated_low, out_proj),
        [fixed((rows, inner)), pl.BlockSpec((inner, WIDE), lambda j, slots: (0, j))],
        [shaped((rows, width), BF16)],
        [pl.BlockSpec((rows, WIDE), lambda j, slots: (0, j))],
        width // WIDE,
        2 * rows * inner * width,
    )
    return out if scatter else move_tiles(out, back_index)


def normed_grad(slots, back_index, lows, weights, normed):
    rows, width = normed.shape
    (out, diag), scatter = tile_product(
        normed_grad_kernel,
        slots,
        (*lows, *weights, normed),
        [fixed(low.shape) for low in lows]
        + [pl.BlockSpec((WIDE, w.shape[1]), lambda j, slots: (j, 0)) for w in weights]
        + [pl.BlockSpec((rows, WIDE), lambda j, slots: (0, j))],
        [shaped((rows, width), BF16), shaped((8, width), F32)],
        [pl.BlockSpec((rows, WIDE), lambda j, slots: (0, j)), pl.BlockSpec((8, WIDE), lambda j, slots: (0, j))],
        width // WIDE,
        2 * rows * width * sum(low.shape[1] for low in lows),
    )
    return (out if scatter else move_tiles(out, back_index)), diag[0]


def swapped(value, axis, bit):
    count = lax.axis_size(axis)
    return lax.ppermute(value, axis, [(k, k ^ (1 << bit)) for k in range(count)])


def axis_bits(axis):
    return lax.axis_size(axis).bit_length() - 1


class RowsOverSeq:
    def __init__(self, grads, seq_index, backwards):
        bits, count = axis_bits("seq"), lax.axis_size("seq")
        self.here = seq_index
        self.total = grads.reshape((2,) * bits + (grads.shape[0] // count, grads.shape[1]))
        self.left = list(range(bits))[::-1]
        self.order = [0] + (list(range(1, bits))[::-1] if backwards else list(range(1, bits)))

    def swap(self):
        bit = self.order.pop(0)
        at, own = self.left.index(bit), (self.here >> bit) & 1
        self.left.pop(at)
        self.keep = lax.dynamic_index_in_dim(self.total, own, at, keepdims=False)
        self.send = lax.dynamic_index_in_dim(self.total, 1 - own, at, keepdims=False)
        return swapped(self.send, "seq", bit)

    def join(self, got):
        total = self.keep.astype(F32) + got.astype(F32)
        self.total = total.astype(self.total.dtype) if self.order else total


class SumByPairs:
    def __init__(self, value, axis):
        self.size, self.axis = value.shape[0], axis
        padded = jnp.pad(value, (0, -self.size % (8 * LANES)))
        self.total, self.order = padded.reshape(-1, LANES), list(range(axis_bits(axis)))

    def swap(self):
        self.keep = self.send = self.total
        return swapped(self.send, self.axis, self.order.pop(0))

    def join(self, got):
        self.total = self.keep + got
        if not self.order:
            self.total = self.total.reshape(-1)[: self.size]


class SumByHalves:
    def __init__(self, value, axis):
        self.total, self.axis, self.here = value, axis, lax.axis_index(axis)
        bits = list(range(axis_bits(axis)))
        self.order = [(bit, True) for bit in bits[::-1]] + [(bit, False) for bit in bits]

    def swap(self):
        bit, self.adds = self.order.pop(0)
        self.own = (self.here >> bit) & 1
        if self.adds:
            half = self.total.shape[0] // 2
            self.keep = lax.dynamic_slice_in_dim(self.total, self.own * half, half, 0)
            self.send = lax.dynamic_slice_in_dim(self.total, (1 - self.own) * half, half, 0)
        else:
            self.keep = self.send = self.total.astype(BF16)
        return swapped(self.send, self.axis, bit)

    def join(self, got):
        if self.adds:
            self.total = self.keep.astype(F32) + got.astype(F32)
            return
        mine, upper = self.keep, self.own == 1
        self.total = jnp.concatenate(
            [jnp.where(upper, got, mine), jnp.where(upper, mine, got)], axis=0
        )


class Chain:
    def __init__(self, part, *makers):
        self.part, self.makers, self.totals = part, list(makers), []

    @property
    def order(self):
        while not self.part.order and self.makers:
            self.totals.append(self.part.total)
            self.part = self.makers.pop(0)(self.part.total)
        return self.part.order

    @property
    def total(self):
        return self.part.total

    def swap(self):
        return self.part.swap()

    def join(self, got):
        self.part.join(got)


def swap_all(parts):
    return [(part, part.swap()) for part in parts if part.order]


def join_all(parts, got, *tokens):
    if not got:
        return
    arrived = lax.optimization_barrier((tuple(piece for _, piece in got), *tokens))[0]
    for (part, _), piece in zip(got, arrived):
        part.join(piece)


def finish_all(parts):
    while any(part.order for part in parts):
        join_all(parts, swap_all(parts))


def carried_states(states, decay, reverse, *covers, results=None):
    count = lax.axis_size("seq")
    sign = -1 if reverse else 1
    both = jnp.concatenate([states, decay], axis=0)
    results = [] if results is None else results

    def cover(reach, got):
        if len(results) == len(covers):
            return got
        result, token = covers[len(results)](reach)
        results.append(result)
        return after(got, token)

    def joined(near, far):
        through = near[LANES : LANES + 1]
        return jnp.concatenate([near[:LANES], jnp.zeros_like(near[LANES:])], axis=0) + through * far

    near, far = (from_behind(both, "seq", sign * k) for k in (1, 2))
    near, far = cover(both, (near, far))
    reach, width = joined(near, far), 2
    while width < count - 1:
        reach = joined(reach, cover(reach, from_behind(reach, "seq", sign * width)))
        width *= 2
    while len(results) < len(covers):
        cover(reach, reach)
    return reach[:LANES], results


def after(value, *tokens):
    return lax.optimization_barrier((value, *tokens))[0]


def from_behind(value, axis, steps):
    count = lax.axis_size(axis)
    initial, last = (max(0, -steps), min(count, count - steps))
    return lax.ppermute(value, axis, [(source, source + steps) for source in range(initial, last)])


def move_tiles(rows, index):
    tile_total = index.shape[0]
    shaped_rows = rows.reshape((tile_total, rows.shape[0] // tile_total) + rows.shape[1:])
    return jnp.take(shaped_rows, index, axis=0, mode="clip").reshape(rows.shape)


def carry_weights(decays, here, reverse):
    count = decays.shape[0]
    ids = jnp.arange(count, dtype=jnp.int32)
    if reverse:
        between = (ids[None, :] < ids[:, None]) & (ids[None, :] > here)
        reached = ids > here
    else:
        between = (ids[None, :] > ids[:, None]) & (ids[None, :] < here)
        reached = ids < here
    chain = jnp.prod(jnp.where(between[:, :, None], decays[None, :, :], 1.0), axis=1)
    return jnp.where(reached[:, None], chain, 0.0)


def padded_rows(parts, rows=8):
    stacked = jnp.concatenate([part.reshape(-1, part.shape[-1]) for part in parts], axis=0)
    return jnp.pad(stacked, ((0, rows - stacked.shape[0]), (0, 0)))


def local(
    tokens,
    packing,
    segment_ids,
    norm_gain,
    gate_proj,
    value_proj,
    shared_proj,
    step_proj,
    conv_value,
    conv_value_bias,
    conv_shared,
    conv_shared_bias,
    step_bias,
    log_decay,
    skip_gain,
    gated_gain,
    out_proj,
    cotangent,
):
    own_rows = tokens.shape[0]
    head_shards = lax.axis_size("head")
    seq_shards = lax.axis_size("seq")
    head_index = lax.axis_index("head")
    seq_index = lax.axis_index("seq")
    shard_rows = own_rows * head_shards
    inner_local = gate_proj.shape[1]
    heads_local = step_proj.shape[1]
    inner_width = inner_local * head_shards
    tile_rows = own_rows // seq_shards
    tile_count = shard_rows // tile_rows
    s = Sizes(shard_rows, inner_local, heads_local)

    packed_tiles = packing.reshape(-1, tile_rows)[:, 0] // tile_rows
    own_device = seq_index * head_shards + head_index
    seq_ids = jnp.arange(seq_shards, dtype=jnp.int32)
    own_tiles = own_device * seq_shards + seq_ids
    tile_match = (own_tiles[:, None] == packed_tiles[None, :]).astype(jnp.int32)
    tile_shard = jnp.arange(packed_tiles.shape[0], dtype=jnp.int32) // tile_count
    dest_shard = jnp.sum(tile_match * tile_shard[None, :], axis=1)
    send_index = jnp.sum(
        (dest_shard[None, :] == seq_ids[:, None]).astype(jnp.int32) * seq_ids[None, :], axis=1
    )
    own_packed = lax.dynamic_slice_in_dim(packed_tiles, seq_index * tile_count, tile_count, 0)
    source_device = own_packed // seq_shards
    arrival = source_device % head_shards * seq_shards + source_device // head_shards
    slot_ids = jnp.arange(tile_count, dtype=jnp.int32)
    back_index = jnp.sum(
        (arrival[None, :] == slot_ids[:, None]).astype(jnp.int32) * slot_ids[None, :], axis=1
    )

    shard_start = seq_index * shard_rows
    around = jnp.concatenate([jnp.full((RIM,), -1, jnp.int32), segment_ids])
    around = lax.dynamic_slice_in_dim(around, shard_start, shard_rows + RIM, 0)
    seg = around[RIM:]
    span_last = around[RIM - 1 :: ROWS]
    before_span = jnp.repeat(span_last[:-1], ROWS)
    end_of_span = jnp.repeat(span_last[1:], ROWS)
    facts = [around[RIM - k : RIM - k + shard_rows] == seg for k in (1, 2, 3)]
    facts += [before_span == seg, end_of_span == seg, seg, seg, seg]
    cols = jnp.stack([fact.astype(F32) for fact in facts], axis=1)
    seg_rows = jnp.broadcast_to(seg.astype(F32).reshape(s.spans, 1, ROWS), (s.spans, 8, ROWS))

    head_pad = ((0, 0), (0, LANES - heads_local))
    heads = padded_rows([step_bias, jnp.exp(log_decay)])
    heads = jnp.pad(heads, head_pad)
    conv_v = padded_rows([conv_value, conv_value_bias])
    conv_ss = padded_rows([conv_shared, conv_shared_bias])
    gains = padded_rows([jnp.repeat(skip_gain, inner_local // heads_local), gated_gain])
    ss_proj = jnp.concatenate([shared_proj, jnp.pad(step_proj, head_pad)], axis=1)

    tok_float = tokens.astype(F32)
    tok_rstd = lax.rsqrt(jnp.mean(tok_float * tok_float, axis=1, keepdims=True) + EPS)
    normed = (tok_float * tok_rstd * norm_gain[None, :]).astype(BF16)

    def to_shard(rows):
        sent = lax.all_to_all(
            move_tiles(rows, send_index), "seq", split_axis=0, concat_axis=0, tiled=True
        )
        return lax.all_gather(sent, "head", axis=0, tiled=True)

    packed_normed = move_tiles(to_shard(normed), arrival)
    arrived_cot = to_shard(cotangent)

    both = dot(packed_normed, jnp.concatenate([ss_proj, value_proj], axis=1))
    rim = from_behind(both[shard_rows - RIM :], "seq", 1)
    x, bc, step, run, run_t, state, decay = forward_states(
        s, both, rim, cols, conv_v, conv_ss, heads
    )

    def project_gate(reach):
        z = dot(after(packed_normed, reach), gate_proj)
        return z, z

    def within(reach):
        y = forward_within(s, after(x, reach), bc, step, run, run_t, cols, seg_rows)
        return y, y

    def cot_products(reach):
        cot = move_tiles(arrived_cot, after(arrival, reach))
        dgo = dot(cot, out_proj, CONTRACT_COLS)
        return (cot, dgo), dgo

    incoming, (y, gate_z, (packed_cot, dgo)) = carried_states(
        state[s.spans - 1], decay[s.spans - 1], False, within, project_gate, cot_products
    )
    scan, sums = forward_finish(
        s, y, x, gate_z, dgo, state, decay, incoming, bc, run, cols, gains
    )
    sums = lax.psum(jnp.stack([sums[:, 0, :], sums[:, 8, :]], axis=1), "head")
    sums = jnp.pad(sums, ((0, 0), (0, 6), (0, 0)))
    gated_low, low_gate, dy, grad, back, gate_rows = gate_back(
        s, inner_width, scan, x, gate_z, dgo, sums, bc, run, cols, gains
    )

    starts = lax.all_gather(jnp.concatenate([grad[0], decay[s.spans - 1]], axis=0), "seq")
    branch = branch_rows(arrival, back_index, gated_low, out_proj)
    dxw, dbc = backward_within(s, x, after(dy, branch), bc, step, run, run_t, cols, seg_rows)
    out_grads = dot(after(gated_low, dbc), packed_cot, CONTRACT_ROWS).astype(BF16)
    gate_grads = dot(after(packed_normed, out_grads), low_gate, CONTRACT_ROWS).astype(BF16)
    branch = lax.psum_scatter(
        after(branch, gate_grads), "head", scatter_dimension=0, tiled=True
    )
    out_sum = RowsOverSeq(out_grads, seq_index, True)
    gate_sum = RowsOverSeq(gate_grads, seq_index, False)
    early = [out_sum, gate_sum]
    got = swap_all(early)
    decays = starts[:, LANES, :]
    outgoing = jnp.sum(
        carry_weights(decays, seq_index, True)[:, None, :] * starts[:, :LANES, :], axis=0
    )
    dy = after(dy, gate_grads, *[part.keep for part in early], *[part.send for part in early])
    low_value, tail, rim_out, taps_v, low_ss, tail_ss, rim_ss_out, taps_ss, small = backward_finish(
        s, both, rim, x, dy, scan, dxw, dbc, state, decay, incoming, grad, back,
        outgoing, bc, step, run, cols, conv_v, conv_ss, heads, gains,
    )
    join_all(early, got, small)
    got = swap_all(early)
    rim_out = after(rim_out, *[part.send for part in early])
    rim_back = from_behind(jnp.concatenate([rim_out, rim_ss_out], axis=1), "seq", -1)
    tail = (jnp.concatenate([tail, tail_ss], axis=1) + rim_back).astype(BF16)
    low_value = lax.dynamic_update_slice(low_value, tail[:, :inner_local], (shard_rows - RIM, 0))
    low_ss = lax.dynamic_update_slice(low_ss, tail[:, inner_local:], (shard_rows - RIM, 0))

    ss_grads = dot(packed_normed, low_ss, CONTRACT_ROWS)
    shared_sum = Chain(
        RowsOverSeq(ss_grads[:, : 2 * LANES], seq_index, False), lambda total: SumByHalves(total, "head")
    )
    step_rows = RowsOverSeq(ss_grads[:, 2 * LANES :].astype(BF16), seq_index, False)
    got += swap_all([shared_sum, step_rows])
    low_gate = after(low_gate, ss_grads)
    d_normed, grad_norm_rows = normed_grad(
        arrival,
        back_index,
        (low_gate, low_value, low_ss),
        (gate_proj, value_proj, ss_proj),
        packed_normed,
    )
    gate_rows, small, taps_v, taps_ss = after((gate_rows, small, taps_v, taps_ss), d_normed)
    arrived, low_value = lax.optimization_barrier(
        (tuple(piece for _, piece in got), after(low_value, d_normed))
    )
    d_normed = lax.psum_scatter(
        after(d_normed, branch), "head", scatter_dimension=0, tiled=True
    )
    for (part, _), piece in zip(got, arrived):
        part.join(piece)
    value_grads = dot(packed_normed, low_value, CONTRACT_ROWS).astype(BF16)

    per_head = [jnp.sum(gate_rows[1].reshape(heads_local, -1), axis=1)]
    per_head += [small[0, :heads_local], small[1, :heads_local]]
    pieces = [taps_v[:5].reshape(-1), gate_rows[0]] + per_head
    own_size = sum(piece.shape[0] for piece in pieces)
    shared_pieces = [taps_ss[:5].reshape(-1), grad_norm_rows]
    flat_sum = Chain(
        SumByPairs(jnp.concatenate(pieces + shared_pieces), "seq"),
        lambda total: SumByPairs(total[own_size:], "head"),
    )
    half = inner_local // 2
    short = [shared_sum, flat_sum, step_rows]
    got = swap_all(short)
    arrived, value_grads = lax.optimization_barrier((tuple(piece for _, piece in got), value_grads))
    for (part, _), piece in zip(got, arrived):
        part.join(piece)
    values = [
        RowsOverSeq(value_grads[:, :half], seq_index, False),
        RowsOverSeq(value_grads[:, half:], seq_index, True),
    ]
    beside = [values, [], values, [], values]
    while any(part.order for part in short):
        got = swap_all(short + (beside.pop(0) if beside else []))
        if len(beside) == 1:
            arrived, branch_back = lax.optimization_barrier(
                (tuple(piece for _, piece in got), branch_back)
            )
            got = [(part, piece) for (part, _), piece in zip(got, arrived)]
        join_all(None, got)
        if len(beside) == 3:
            branch = after(branch, shared_sum.total)
            branch_back = lax.all_to_all(branch, "seq", split_axis=0, concat_axis=0, tiled=True)
    last = swap_all(early)
    normed_back = lax.all_to_all(d_normed, "seq", split_axis=0, concat_axis=0, tiled=True)
    arrived, normed_back = lax.optimization_barrier(
        (tuple(piece for _, piece in last), normed_back)
    )
    for (part, _), piece in zip(last, arrived):
        part.join(piece)
    finish_all(values + early)
    everything, grad_shared, shared_sums = flat_sum.totals[0], shared_sum.total, flat_sum.total
    grad_out_proj, grad_gate = out_sum.total, gate_sum.total
    grad_value = jnp.concatenate([part.total for part in values], axis=1)
    grad_step_proj = step_rows.total[:, :heads_local]
    grad_shared = lax.all_gather(grad_shared, "seq", axis=0, tiled=True).astype(F32)

    branch_given = move_tiles(branch_back, dest_shard).astype(F32)
    d_normed_given = move_tiles(normed_back, dest_shard).astype(F32)
    mixed_rows = (tok_float + branch_given).astype(BF16)
    scaled = d_normed_given * norm_gain[None, :]
    row_dot = jnp.sum(scaled * tok_float, axis=1, keepdims=True) / tokens.shape[1]
    d_tok = tok_rstd * scaled - tok_float * (tok_rstd * tok_rstd * tok_rstd * row_dot)
    grad_tokens = (cotangent.astype(F32) + d_tok).astype(BF16)

    own_taps = everything[: 5 * inner_local].reshape(5, inner_local)
    rest = everything[5 * inner_local : own_size]
    grad_gated = rest[:inner_local]
    rest = rest[inner_local:]
    grad_skip = rest[:heads_local]
    grad_step_bias = rest[heads_local : 2 * heads_local]
    grad_log_decay = rest[2 * heads_local :]
    shared_taps = shared_sums[: 10 * LANES].reshape(5, 2 * LANES)
    grad_norm_gain = shared_sums[10 * LANES : 10 * LANES + norm_gain.shape[0]] / norm_gain
    return (
        mixed_rows,
        grad_tokens,
        grad_norm_gain,
        grad_gate,
        grad_value,
        grad_shared,
        grad_step_proj,
        own_taps[:4],
        own_taps[4],
        shared_taps[:4],
        shared_taps[4],
        grad_step_bias,
        grad_log_decay,
        grad_skip,
        grad_gated,
        grad_out_proj,
    )


def solution(mesh):
    placed = (
        P(("seq", "head"), None),
        P(),
        P(),
        P(),
        P(None, "head"),
        P(None, "head"),
        P(),
        P(None, "head"),
        P(None, "head"),
        P("head"),
        P(),
        P(),
        P("head"),
        P("head"),
        P("head"),
        P("head"),
        P("head", None),
        P(("seq", "head"), None),
    )
    return jax.shard_map(
        local,
        mesh=mesh,
        in_specs=placed,
        out_specs=(
            P(("seq", "head"), None),
            P(("seq", "head"), None),
            P(),
            P("seq", "head"),
            P("seq", "head"),
            P(),
            P("seq", "head"),
            P(None, "head"),
            P("head"),
            P(),
            P(),
            P("head"),
            P("head"),
            P("head"),
            P("head"),
            P(("head", "seq"), None),
        ),
        check_vma=False,
    )
```

```python
import jax
import jax.numpy as jnp
from jax import lax
from jax.experimental import pallas as pl
from jax.experimental.pallas import tpu as pltpu
from jax.sharding import PartitionSpec as P

EPS = 1e-05
ROWS = 128
LANES = 128
HALF = 64
RIM = 8
FAR = -1e30
UNROLL = 8
F32 = jnp.float32
BF16 = jnp.bfloat16
VMEM_BYTES = 56 * 1024 * 1024
CONTRACT_ROWS = (((0,), (0,)), ((), ()))
CONTRACT_COLS = (((1,), (1,)), ((), ()))


def dot(a, b, dims=(((1,), (0,)), ((), ()))):
    return lax.dot_general(a, b, dims, preferred_element_type=F32)


def two_parts(x):
    upper = x.astype(BF16)
    return upper, (x - upper.astype(F32)).astype(BF16)


def three_parts(x):
    upper, rest = x.astype(BF16), x
    rest = x - upper.astype(F32)
    middle = rest.astype(BF16)
    return upper, middle, (rest - middle.astype(F32)).astype(BF16)


def in_two(x):
    return jnp.concatenate(two_parts(x), axis=1)


def twice(x):
    return jnp.concatenate([x, x], axis=0)


def b_parts(bc_ref, at):
    return bc_ref[at, : 2 * LANES]


def c_parts(bc_ref, at):
    return bc_ref[at, 2 * LANES :]


def cross_product(bc_ref, at):
    b, c = b_parts(bc_ref, at), c_parts(bc_ref, at)
    upper = jnp.concatenate([b[:, :LANES], b[:, :LANES]], axis=1)
    return dot(c, upper, CONTRACT_COLS) + dot(c[:, :LANES], b[:, LANES:], CONTRACT_COLS)


def lane_ids(rows):
    return lax.broadcasted_iota(jnp.int32, (rows, LANES), 1)


def row_ids(rows):
    return lax.broadcasted_iota(jnp.int32, (rows, LANES), 0)


def from_head(block, head):
    index = head + jnp.zeros(block.shape, jnp.int32)
    return jnp.take_along_axis(block, index, axis=1)


def head_cols(block, pair):
    return from_head(block, 2 * pair), from_head(block, 2 * pair + 1)


def head_pair(block, pair):
    return from_head(block, 2 * pair + jnp.where(lane_ids(block.shape[0]) < HALF, 0, 1))


def head_selector(pair):
    lane = row_ids(LANES)
    head = 2 * pair + jnp.where(lane < HALF, 0, 1)
    return (lane_ids(LANES) == head).astype(F32).astype(BF16)


def split_sum(x, selector):
    upper, lower = two_parts(x)
    stacked = jnp.concatenate([upper, lower], axis=1)
    return dot(stacked, jnp.concatenate([selector, selector], axis=0))


def lower_ones():
    return (row_ids(ROWS) >= lane_ids(ROWS)).astype(F32).astype(BF16)


def upper_ones():
    return (row_ids(ROWS) <= lane_ids(ROWS)).astype(F32).astype(BF16)


def spread(ref, row, col):
    return jnp.broadcast_to(ref[pl.ds(row, ROWS), col : col + 1], (ROWS, LANES))


def softplus(x):
    return jnp.maximum(x, 0.0) + jnp.log1p(jnp.exp(-jnp.abs(x)))


def sigmoid(x):
    return 1.0 / (1.0 + jnp.exp(-x))


def span_start(q):
    return pl.multiple_of(q * ROWS, ROWS)


def loop(count, body):
    def step(q, carry):
        body(q)
        return carry

    lax.fori_loop(0, count, step, 0, unroll=UNROLL)


def conv_span(pad_ref, same_ref, row, taps, bias):
    long = pad_ref[pl.ds(row, ROWS + RIM), :]
    total = bias + taps[3:4] * long[RIM:]
    shifted = []
    for back in (1, 2, 3):
        moved = pad_ref[pl.ds(row + RIM - back, ROWS), :]
        moved = moved * same_ref[back - 1, pl.ds(row, ROWS), :]
        shifted.append(moved)
        total = total + taps[3 - back : 4 - back] * moved
    return total, [long[RIM:]] + shifted


def forward_states_kernel(
    value_ref, ss_ref, rim_v_ref, rim_ss_ref, cols_ref, conv_ref, conv_ss_ref, heads_ref,
    x_ref, bc_ref, step_ref, run_ref, run_t_ref, state_ref, decay_ref,
    pad, same, cont, last, bt,
):
    pair = pl.program_id(0)
    rows = value_ref.shape[0]
    spans = rows // ROWS
    width = run_t_ref.shape[1]

    @pl.when(pair == 0)
    def _():
        def masks(q):
            row = span_start(q)
            for k in range(3):
                same[k, pl.ds(row, ROWS), :] = spread(cols_ref, row, k)
            cont[pl.ds(row, ROWS), :] = spread(cols_ref, row, 3)
            last[pl.ds(row, ROWS), :] = spread(cols_ref, row, 4)

        loop(spans, masks)
        for part in range(2):
            lanes = slice(part * LANES, (part + 1) * LANES)
            pad[0:RIM, :] = rim_ss_ref[:, lanes]
            pad[RIM:, :] = ss_ref[:, lanes]
            taps, bias = conv_ss_ref[0:4, lanes], conv_ss_ref[4:5, lanes]

            def shared(q):
                row = span_start(q)
                pre, _ = conv_span(pad, same, row, taps, bias)
                act = pre * sigmoid(pre)
                bc_ref[pl.ds(row, ROWS), 2 * part * LANES : 2 * (part + 1) * LANES] = in_two(act)
                if part == 0:
                    bt[q] = in_two(jnp.transpose(act))

            loop(spans, shared)

        bias, rate = heads_ref[0:1, :], heads_ref[1:2, :]
        tri, tri_t = lower_ones(), upper_ones()

        def steps(q):
            row = span_start(q)
            size = softplus(ss_ref[pl.ds(row, ROWS), 2 * LANES :] + bias)
            step_ref[pl.ds(row, ROWS), :] = size
            parts = three_parts(-size * rate)
            run_ref[pl.ds(row, ROWS), :] = sum(dot(tri, part) for part in parts)
            turned = sum(dot(part, tri_t, CONTRACT_ROWS) for part in parts)
            run_t_ref[q] = turned[:width]

        loop(spans, steps)

    pad[0:RIM, :] = rim_v_ref[...]
    pad[RIM:, :] = value_ref[...]
    taps, bias = conv_ref[0:4], conv_ref[4:5]

    def span(q, carry):
        state, decay = carry
        row = span_start(q)
        at = pl.ds(row, ROWS)
        pre, _ = conv_span(pad, same, row, taps, bias)
        x = pre * sigmoid(pre)
        x_ref[at, :] = x
        size = head_pair(step_ref[at, :], pair)
        run = head_pair(run_ref[at, :], pair)
        enter = jnp.exp(run[ROWS - 1 :]) * cont[pl.ds(row + ROWS - 8, 8), :][7:8]
        to_end = jnp.exp(run[ROWS - 1 :] - run) * last[at, :]
        state = state * enter + dot(bt[q], twice((x * size * to_end).astype(BF16)))
        decay = decay * enter
        state_ref[q] = state
        decay_ref[q] = jnp.broadcast_to(decay, (8, LANES))
        return state, decay

    lax.fori_loop(
        0, spans, span, (jnp.zeros((LANES, LANES), F32), jnp.ones((1, LANES), F32)),
        unroll=UNROLL,
    )


def span_masks(cols_ref, seg_rows_ref, bias_ref, spans):
    causal = row_ids(ROWS) >= lane_ids(ROWS)

    def mask(q):
        own = spread(cols_ref, span_start(q), 5)
        other = jnp.broadcast_to(seg_rows_ref[q, 0:1, :], (ROWS, ROWS))
        bias_ref[q] = jnp.where(causal & (own == other), 0.0, FAR)

    loop(spans, mask)


def decay_pair(run_ref, run_t_ref, mask_ref, q, pair):
    first, second = head_cols(run_ref[pl.ds(span_start(q), ROWS), :], pair)
    rows = run_t_ref[q, pl.ds(2 * pair, 2), :]
    mask = mask_ref[q]
    return jnp.exp(first - rows[0:1] + mask), jnp.exp(second - rows[1:2] + mask)


def heads_apart(x):
    lane = lane_ids(x.shape[0])
    zero = jnp.zeros_like(x)
    return jnp.concatenate([jnp.where(lane < HALF, x, zero), jnp.where(lane < HALF, zero, x)], axis=0)


def forward_within_kernel(
    x_ref, bc_ref, step_ref, run_ref, run_t_ref, cols_ref, seg_rows_ref, y_ref, mask, cross
):
    pair = pl.program_id(0)
    spans = x_ref.shape[0] // ROWS

    @pl.when(pair == 0)
    def _():
        span_masks(cols_ref, seg_rows_ref, mask, spans)

        def products(q):
            at = pl.ds(span_start(q), ROWS)
            cross[q] = cross_product(bc_ref, at)

        loop(spans, products)

    def span(q):
        at = pl.ds(span_start(q), ROWS)
        size = head_pair(step_ref[at, :], pair)
        weighted = x_ref[at, :] * size
        first, second = decay_pair(run_ref, run_t_ref, mask, q, pair)
        mix = jnp.concatenate([first * cross[q], second * cross[q]], axis=1).astype(BF16)
        y_ref[at, :] = dot(mix, heads_apart(weighted).astype(BF16))

    loop(spans, span)


def entering(state_ref, decay_ref, incoming, q, before):
    at = jnp.maximum(before, 0)
    local = state_ref[at] + decay_ref[at, 0:1, :] * incoming
    return jnp.where(before >= 0, local, incoming)


def row_sums(acc_ref, out_ref, base, spans):
    ones = jnp.ones((8, LANES), BF16)

    def total(q):
        parts = three_parts(acc_ref[pl.ds(span_start(q), ROWS), :])
        out_ref[q, base : base + 8, :] = sum(dot(ones, part, CONTRACT_COLS) for part in parts)

    loop(spans, total)


def forward_finish_kernel(
    y_ref, x_ref, z_ref, dgo_ref, state_ref, decay_ref, in_ref, bc_ref, run_ref, cols_ref, gains_ref,
    scan_ref, sums_ref, cont, squares, inner,
):
    pair = pl.program_id(0)
    spans = y_ref.shape[0] // ROWS

    @pl.when(pair == 0)
    def _():
        def masks(q):
            row = span_start(q)
            cont[pl.ds(row, ROWS), :] = spread(cols_ref, row, 3)

        loop(spans, masks)
        squares[...] = jnp.zeros_like(squares)
        inner[...] = jnp.zeros_like(inner)

    incoming = in_ref[...]
    skip, gain = gains_ref[0:1], gains_ref[1:2]

    def span(q):
        at = pl.ds(span_start(q), ROWS)
        run = head_pair(run_ref[at, :], pair)
        state = entering(state_ref, decay_ref, incoming, q, q - 1)
        upper, lower = two_parts(state)
        c = c_parts(bc_ref, at)
        carried = dot(c, twice(upper)) + dot(c[:, :LANES], lower)
        scan = y_ref[at, :] + carried * (jnp.exp(run) * cont[at, :])
        scan_ref[at, :] = scan
        z = z_ref[at, :]
        gated = (scan + skip * x_ref[at, :]) * (z * sigmoid(z))
        squares[at, :] += gated * gated
        inner[at, :] += gain * dgo_ref[at, :] * gated

    loop(spans, span)

    @pl.when(pair == pl.num_programs(0) - 1)
    def _():
        row_sums(squares, sums_ref, 0, spans)
        row_sums(inner, sums_ref, 8, spans)


def gate_back_kernel(
    inner_width,
    scan_ref, x_ref, z_ref, dgo_ref, sums_ref, bc_ref, run_ref, cols_ref, gains_ref,
    out_ref, dz_ref, dy_ref, grad_ref, decay_ref, rows_ref,
    cont, rstd, coef, ct,
):
    pair = pl.program_id(0)
    spans = scan_ref.shape[0] // ROWS

    @pl.when(pair == 0)
    def _():
        def masks(q):
            row = span_start(q)
            at = pl.ds(row, ROWS)
            cont[at, :] = spread(cols_ref, row, 3)
            ct[q] = jnp.concatenate(
                [
                    jnp.transpose(bc_ref[at, k * LANES : (k + 1) * LANES].astype(F32)).astype(BF16)
                    for k in (2, 3)
                ],
                axis=1,
            )
            square = jnp.broadcast_to(sums_ref[q, 0:1, :], (ROWS, LANES))
            cross = jnp.broadcast_to(sums_ref[q, 1:2, :], (ROWS, LANES))
            root = lax.rsqrt(square / inner_width + EPS)
            rstd[at, :] = jnp.transpose(root)
            coef[at, :] = jnp.transpose(root * root * root * cross / inner_width)

        loop(spans, masks)

    skip, gain = gains_ref[0:1], gains_ref[1:2]
    rows_ref[...] = jnp.zeros_like(rows_ref)

    def span(k, carry):
        leaving, decay = carry
        q = spans - 1 - k
        at = pl.ds(span_start(q), ROWS)
        x, z, dgo = x_ref[at, :], z_ref[at, :], dgo_ref[at, :]
        scanned = scan_ref[at, :] + skip * x
        gate = sigmoid(z)
        silu = z * gate
        gated = scanned * silu
        normed = gated * rstd[at, :]
        out_ref[at, :] = (normed * gain).astype(BF16)
        d_gated = rstd[at, :] * (dgo * gain) - gated * coef[at, :]
        d_scan = d_gated * silu
        dz_ref[at, :] = (d_gated * scanned * (gate * (1.0 + z * (1.0 - gate)))).astype(BF16)
        dy_ref[at, :] = d_scan
        rows_ref[0:1] += jnp.sum(dgo * normed, axis=0, keepdims=True)
        rows_ref[1:2] += jnp.sum(d_scan * x, axis=0, keepdims=True)
        run = head_pair(run_ref[at, :], pair)
        enter = jnp.exp(run) * cont[at, :]
        upper, lower = two_parts(d_scan * enter)
        turned = ct[q]
        leaving = leaving * enter[ROWS - 1 :] + dot(turned, twice(upper)) + dot(turned[:, :ROWS], lower)
        decay = decay * enter[ROWS - 1 :]
        grad_ref[q] = leaving
        decay_ref[q] = jnp.broadcast_to(decay, (8, LANES))
        return leaving, decay

    lax.fori_loop(
        0, spans, span, (jnp.zeros((LANES, LANES), F32), jnp.ones((1, LANES), F32)),
        unroll=UNROLL,
    )


def backward_within_kernel(
    x_ref, dy_ref, bc_ref, step_ref, run_ref, run_t_ref, cols_ref, seg_rows_ref,
    dxw_ref, dbc_ref, mask, cross, d_cross,
):
    pair = pl.program_id(0)
    spans = x_ref.shape[0] // ROWS

    @pl.when(pair == 0)
    def _():
        span_masks(cols_ref, seg_rows_ref, mask, spans)

        def products(q):
            at = pl.ds(span_start(q), ROWS)
            cross[q] = cross_product(bc_ref, at)
            d_cross[q] = jnp.zeros((ROWS, ROWS), F32)

        loop(spans, products)

    def span(q):
        at = pl.ds(span_start(q), ROWS)
        size = head_pair(step_ref[at, :], pair)
        weighted = (x_ref[at, :] * size).astype(BF16)
        first, second = decay_pair(run_ref, run_t_ref, mask, q, pair)
        dy, dy_rest = two_parts(dy_ref[at, :])
        apart = heads_apart(dy)
        both = jnp.concatenate([apart, heads_apart(dy_rest)], axis=1)
        d_mix = dot(both, jnp.concatenate([weighted, weighted], axis=1), CONTRACT_COLS)
        d_cross[q] += first * d_mix[:ROWS] + second * d_mix[ROWS:]
        mix = jnp.concatenate([first * cross[q], second * cross[q]], axis=0).astype(BF16)
        dxw_ref[at, :] = dot(mix, apart, CONTRACT_ROWS)

    loop(spans, span)

    @pl.when(pair == pl.num_programs(0) - 1)
    def _():
        def shared(q):
            at = pl.ds(span_start(q), ROWS)
            grad = d_cross[q].astype(BF16)
            b, c = b_parts(bc_ref, at), c_parts(bc_ref, at)
            both = dot(grad, c, CONTRACT_ROWS)
            dbc_ref[at, :LANES] = both[:, :LANES] + both[:, LANES:]
            both = dot(grad, b)
            dbc_ref[at, LANES:] = both[:, :LANES] + both[:, LANES:]

        loop(spans, shared)


def conv_back(pad_ref, d_pre, same, taps, spans, store, rim_store):
    def span(q):
        at = pl.ds(span_start(q), ROWS + RIM)
        long = d_pre[at, :]
        total = taps[3:4] * long[:ROWS]
        for ahead in (1, 2, 3):
            start = span_start(q) + ahead
            moved = d_pre[pl.ds(start, ROWS), :] * same[ahead - 1, pl.ds(start, ROWS), :]
            total = total + taps[3 - ahead : 4 - ahead] * moved
        store(q, total)

    loop(spans, span)
    head = d_pre[0:RIM, :]
    total = jnp.zeros((RIM, LANES), F32)
    for ahead in (1, 2, 3):
        masked = head * same[ahead - 1, 0:RIM, :]
        both = jnp.concatenate([jnp.zeros((RIM, LANES), F32), masked], axis=0)
        total = total + taps[3 - ahead : 4 - ahead] * pltpu.roll(both, 2 * RIM - ahead, axis=0)[:RIM]
    rim_store(total)


def tap_sums(d_pre, shifted):
    sums = [jnp.sum(d_pre * shifted[3 - k], axis=0, keepdims=True) for k in range(4)]
    sums.append(jnp.sum(d_pre, axis=0, keepdims=True))
    return jnp.concatenate(sums + [jnp.zeros((3, LANES), F32)], axis=0)


def silu_grad(pre):
    gate = sigmoid(pre)
    return gate * (1.0 + pre * (1.0 - gate))


def backward_finish_kernel(
    value_ref, ss_ref, rim_v_ref, rim_ss_ref, x_ref, dy_ref, scan_ref, dxw_ref, dbc_ref,
    state_ref, decay_ref, in_ref, grad_ref, back_ref, out_ref,
    bc_ref, step_ref, run_ref, cols_ref, conv_ref, conv_ss_ref, heads_ref, gains_ref,
    low_ref, tail_ref, rim_ref, taps_ref, low_ss_ref, tail_ss_ref, rim_ss_out_ref, taps_ss_ref, small_ref,
    pad, d_pre, same, cont, last, d_run, d_step, d_bc,
):
    pair = pl.program_id(0)
    rows = value_ref.shape[0]
    spans = rows // ROWS

    @pl.when(pair == 0)
    def _():
        def masks(q):
            row = span_start(q)
            for k in range(3):
                same[k, pl.ds(row, ROWS), :] = spread(cols_ref, row, k)
            cont[pl.ds(row, ROWS), :] = spread(cols_ref, row, 3)
            last[pl.ds(row, ROWS), :] = spread(cols_ref, row, 4)

        loop(spans, masks)
        same[:, rows:, :] = jnp.zeros((3, RIM, LANES), F32)
        d_pre[rows:, :] = jnp.zeros((RIM, LANES), F32)
        d_run[...] = jnp.zeros_like(d_run)
        d_step[...] = jnp.zeros_like(d_step)
        d_bc[...] = dbc_ref[...]

    pad[0:RIM, :] = rim_v_ref[...]
    pad[RIM:, :] = value_ref[...]
    taps, bias = conv_ref[0:4], conv_ref[4:5]
    skip = gains_ref[0:1]
    incoming, outgoing = in_ref[...], out_ref[...]
    selector = head_selector(pair)
    taps_ref[...] = jnp.zeros_like(taps_ref)
    final_row = row_ids(ROWS) == ROWS - 1

    def span(q):
        row = span_start(q)
        at = pl.ds(row, ROWS)
        x, dy = x_ref[at, :], dy_ref[at, :]
        size = head_pair(step_ref[at, :], pair)
        run = head_pair(run_ref[at, :], pair)
        enter = jnp.exp(run) * cont[at, :]
        to_end = jnp.exp(run[ROWS - 1 :] - run) * last[at, :]
        state, state_rest = two_parts(entering(state_ref, decay_ref, incoming, q, q - 1))
        after = state_ref[q] + decay_ref[q, 0:1, :] * incoming
        ahead = jnp.minimum(q + 1, spans - 1)
        grad = jnp.where(
            q + 1 < spans, grad_ref[ahead] + back_ref[ahead, 0:1, :] * outgoing, outgoing
        )
        weighted = x * size
        low_grad = grad.astype(BF16)
        d_weighted = dxw_ref[at, :] + to_end * dot(b_parts(bc_ref, at), twice(low_grad))
        entered = in_two(dy * enter)
        d_bc[at, LANES:] += dot(
            entered, jnp.concatenate([state, state], axis=1), CONTRACT_COLS
        ) + dot(entered[:, :LANES], state_rest, CONTRACT_COLS)
        d_bc[at, :LANES] += dot((weighted * to_end).astype(BF16), low_grad, CONTRACT_COLS)
        turn = dy.astype(BF16).astype(F32) * scan_ref[at, :]
        turn = turn - d_weighted * weighted.astype(BF16).astype(F32)
        turn = turn + jnp.where(final_row, jnp.sum(grad * after, axis=0, keepdims=True), 0.0)
        d_run[at, :] += split_sum(turn, selector)
        d_step[at, :] += split_sum(d_weighted * x, selector)
        pre, shifted = conv_span(pad, same, row, taps, bias)
        d_act = (d_weighted * size + skip * dy) * silu_grad(pre)
        d_pre[at, :] = d_act
        taps_ref[...] += tap_sums(d_act, shifted)

    loop(spans, span)

    def keep(q, total):
        low_ref[pl.ds(span_start(q), ROWS), :] = total.astype(BF16)

        @pl.when(q == spans - 1)
        def _():
            tail_ref[...] = total[ROWS - RIM :]

    def keep_rim(total):
        rim_ref[...] = total

    conv_back(pad, d_pre, same, taps, spans, keep, keep_rim)

    @pl.when(pair == pl.num_programs(0) - 1)
    def _():
        for part in range(2):
            lanes = slice(part * LANES, (part + 1) * LANES)
            pad[0:RIM, :] = rim_ss_ref[:, lanes]
            pad[RIM:, :] = ss_ref[:, lanes]
            part_taps, part_bias = conv_ss_ref[0:4, lanes], conv_ss_ref[4:5, lanes]
            taps_ss_ref[:, lanes] = jnp.zeros((8, LANES), F32)

            def shared(q):
                row = span_start(q)
                at = pl.ds(row, ROWS)
                pre, shifted = conv_span(pad, same, row, part_taps, part_bias)
                d_act = d_bc[at, lanes] * silu_grad(pre)
                d_pre[at, :] = d_act
                taps_ss_ref[:, lanes] += tap_sums(d_act, shifted)

            loop(spans, shared)

            def keep_ss(q, total):
                low_ss_ref[pl.ds(span_start(q), ROWS), lanes] = total.astype(BF16)

                @pl.when(q == spans - 1)
                def _():
                    tail_ss_ref[:, lanes] = total[ROWS - RIM :]

            def keep_rim_ss(total):
                rim_ss_out_ref[:, lanes] = total

            conv_back(pad, d_pre, same, part_taps, spans, keep_ss, keep_rim_ss)

        step_bias, rate = heads_ref[0:1, :], heads_ref[1:2, :]
        small_ref[...] = jnp.zeros_like(small_ref)
        tri_t = upper_ones()

        def steps(q):
            at = pl.ds(span_start(q), ROWS)
            d_decay = sum(dot(tri_t, part) for part in three_parts(d_run[at, :]))
            slope = sigmoid(ss_ref[at, 2 * LANES :] + step_bias)
            d_raw = (d_step[at, :] - d_decay * rate) * slope
            low_ss_ref[at, 2 * LANES :] = d_raw.astype(BF16)
            small_ref[0:1] += jnp.sum(d_raw, axis=0, keepdims=True)
            small_ref[1:2] -= jnp.sum(d_decay * step_ref[at, :] * rate, axis=0, keepdims=True)

        loop(spans, steps)


def store_tiles(slots_ref, out_ref, value, scatter):
    if not scatter:
        out_ref[...] = value
        return
    tile = value.shape[0] // slots_ref.shape[0]
    for k in range(slots_ref.shape[0]):
        start = pl.multiple_of(slots_ref[k] * tile, tile)
        out_ref[pl.ds(start, tile), :] = value[k * tile : (k + 1) * tile]


def branch_kernel(scatter, slots_ref, rows_ref, weight_ref, out_ref):
    store_tiles(slots_ref, out_ref, dot(rows_ref[...], weight_ref[...]).astype(BF16), scatter)


def normed_grad_kernel(
    scatter, slots_ref, gate_ref, value_ref, ss_ref, gate_w, value_w, ss_w, normed_ref, out_ref, diag_ref
):
    total = dot(gate_ref[...], gate_w[...], CONTRACT_COLS)
    total = total + dot(value_ref[...], value_w[...], CONTRACT_COLS)
    total = total + dot(ss_ref[...], ss_w[...], CONTRACT_COLS)
    store_tiles(slots_ref, out_ref, total.astype(BF16), scatter)
    sums = jnp.sum(total * normed_ref[...].astype(F32), axis=0, keepdims=True)
    diag_ref[...] = jnp.broadcast_to(sums, diag_ref.shape)


def whole(shape):
    return pl.BlockSpec(shape, lambda j: (0,) * len(shape))


def columns(rows, width=LANES):
    return pl.BlockSpec((rows, width), lambda j: (0, j))


def value_columns(rows):
    return pl.BlockSpec((rows, LANES), lambda j: (0, j + 3))


def stacks(count, rows):
    return pl.BlockSpec((count, rows, LANES), lambda j: (0, 0, j))


def params():
    return pltpu.CompilerParams(vmem_limit_bytes=VMEM_BYTES, dimension_semantics=("arbitrary",))


def shaped(shape, dtype):
    return jax.ShapeDtypeStruct(shape, dtype)


def scratch(*shape, dtype=F32):
    return pltpu.VMEM(shape, dtype)


class Sizes:
    def __init__(self, rows, inner, heads):
        self.rows, self.inner, self.heads = rows, inner, heads
        self.spans, self.pairs = rows // ROWS, inner // LANES
        self.width = max(8, heads)

    def cost(self):
        cells = self.rows * self.inner
        return pl.CostEstimate(flops=1, bytes_accessed=1, transcendentals=0)


def forward_states(s, both, rim, cols, conv_v, conv_ss, heads):
    return pl.pallas_call(
        forward_states_kernel,
        grid=(s.pairs,),
        in_specs=[
            value_columns(s.rows), whole((s.rows, 3 * LANES)), value_columns(RIM), whole((RIM, 3 * LANES)),
            whole((s.rows, 8)), columns(8), whole((8, 2 * LANES)), whole((8, LANES)),
        ],
        out_specs=[
            columns(s.rows), whole((s.rows, 4 * LANES)), whole((s.rows, LANES)), whole((s.rows, LANES)),
            whole((s.spans, s.width, LANES)), stacks(s.spans, LANES), stacks(s.spans, 8),
        ],
        out_shape=[
            shaped((s.rows, s.inner), F32), shaped((s.rows, 4 * LANES), BF16),
            shaped((s.rows, LANES), F32), shaped((s.rows, LANES), F32),
            shaped((s.spans, s.width, LANES), F32),
            shaped((s.spans, LANES, s.inner), F32), shaped((s.spans, 8, s.inner), F32),
        ],
        scratch_shapes=[
            scratch(s.rows + RIM, LANES), scratch(3, s.rows, LANES), scratch(s.rows, LANES),
            scratch(s.rows, LANES), scratch(s.spans, LANES, 2 * ROWS, dtype=BF16),
        ],
        compiler_params=params(),
        cost_estimate=s.cost(),
        name="forward_states",
    )(both, both, rim, rim, cols, conv_v, conv_ss, heads)


def forward_within(s, x, bc, step, run, run_t, cols, seg_rows):
    return pl.pallas_call(
        forward_within_kernel,
        grid=(s.pairs,),
        in_specs=[
            columns(s.rows), whole((s.rows, 4 * LANES)), whole((s.rows, LANES)), whole((s.rows, LANES)),
            whole((s.spans, s.width, LANES)), whole((s.rows, 8)), whole((s.spans, 8, LANES)),
        ],
        out_specs=columns(s.rows),
        out_shape=shaped((s.rows, s.inner), F32),
        scratch_shapes=[scratch(s.spans, ROWS, ROWS), scratch(s.spans, ROWS, ROWS)],
        compiler_params=params(),
        cost_estimate=s.cost(),
        name="forward_within",
    )(x, bc, step, run, run_t, cols, seg_rows)


def forward_finish(s, y, x, z, dgo, state, decay, incoming, bc, run, cols, gains):
    return pl.pallas_call(
        forward_finish_kernel,
        grid=(s.pairs,),
        in_specs=[
            columns(s.rows), columns(s.rows), columns(s.rows), columns(s.rows),
            stacks(s.spans, LANES), stacks(s.spans, 8), columns(LANES),
            whole((s.rows, 4 * LANES)), whole((s.rows, LANES)), whole((s.rows, 8)), columns(8),
        ],
        out_specs=[columns(s.rows), whole((s.spans, 16, LANES))],
        out_shape=[shaped((s.rows, s.inner), F32), shaped((s.spans, 16, LANES), F32)],
        scratch_shapes=[scratch(s.rows, LANES)] * 3,
        compiler_params=params(),
        cost_estimate=s.cost(),
        name="forward_finish",
    )(y, x, z, dgo, state, decay, incoming, bc, run, cols, gains)


def gate_back(s, inner_width, scan, x, z, dgo, sums, bc, run, cols, gains):
    def kernel(*refs):
        gate_back_kernel(inner_width, *refs)

    return pl.pallas_call(
        kernel,
        grid=(s.pairs,),
        in_specs=[
            columns(s.rows), columns(s.rows), columns(s.rows), columns(s.rows),
            whole((s.spans, 8, LANES)), whole((s.rows, 4 * LANES)), whole((s.rows, LANES)),
            whole((s.rows, 8)), columns(8),
        ],
        out_specs=[
            columns(s.rows), columns(s.rows), columns(s.rows), stacks(s.spans, LANES),
            stacks(s.spans, 8), columns(8),
        ],
        out_shape=[
            shaped((s.rows, s.inner), BF16), shaped((s.rows, s.inner), BF16),
            shaped((s.rows, s.inner), F32), shaped((s.spans, LANES, s.inner), F32),
            shaped((s.spans, 8, s.inner), F32), shaped((8, s.inner), F32),
        ],
        scratch_shapes=[scratch(s.rows, LANES)] * 3 + [scratch(s.spans, LANES, 2 * ROWS, dtype=BF16)],
        compiler_params=params(),
        cost_estimate=s.cost(),
        name="gate_back",
    )(scan, x, z, dgo, sums, bc, run, cols, gains)


def backward_within(s, x, dy, bc, step, run, run_t, cols, seg_rows):
    return pl.pallas_call(
        backward_within_kernel,
        grid=(s.pairs,),
        in_specs=[
            columns(s.rows), columns(s.rows), whole((s.rows, 4 * LANES)), whole((s.rows, LANES)),
            whole((s.rows, LANES)), whole((s.spans, s.width, LANES)), whole((s.rows, 8)),
            whole((s.spans, 8, LANES)),
        ],
        out_specs=[columns(s.rows), whole((s.rows, 2 * LANES))],
        out_shape=[shaped((s.rows, s.inner), F32), shaped((s.rows, 2 * LANES), F32)],
        scratch_shapes=[scratch(s.spans, ROWS, ROWS)] * 3,
        compiler_params=params(),
        cost_estimate=s.cost(),
        name="backward_within",
    )(x, dy, bc, step, run, run_t, cols, seg_rows)


def backward_finish(
    s, both, rim, x, dy, scan, dxw, dbc, state, decay, incoming, grad, back, outgoing,
    bc, step, run, cols, conv_v, conv_ss, heads, gains,
):
    return pl.pallas_call(
        backward_finish_kernel,
        grid=(s.pairs,),
        in_specs=[
            value_columns(s.rows), whole((s.rows, 3 * LANES)), value_columns(RIM), whole((RIM, 3 * LANES)),
            columns(s.rows), columns(s.rows), columns(s.rows), columns(s.rows), whole((s.rows, 2 * LANES)),
            stacks(s.spans, LANES), stacks(s.spans, 8), columns(LANES),
            stacks(s.spans, LANES), stacks(s.spans, 8), columns(LANES),
            whole((s.rows, 4 * LANES)), whole((s.rows, LANES)), whole((s.rows, LANES)), whole((s.rows, 8)),
            columns(8), whole((8, 2 * LANES)), whole((8, LANES)), columns(8),
        ],
        out_specs=[
            columns(s.rows), columns(RIM), columns(RIM), columns(8),
            whole((s.rows, 3 * LANES)), whole((RIM, 2 * LANES)), whole((RIM, 2 * LANES)),
            whole((8, 2 * LANES)), whole((8, LANES)),
        ],
        out_shape=[
            shaped((s.rows, s.inner), BF16), shaped((RIM, s.inner), F32), shaped((RIM, s.inner), F32),
            shaped((8, s.inner), F32), shaped((s.rows, 3 * LANES), BF16), shaped((RIM, 2 * LANES), F32),
            shaped((RIM, 2 * LANES), F32), shaped((8, 2 * LANES), F32), shaped((8, LANES), F32),
        ],
        scratch_shapes=[
            scratch(s.rows + RIM, LANES), scratch(s.rows + RIM, LANES), scratch(3, s.rows + RIM, LANES),
            scratch(s.rows, LANES), scratch(s.rows, LANES), scratch(s.rows, LANES), scratch(s.rows, LANES),
            scratch(s.rows, 2 * LANES),
        ],
        compiler_params=params(),
        cost_estimate=s.cost(),
        name="backward_finish",
    )(
        both, both, rim, rim, x, dy, scan, dxw, dbc, state, decay, incoming, grad, back, outgoing,
        bc, step, run, cols, conv_v, conv_ss, heads, gains,
    )


WIDE = 256


def tile_product(kernel, slots, operands, specs, outs, out_specs, blocks, flops):
    rows = operands[0].shape[0]
    scatter = (rows // slots.shape[0]) % 16 == 0

    def body(*refs):
        kernel(scatter, *refs)

    results = pl.pallas_call(
        body,
        grid_spec=pltpu.PrefetchScalarGridSpec(
            num_scalar_prefetch=1, grid=(blocks,), in_specs=specs, out_specs=out_specs
        ),
        out_shape=outs,
        compiler_params=params(),
        cost_estimate=pl.CostEstimate(flops=1, bytes_accessed=1, transcendentals=0),
        name=kernel.__name__,
    )(slots, *operands)
    return results, scatter


def fixed(shape):
    return pl.BlockSpec(shape, lambda j, slots: (0,) * len(shape))


def branch_rows(slots, back_index, gated_low, out_proj):
    rows, inner = gated_low.shape
    width = out_proj.shape[1]
    [out], scatter = tile_product(
        branch_kernel,
        slots,
        (gated_low, out_proj),
        [fixed((rows, inner)), pl.BlockSpec((inner, WIDE), lambda j, slots: (0, j))],
        [shaped((rows, width), BF16)],
        [pl.BlockSpec((rows, WIDE), lambda j, slots: (0, j))],
        width // WIDE,
        2 * rows * inner * width,
    )
    return out if scatter else move_tiles(out, back_index)


def normed_grad(slots, back_index, lows, weights, normed):
    rows, width = normed.shape
    (out, diag), scatter = tile_product(
        normed_grad_kernel,
        slots,
        (*lows, *weights, normed),
        [fixed(low.shape) for low in lows]
        + [pl.BlockSpec((WIDE, w.shape[1]), lambda j, slots: (j, 0)) for w in weights]
        + [pl.BlockSpec((rows, WIDE), lambda j, slots: (0, j))],
        [shaped((rows, width), BF16), shaped((8, width), F32)],
        [pl.BlockSpec((rows, WIDE), lambda j, slots: (0, j)), pl.BlockSpec((8, WIDE), lambda j, slots: (0, j))],
        width // WIDE,
        2 * rows * width * sum(low.shape[1] for low in lows),
    )
    return (out if scatter else move_tiles(out, back_index)), diag[0]


def swapped(value, axis, bit):
    count = lax.axis_size(axis)
    return lax.ppermute(value, axis, [(k, k ^ (1 << bit)) for k in range(count)])


def axis_bits(axis):
    return lax.axis_size(axis).bit_length() - 1


class RowsOverSeq:
    def __init__(self, grads, seq_index, backwards):
        bits, count = axis_bits("seq"), lax.axis_size("seq")
        self.here = seq_index
        self.total = grads.reshape((2,) * bits + (grads.shape[0] // count, grads.shape[1]))
        self.left = list(range(bits))[::-1]
        self.order = [0] + (list(range(1, bits))[::-1] if backwards else list(range(1, bits)))

    def swap(self):
        bit = self.order.pop(0)
        at, own = self.left.index(bit), (self.here >> bit) & 1
        self.left.pop(at)
        self.keep = lax.dynamic_index_in_dim(self.total, own, at, keepdims=False)
        self.send = lax.dynamic_index_in_dim(self.total, 1 - own, at, keepdims=False)
        return swapped(self.send, "seq", bit)

    def join(self, got):
        total = self.keep.astype(F32) + got.astype(F32)
        self.total = total.astype(self.total.dtype) if self.order else total


class SumByPairs:
    def __init__(self, value, axis):
        self.size, self.axis = value.shape[0], axis
        padded = jnp.pad(value, (0, -self.size % (8 * LANES)))
        self.total, self.order = padded.reshape(-1, LANES), list(range(axis_bits(axis)))

    def swap(self):
        self.keep = self.send = self.total
        return swapped(self.send, self.axis, self.order.pop(0))

    def join(self, got):
        self.total = self.keep + got
        if not self.order:
            self.total = self.total.reshape(-1)[: self.size]


class SumByHalves:
    def __init__(self, value, axis):
        self.total, self.axis, self.here = value, axis, lax.axis_index(axis)
        bits = list(range(axis_bits(axis)))
        self.order = [(bit, True) for bit in bits[::-1]] + [(bit, False) for bit in bits]

    def swap(self):
        bit, self.adds = self.order.pop(0)
        self.own = (self.here >> bit) & 1
        if self.adds:
            half = self.total.shape[0] // 2
            self.keep = lax.dynamic_slice_in_dim(self.total, self.own * half, half, 0)
            self.send = lax.dynamic_slice_in_dim(self.total, (1 - self.own) * half, half, 0)
        else:
            self.keep = self.send = self.total.astype(BF16)
        return swapped(self.send, self.axis, bit)

    def join(self, got):
        if self.adds:
            self.total = self.keep.astype(F32) + got.astype(F32)
            return
        mine, upper = self.keep, self.own == 1
        self.total = jnp.concatenate(
            [jnp.where(upper, got, mine), jnp.where(upper, mine, got)], axis=0
        )


class Chain:
    def __init__(self, part, *makers):
        self.part, self.makers, self.totals = part, list(makers), []

    @property
    def order(self):
        while not self.part.order and self.makers:
            self.totals.append(self.part.total)
            self.part = self.makers.pop(0)(self.part.total)
        return self.part.order

    @property
    def total(self):
        return self.part.total

    def swap(self):
        return self.part.swap()

    def join(self, got):
        self.part.join(got)


def swap_all(parts):
    return [(part, part.swap()) for part in parts if part.order]


def join_all(parts, got, *tokens):
    if not got:
        return
    arrived = lax.optimization_barrier((tuple(piece for _, piece in got), *tokens))[0]
    for (part, _), piece in zip(got, arrived):
        part.join(piece)


def finish_all(parts):
    while any(part.order for part in parts):
        join_all(parts, swap_all(parts))


def carried_states(states, decay, reverse, *covers, results=None):
    count = lax.axis_size("seq")
    sign = -1 if reverse else 1
    both = jnp.concatenate([states, decay], axis=0)
    results = [] if results is None else results

    def cover(reach, got):
        if len(results) == len(covers):
            return got
        result, token = covers[len(results)](reach)
        results.append(result)
        return after(got, token)

    def joined(near, far):
        through = near[LANES : LANES + 1]
        return jnp.concatenate([near[:LANES], jnp.zeros_like(near[LANES:])], axis=0) + through * far

    near, far = (from_behind(both, "seq", sign * k) for k in (1, 2))
    near, far = cover(both, (near, far))
    reach, width = joined(near, far), 2
    while width < count - 1:
        reach = joined(reach, cover(reach, from_behind(reach, "seq", sign * width)))
        width *= 2
    while len(results) < len(covers):
        cover(reach, reach)
    return reach[:LANES], results


def after(value, *tokens):
    return lax.optimization_barrier((value, *tokens))[0]


def from_behind(value, axis, steps):
    count = lax.axis_size(axis)
    initial, last = (max(0, -steps), min(count, count - steps))
    return lax.ppermute(value, axis, [(source, source + steps) for source in range(initial, last)])


def move_tiles(rows, index):
    tile_total = index.shape[0]
    shaped_rows = rows.reshape((tile_total, rows.shape[0] // tile_total) + rows.shape[1:])
    return jnp.take(shaped_rows, index, axis=0, mode="clip").reshape(rows.shape)


def carry_weights(decays, here, reverse):
    count = decays.shape[0]
    ids = jnp.arange(count, dtype=jnp.int32)
    if reverse:
        between = (ids[None, :] < ids[:, None]) & (ids[None, :] > here)
        reached = ids > here
    else:
        between = (ids[None, :] > ids[:, None]) & (ids[None, :] < here)
        reached = ids < here
    chain = jnp.prod(jnp.where(between[:, :, None], decays[None, :, :], 1.0), axis=1)
    return jnp.where(reached[:, None], chain, 0.0)


def padded_rows(parts, rows=8):
    stacked = jnp.concatenate([part.reshape(-1, part.shape[-1]) for part in parts], axis=0)
    return jnp.pad(stacked, ((0, rows - stacked.shape[0]), (0, 0)))


def local(
    tokens,
    packing,
    segment_ids,
    norm_gain,
    gate_proj,
    value_proj,
    shared_proj,
    step_proj,
    conv_value,
    conv_value_bias,
    conv_shared,
    conv_shared_bias,
    step_bias,
    log_decay,
    skip_gain,
    gated_gain,
    out_proj,
    cotangent,
):
    own_rows = tokens.shape[0]
    head_shards = lax.axis_size("head")
    seq_shards = lax.axis_size("seq")
    head_index = lax.axis_index("head")
    seq_index = lax.axis_index("seq")
    shard_rows = own_rows * head_shards
    inner_local = gate_proj.shape[1]
    heads_local = step_proj.shape[1]
    inner_width = inner_local * head_shards
    tile_rows = own_rows // seq_shards
    tile_count = shard_rows // tile_rows
    s = Sizes(shard_rows, inner_local, heads_local)

    packed_tiles = packing.reshape(-1, tile_rows)[:, 0] // tile_rows
    own_device = seq_index * head_shards + head_index
    seq_ids = jnp.arange(seq_shards, dtype=jnp.int32)
    own_tiles = own_device * seq_shards + seq_ids
    tile_match = (own_tiles[:, None] == packed_tiles[None, :]).astype(jnp.int32)
    tile_shard = jnp.arange(packed_tiles.shape[0], dtype=jnp.int32) // tile_count
    dest_shard = jnp.sum(tile_match * tile_shard[None, :], axis=1)
    send_index = jnp.sum(
        (dest_shard[None, :] == seq_ids[:, None]).astype(jnp.int32) * seq_ids[None, :], axis=1
    )
    own_packed = lax.dynamic_slice_in_dim(packed_tiles, seq_index * tile_count, tile_count, 0)
    source_device = own_packed // seq_shards
    arrival = source_device % head_shards * seq_shards + source_device // head_shards
    slot_ids = jnp.arange(tile_count, dtype=jnp.int32)
    back_index = jnp.sum(
        (arrival[None, :] == slot_ids[:, None]).astype(jnp.int32) * slot_ids[None, :], axis=1
    )

    shard_start = seq_index * shard_rows
    around = jnp.concatenate([jnp.full((RIM,), -1, jnp.int32), segment_ids])
    around = lax.dynamic_slice_in_dim(around, shard_start, shard_rows + RIM, 0)
    seg = around[RIM:]
    span_last = around[RIM - 1 :: ROWS]
    before_span = jnp.repeat(span_last[:-1], ROWS)
    end_of_span = jnp.repeat(span_last[1:], ROWS)
    facts = [around[RIM - k : RIM - k + shard_rows] == seg for k in (1, 2, 3)]
    facts += [before_span == seg, end_of_span == seg, seg, seg, seg]
    cols = jnp.stack([fact.astype(F32) for fact in facts], axis=1)
    seg_rows = jnp.broadcast_to(seg.astype(F32).reshape(s.spans, 1, ROWS), (s.spans, 8, ROWS))

    head_pad = ((0, 0), (0, LANES - heads_local))
    heads = padded_rows([step_bias, jnp.exp(log_decay)])
    heads = jnp.pad(heads, head_pad)
    conv_v = padded_rows([conv_value, conv_value_bias])
    conv_ss = padded_rows([conv_shared, conv_shared_bias])
    gains = padded_rows([jnp.repeat(skip_gain, inner_local // heads_local), gated_gain])
    ss_proj = jnp.concatenate([shared_proj, jnp.pad(step_proj, head_pad)], axis=1)

    tok_float = tokens.astype(F32)
    tok_rstd = lax.rsqrt(jnp.mean(tok_float * tok_float, axis=1, keepdims=True) + EPS)
    normed = (tok_float * tok_rstd * norm_gain[None, :]).astype(BF16)

    def to_shard(rows):
        sent = lax.all_to_all(
            move_tiles(rows, send_index), "seq", split_axis=0, concat_axis=0, tiled=True
        )
        return lax.all_gather(sent, "head", axis=0, tiled=True)

    packed_normed = move_tiles(to_shard(normed), arrival)
    arrived_cot = to_shard(cotangent)

    both = dot(packed_normed, jnp.concatenate([ss_proj, value_proj], axis=1))
    rim = from_behind(both[shard_rows - RIM :], "seq", 1)
    x, bc, step, run, run_t, state, decay = forward_states(
        s, both, rim, cols, conv_v, conv_ss, heads
    )

    def project_gate(reach):
        z = dot(after(packed_normed, reach), gate_proj)
        return z, z

    def within(reach):
        y = forward_within(s, after(x, reach), bc, step, run, run_t, cols, seg_rows)
        return y, y

    def cot_products(reach):
        cot = move_tiles(arrived_cot, after(arrival, reach))
        dgo = dot(cot, out_proj, CONTRACT_COLS)
        return (cot, dgo), dgo

    incoming, (y, gate_z, (packed_cot, dgo)) = carried_states(
        state[s.spans - 1], decay[s.spans - 1], False, within, project_gate, cot_products
    )
    scan, sums = forward_finish(
        s, y, x, gate_z, dgo, state, decay, incoming, bc, run, cols, gains
    )
    sums = lax.psum(jnp.stack([sums[:, 0, :], sums[:, 8, :]], axis=1), "head")
    sums = jnp.pad(sums, ((0, 0), (0, 6), (0, 0)))
    gated_low, low_gate, dy, grad, back, gate_rows = gate_back(
        s, inner_width, scan, x, gate_z, dgo, sums, bc, run, cols, gains
    )

    starts = lax.all_gather(jnp.concatenate([grad[0], decay[s.spans - 1]], axis=0), "seq")
    branch = branch_rows(arrival, back_index, gated_low, out_proj)
    dxw, dbc = backward_within(s, x, after(dy, branch), bc, step, run, run_t, cols, seg_rows)
    out_grads = dot(after(gated_low, dbc), packed_cot, CONTRACT_ROWS).astype(BF16)
    gate_grads = dot(after(packed_normed, out_grads), low_gate, CONTRACT_ROWS).astype(BF16)
    branch = lax.psum_scatter(
        after(branch, gate_grads), "head", scatter_dimension=0, tiled=True
    )
    out_sum = RowsOverSeq(out_grads, seq_index, True)
    gate_sum = RowsOverSeq(gate_grads, seq_index, False)
    early = [out_sum, gate_sum]
    got = swap_all(early)
    decays = starts[:, LANES, :]
    outgoing = jnp.sum(
        carry_weights(decays, seq_index, True)[:, None, :] * starts[:, :LANES, :], axis=0
    )
    dy = after(dy, gate_grads, *[part.keep for part in early], *[part.send for part in early])
    low_value, tail, rim_out, taps_v, low_ss, tail_ss, rim_ss_out, taps_ss, small = backward_finish(
        s, both, rim, x, dy, scan, dxw, dbc, state, decay, incoming, grad, back,
        outgoing, bc, step, run, cols, conv_v, conv_ss, heads, gains,
    )
    join_all(early, got, small)
    got = swap_all(early)
    rim_out = after(rim_out, *[part.send for part in early])
    rim_back = from_behind(jnp.concatenate([rim_out, rim_ss_out], axis=1), "seq", -1)
    tail = (jnp.concatenate([tail, tail_ss], axis=1) + rim_back).astype(BF16)
    low_value = lax.dynamic_update_slice(low_value, tail[:, :inner_local], (shard_rows - RIM, 0))
    low_ss = lax.dynamic_update_slice(low_ss, tail[:, inner_local:], (shard_rows - RIM, 0))

    ss_grads = dot(packed_normed, low_ss, CONTRACT_ROWS)
    shared_sum = Chain(
        RowsOverSeq(ss_grads[:, : 2 * LANES], seq_index, False), lambda total: SumByHalves(total, "head")
    )
    step_rows = RowsOverSeq(ss_grads[:, 2 * LANES :].astype(BF16), seq_index, False)
    got += swap_all([shared_sum, step_rows])
    low_gate = after(low_gate, ss_grads)
    d_normed, grad_norm_rows = normed_grad(
        arrival,
        back_index,
        (low_gate, low_value, low_ss),
        (gate_proj, value_proj, ss_proj),
        packed_normed,
    )
    arrived, low_value = lax.optimization_barrier(
        (tuple(piece for _, piece in got), after(low_value, d_normed))
    )
    d_normed = lax.psum_scatter(
        after(d_normed, branch), "head", scatter_dimension=0, tiled=True
    )
    for (part, _), piece in zip(got, arrived):
        part.join(piece)
    value_grads = dot(packed_normed, low_value, CONTRACT_ROWS).astype(BF16)

    first = swap_all([shared_sum, step_rows])
    gate_rows, small, taps_v, taps_ss, grad_norm_rows = after(
        (gate_rows, small, taps_v, taps_ss, grad_norm_rows), shared_sum.part.send
    )
    per_head = [jnp.sum(gate_rows[1].reshape(heads_local, -1), axis=1)]
    per_head += [small[0, :heads_local], small[1, :heads_local]]
    pieces = [taps_v[:5].reshape(-1), gate_rows[0]] + per_head
    own_size = sum(piece.shape[0] for piece in pieces)
    shared_pieces = [taps_ss[:5].reshape(-1), grad_norm_rows]
    flat_sum = Chain(
        SumByPairs(jnp.concatenate(pieces + shared_pieces), "seq"),
        lambda total: SumByPairs(total[own_size:], "head"),
    )
    half = inner_local // 2
    short = [shared_sum, flat_sum, step_rows]
    got = first + swap_all([flat_sum])
    arrived, value_grads = lax.optimization_barrier((tuple(piece for _, piece in got), value_grads))
    for (part, _), piece in zip(got, arrived):
        part.join(piece)
    values = [
        RowsOverSeq(value_grads[:, :half], seq_index, False),
        RowsOverSeq(value_grads[:, half:], seq_index, True),
    ]
    beside = [values, [], values, [], values]
    while any(part.order for part in short):
        got = swap_all(short + (beside.pop(0) if beside else []))
        if len(beside) == 1:
            arrived, branch_back = lax.optimization_barrier(
                (tuple(piece for _, piece in got), branch_back)
            )
            got = [(part, piece) for (part, _), piece in zip(got, arrived)]
        join_all(None, got)
        if len(beside) == 3:
            branch = after(branch, shared_sum.total)
            branch_back = lax.all_to_all(branch, "seq", split_axis=0, concat_axis=0, tiled=True)
    last = swap_all(early)
    normed_back = lax.all_to_all(d_normed, "seq", split_axis=0, concat_axis=0, tiled=True)
    arrived, normed_back = lax.optimization_barrier(
        (tuple(piece for _, piece in last), normed_back)
    )
    for (part, _), piece in zip(last, arrived):
        part.join(piece)
    finish_all(values + early)
    everything, grad_shared, shared_sums = flat_sum.totals[0], shared_sum.total, flat_sum.total
    grad_out_proj, grad_gate = out_sum.total, gate_sum.total
    grad_value = jnp.concatenate([part.total for part in values], axis=1)
    grad_step_proj = step_rows.total[:, :heads_local]
    grad_shared = lax.all_gather(grad_shared, "seq", axis=0, tiled=True).astype(F32)

    branch_given = move_tiles(branch_back, dest_shard).astype(F32)
    d_normed_given = move_tiles(normed_back, dest_shard).astype(F32)
    mixed_rows = (tok_float + branch_given).astype(BF16)
    scaled = d_normed_given * norm_gain[None, :]
    row_dot = jnp.sum(scaled * tok_float, axis=1, keepdims=True) / tokens.shape[1]
    d_tok = tok_rstd * scaled - tok_float * (tok_rstd * tok_rstd * tok_rstd * row_dot)
    grad_tokens = (cotangent.astype(F32) + d_tok).astype(BF16)

    own_taps = everything[: 5 * inner_local].reshape(5, inner_local)
    rest = everything[5 * inner_local : own_size]
    grad_gated = rest[:inner_local]
    rest = rest[inner_local:]
    grad_skip = rest[:heads_local]
    grad_step_bias = rest[heads_local : 2 * heads_local]
    grad_log_decay = rest[2 * heads_local :]
    shared_taps = shared_sums[: 10 * LANES].reshape(5, 2 * LANES)
    grad_norm_gain = shared_sums[10 * LANES : 10 * LANES + norm_gain.shape[0]] / norm_gain
    return (
        mixed_rows,
        grad_tokens,
        grad_norm_gain,
        grad_gate,
        grad_value,
        grad_shared,
        grad_step_proj,
        own_taps[:4],
        own_taps[4],
        shared_taps[:4],
        shared_taps[4],
        grad_step_bias,
        grad_log_decay,
        grad_skip,
        grad_gated,
        grad_out_proj,
    )


def solution(mesh):
    placed = (
        P(("seq", "head"), None),
        P(),
        P(),
        P(),
        P(None, "head"),
        P(None, "head"),
        P(),
        P(None, "head"),
        P(None, "head"),
        P("head"),
        P(),
        P(),
        P("head"),
        P("head"),
        P("head"),
        P("head"),
        P("head", None),
        P(("seq", "head"), None),
    )
    return jax.shard_map(
        local,
        mesh=mesh,
        in_specs=placed,
        out_specs=(
            P(("seq", "head"), None),
            P(("seq", "head"), None),
            P(),
            P("seq", "head"),
            P("seq", "head"),
            P(),
            P("seq", "head"),
            P(None, "head"),
            P("head"),
            P(),
            P(),
            P("head"),
            P("head"),
            P("head"),
            P("head"),
            P(("head", "seq"), None),
        ),
        check_vma=False,
    )
```

```python
import jax
import jax.numpy as jnp
from jax import lax
from jax.experimental import pallas as pl
from jax.experimental.pallas import tpu as pltpu
from jax.sharding import PartitionSpec as P

EPS = 1e-05
ROWS = 128
LANES = 128
HALF = 64
RIM = 8
FAR = -1e30
UNROLL = 8
F32 = jnp.float32
BF16 = jnp.bfloat16
VMEM_BYTES = 56 * 1024 * 1024
CONTRACT_ROWS = (((0,), (0,)), ((), ()))
CONTRACT_COLS = (((1,), (1,)), ((), ()))


def dot(a, b, dims=(((1,), (0,)), ((), ()))):
    return lax.dot_general(a, b, dims, preferred_element_type=F32)


def two_parts(x):
    upper = x.astype(BF16)
    return upper, (x - upper.astype(F32)).astype(BF16)


def three_parts(x):
    upper, rest = x.astype(BF16), x
    rest = x - upper.astype(F32)
    middle = rest.astype(BF16)
    return upper, middle, (rest - middle.astype(F32)).astype(BF16)


def in_two(x):
    return jnp.concatenate(two_parts(x), axis=1)


def twice(x):
    return jnp.concatenate([x, x], axis=0)


def b_parts(bc_ref, at):
    return bc_ref[at, : 2 * LANES]


def c_parts(bc_ref, at):
    return bc_ref[at, 2 * LANES :]


def cross_product(bc_ref, at):
    b, c = b_parts(bc_ref, at), c_parts(bc_ref, at)
    upper = jnp.concatenate([b[:, :LANES], b[:, :LANES]], axis=1)
    return dot(c, upper, CONTRACT_COLS) + dot(c[:, :LANES], b[:, LANES:], CONTRACT_COLS)


def lane_ids(rows):
    return lax.broadcasted_iota(jnp.int32, (rows, LANES), 1)


def row_ids(rows):
    return lax.broadcasted_iota(jnp.int32, (rows, LANES), 0)


def from_head(block, head):
    index = head + jnp.zeros(block.shape, jnp.int32)
    return jnp.take_along_axis(block, index, axis=1)


def head_cols(block, pair):
    return from_head(block, 2 * pair), from_head(block, 2 * pair + 1)


def head_pair(block, pair):
    return from_head(block, 2 * pair + jnp.where(lane_ids(block.shape[0]) < HALF, 0, 1))


def head_selector(pair):
    lane = row_ids(LANES)
    head = 2 * pair + jnp.where(lane < HALF, 0, 1)
    return (lane_ids(LANES) == head).astype(F32).astype(BF16)


def split_sum(x, selector):
    upper, lower = two_parts(x)
    stacked = jnp.concatenate([upper, lower], axis=1)
    return dot(stacked, jnp.concatenate([selector, selector], axis=0))


def lower_ones():
    return (row_ids(ROWS) >= lane_ids(ROWS)).astype(F32).astype(BF16)


def upper_ones():
    return (row_ids(ROWS) <= lane_ids(ROWS)).astype(F32).astype(BF16)


def spread(ref, row, col):
    return jnp.broadcast_to(ref[pl.ds(row, ROWS), col : col + 1], (ROWS, LANES))


def softplus(x):
    return jnp.maximum(x, 0.0) + jnp.log1p(jnp.exp(-jnp.abs(x)))


def sigmoid(x):
    return 1.0 / (1.0 + jnp.exp(-x))


def span_start(q):
    return pl.multiple_of(q * ROWS, ROWS)


def loop(count, body):
    def step(q, carry):
        body(q)
        return carry

    lax.fori_loop(0, count, step, 0, unroll=UNROLL)


def conv_span(pad_ref, same_ref, row, taps, bias):
    long = pad_ref[pl.ds(row, ROWS + RIM), :]
    total = bias + taps[3:4] * long[RIM:]
    shifted = []
    for back in (1, 2, 3):
        moved = pad_ref[pl.ds(row + RIM - back, ROWS), :]
        moved = moved * same_ref[back - 1, pl.ds(row, ROWS), :]
        shifted.append(moved)
        total = total + taps[3 - back : 4 - back] * moved
    return total, [long[RIM:]] + shifted


def forward_states_kernel(
    value_ref, ss_ref, rim_v_ref, rim_ss_ref, cols_ref, conv_ref, conv_ss_ref, heads_ref,
    x_ref, bc_ref, step_ref, run_ref, run_t_ref, state_ref, decay_ref,
    pad, same, cont, last, bt,
):
    pair = pl.program_id(0)
    rows = value_ref.shape[0]
    spans = rows // ROWS
    width = run_t_ref.shape[1]

    @pl.when(pair == 0)
    def _():
        def masks(q):
            row = span_start(q)
            for k in range(3):
                same[k, pl.ds(row, ROWS), :] = spread(cols_ref, row, k)
            cont[pl.ds(row, ROWS), :] = spread(cols_ref, row, 3)
            last[pl.ds(row, ROWS), :] = spread(cols_ref, row, 4)

        loop(spans, masks)
        for part in range(2):
            lanes = slice(part * LANES, (part + 1) * LANES)
            pad[0:RIM, :] = rim_ss_ref[:, lanes]
            pad[RIM:, :] = ss_ref[:, lanes]
            taps, bias = conv_ss_ref[0:4, lanes], conv_ss_ref[4:5, lanes]

            def shared(q):
                row = span_start(q)
                pre, _ = conv_span(pad, same, row, taps, bias)
                act = pre * sigmoid(pre)
                bc_ref[pl.ds(row, ROWS), 2 * part * LANES : 2 * (part + 1) * LANES] = in_two(act)
                if part == 0:
                    bt[q] = in_two(jnp.transpose(act))

            loop(spans, shared)

        bias, rate = heads_ref[0:1, :], heads_ref[1:2, :]
        tri, tri_t = lower_ones(), upper_ones()

        def steps(q):
            row = span_start(q)
            size = softplus(ss_ref[pl.ds(row, ROWS), 2 * LANES :] + bias)
            step_ref[pl.ds(row, ROWS), :] = size
            parts = three_parts(-size * rate)
            run_ref[pl.ds(row, ROWS), :] = sum(dot(tri, part) for part in parts)
            turned = sum(dot(part, tri_t, CONTRACT_ROWS) for part in parts)
            run_t_ref[q] = turned[:width]

        loop(spans, steps)

    pad[0:RIM, :] = rim_v_ref[...]
    pad[RIM:, :] = value_ref[...]
    taps, bias = conv_ref[0:4], conv_ref[4:5]

    def span(q, carry):
        state, decay = carry
        row = span_start(q)
        at = pl.ds(row, ROWS)
        pre, _ = conv_span(pad, same, row, taps, bias)
        x = pre * sigmoid(pre)
        x_ref[at, :] = x
        size = head_pair(step_ref[at, :], pair)
        run = head_pair(run_ref[at, :], pair)
        enter = jnp.exp(run[ROWS - 1 :]) * cont[pl.ds(row + ROWS - 8, 8), :][7:8]
        to_end = jnp.exp(run[ROWS - 1 :] - run) * last[at, :]
        state = state * enter + dot(bt[q], twice((x * size * to_end).astype(BF16)))
        decay = decay * enter
        state_ref[q] = state
        decay_ref[q] = jnp.broadcast_to(decay, (8, LANES))
        return state, decay

    lax.fori_loop(
        0, spans, span, (jnp.zeros((LANES, LANES), F32), jnp.ones((1, LANES), F32)),
        unroll=UNROLL,
    )


def span_masks(cols_ref, seg_rows_ref, bias_ref, spans):
    causal = row_ids(ROWS) >= lane_ids(ROWS)

    def mask(q):
        own = spread(cols_ref, span_start(q), 5)
        other = jnp.broadcast_to(seg_rows_ref[q, 0:1, :], (ROWS, ROWS))
        bias_ref[q] = jnp.where(causal & (own == other), 0.0, FAR)

    loop(spans, mask)


def decay_pair(run_ref, run_t_ref, mask_ref, q, pair):
    first, second = head_cols(run_ref[pl.ds(span_start(q), ROWS), :], pair)
    rows = run_t_ref[q, pl.ds(2 * pair, 2), :]
    mask = mask_ref[q]
    return jnp.exp(first - rows[0:1] + mask), jnp.exp(second - rows[1:2] + mask)


def heads_apart(x):
    lane = lane_ids(x.shape[0])
    zero = jnp.zeros_like(x)
    return jnp.concatenate([jnp.where(lane < HALF, x, zero), jnp.where(lane < HALF, zero, x)], axis=0)


def forward_within_kernel(
    x_ref, bc_ref, step_ref, run_ref, run_t_ref, cols_ref, seg_rows_ref, y_ref, mask, cross
):
    pair = pl.program_id(0)
    spans = x_ref.shape[0] // ROWS

    @pl.when(pair == 0)
    def _():
        span_masks(cols_ref, seg_rows_ref, mask, spans)

        def products(q):
            at = pl.ds(span_start(q), ROWS)
            cross[q] = cross_product(bc_ref, at)

        loop(spans, products)

    def span(q):
        at = pl.ds(span_start(q), ROWS)
        size = head_pair(step_ref[at, :], pair)
        weighted = x_ref[at, :] * size
        first, second = decay_pair(run_ref, run_t_ref, mask, q, pair)
        mix = jnp.concatenate([first * cross[q], second * cross[q]], axis=1).astype(BF16)
        y_ref[at, :] = dot(mix, heads_apart(weighted).astype(BF16))

    loop(spans, span)


def entering(state_ref, decay_ref, incoming, q, before):
    at = jnp.maximum(before, 0)
    local = state_ref[at] + decay_ref[at, 0:1, :] * incoming
    return jnp.where(before >= 0, local, incoming)


def row_sums(acc_ref, out_ref, base, spans):
    ones = jnp.ones((8, LANES), BF16)

    def total(q):
        parts = three_parts(acc_ref[pl.ds(span_start(q), ROWS), :])
        out_ref[q, base : base + 8, :] = sum(dot(ones, part, CONTRACT_COLS) for part in parts)

    loop(spans, total)


def forward_finish_kernel(
    y_ref, x_ref, z_ref, dgo_ref, state_ref, decay_ref, in_ref, bc_ref, run_ref, cols_ref, gains_ref,
    scan_ref, sums_ref, cont, squares, inner,
):
    pair = pl.program_id(0)
    spans = y_ref.shape[0] // ROWS

    @pl.when(pair == 0)
    def _():
        def masks(q):
            row = span_start(q)
            cont[pl.ds(row, ROWS), :] = spread(cols_ref, row, 3)

        loop(spans, masks)
        squares[...] = jnp.zeros_like(squares)
        inner[...] = jnp.zeros_like(inner)

    incoming = in_ref[...]
    skip, gain = gains_ref[0:1], gains_ref[1:2]

    def span(q):
        at = pl.ds(span_start(q), ROWS)
        run = head_pair(run_ref[at, :], pair)
        state = entering(state_ref, decay_ref, incoming, q, q - 1)
        upper, lower = two_parts(state)
        c = c_parts(bc_ref, at)
        carried = dot(c, twice(upper)) + dot(c[:, :LANES], lower)
        scan = y_ref[at, :] + carried * (jnp.exp(run) * cont[at, :])
        scan_ref[at, :] = scan
        z = z_ref[at, :]
        gated = (scan + skip * x_ref[at, :]) * (z * sigmoid(z))
        squares[at, :] += gated * gated
        inner[at, :] += gain * dgo_ref[at, :] * gated

    loop(spans, span)

    @pl.when(pair == pl.num_programs(0) - 1)
    def _():
        row_sums(squares, sums_ref, 0, spans)
        row_sums(inner, sums_ref, 8, spans)


def gate_back_kernel(
    inner_width,
    scan_ref, x_ref, z_ref, dgo_ref, sums_ref, bc_ref, run_ref, cols_ref, gains_ref,
    out_ref, dz_ref, dy_ref, grad_ref, decay_ref, rows_ref,
    cont, rstd, coef, ct,
):
    pair = pl.program_id(0)
    spans = scan_ref.shape[0] // ROWS

    @pl.when(pair == 0)
    def _():
        def masks(q):
            row = span_start(q)
            at = pl.ds(row, ROWS)
            cont[at, :] = spread(cols_ref, row, 3)
            ct[q] = jnp.concatenate(
                [
                    jnp.transpose(bc_ref[at, k * LANES : (k + 1) * LANES].astype(F32)).astype(BF16)
                    for k in (2, 3)
                ],
                axis=1,
            )
            square = jnp.broadcast_to(sums_ref[q, 0:1, :], (ROWS, LANES))
            cross = jnp.broadcast_to(sums_ref[q, 1:2, :], (ROWS, LANES))
            root = lax.rsqrt(square / inner_width + EPS)
            rstd[at, :] = jnp.transpose(root)
            coef[at, :] = jnp.transpose(root * root * root * cross / inner_width)

        loop(spans, masks)

    skip, gain = gains_ref[0:1], gains_ref[1:2]
    rows_ref[...] = jnp.zeros_like(rows_ref)

    def span(k, carry):
        leaving, decay = carry
        q = spans - 1 - k
        at = pl.ds(span_start(q), ROWS)
        x, z, dgo = x_ref[at, :], z_ref[at, :], dgo_ref[at, :]
        scanned = scan_ref[at, :] + skip * x
        gate = sigmoid(z)
        silu = z * gate
        gated = scanned * silu
        normed = gated * rstd[at, :]
        out_ref[at, :] = (normed * gain).astype(BF16)
        d_gated = rstd[at, :] * (dgo * gain) - gated * coef[at, :]
        d_scan = d_gated * silu
        dz_ref[at, :] = (d_gated * scanned * (gate * (1.0 + z * (1.0 - gate)))).astype(BF16)
        dy_ref[at, :] = d_scan
        rows_ref[0:1] += jnp.sum(dgo * normed, axis=0, keepdims=True)
        rows_ref[1:2] += jnp.sum(d_scan * x, axis=0, keepdims=True)
        run = head_pair(run_ref[at, :], pair)
        enter = jnp.exp(run) * cont[at, :]
        upper, lower = two_parts(d_scan * enter)
        turned = ct[q]
        leaving = leaving * enter[ROWS - 1 :] + dot(turned, twice(upper)) + dot(turned[:, :ROWS], lower)
        decay = decay * enter[ROWS - 1 :]
        grad_ref[q] = leaving
        decay_ref[q] = jnp.broadcast_to(decay, (8, LANES))
        return leaving, decay

    lax.fori_loop(
        0, spans, span, (jnp.zeros((LANES, LANES), F32), jnp.ones((1, LANES), F32)),
        unroll=UNROLL,
    )


def backward_within_kernel(
    x_ref, dy_ref, bc_ref, step_ref, run_ref, run_t_ref, cols_ref, seg_rows_ref,
    dxw_ref, dbc_ref, mask, cross, d_cross,
):
    pair = pl.program_id(0)
    spans = x_ref.shape[0] // ROWS

    @pl.when(pair == 0)
    def _():
        span_masks(cols_ref, seg_rows_ref, mask, spans)

        def products(q):
            at = pl.ds(span_start(q), ROWS)
            cross[q] = cross_product(bc_ref, at)
            d_cross[q] = jnp.zeros((ROWS, ROWS), F32)

        loop(spans, products)

    def span(q):
        at = pl.ds(span_start(q), ROWS)
        size = head_pair(step_ref[at, :], pair)
        weighted = (x_ref[at, :] * size).astype(BF16)
        first, second = decay_pair(run_ref, run_t_ref, mask, q, pair)
        dy, dy_rest = two_parts(dy_ref[at, :])
        apart = heads_apart(dy)
        both = jnp.concatenate([apart, heads_apart(dy_rest)], axis=1)
        d_mix = dot(both, jnp.concatenate([weighted, weighted], axis=1), CONTRACT_COLS)
        d_cross[q] += first * d_mix[:ROWS] + second * d_mix[ROWS:]
        mix = jnp.concatenate([first * cross[q], second * cross[q]], axis=0).astype(BF16)
        dxw_ref[at, :] = dot(mix, apart, CONTRACT_ROWS)

    loop(spans, span)

    @pl.when(pair == pl.num_programs(0) - 1)
    def _():
        def shared(q):
            at = pl.ds(span_start(q), ROWS)
            grad = d_cross[q].astype(BF16)
            b, c = b_parts(bc_ref, at), c_parts(bc_ref, at)
            both = dot(grad, c, CONTRACT_ROWS)
            dbc_ref[at, :LANES] = both[:, :LANES] + both[:, LANES:]
            both = dot(grad, b)
            dbc_ref[at, LANES:] = both[:, :LANES] + both[:, LANES:]

        loop(spans, shared)


def conv_back(pad_ref, d_pre, same, taps, spans, store, rim_store):
    def span(q):
        at = pl.ds(span_start(q), ROWS + RIM)
        long = d_pre[at, :]
        total = taps[3:4] * long[:ROWS]
        for ahead in (1, 2, 3):
            start = span_start(q) + ahead
            moved = d_pre[pl.ds(start, ROWS), :] * same[ahead - 1, pl.ds(start, ROWS), :]
            total = total + taps[3 - ahead : 4 - ahead] * moved
        store(q, total)

    loop(spans, span)
    head = d_pre[0:RIM, :]
    total = jnp.zeros((RIM, LANES), F32)
    for ahead in (1, 2, 3):
        masked = head * same[ahead - 1, 0:RIM, :]
        both = jnp.concatenate([jnp.zeros((RIM, LANES), F32), masked], axis=0)
        total = total + taps[3 - ahead : 4 - ahead] * pltpu.roll(both, 2 * RIM - ahead, axis=0)[:RIM]
    rim_store(total)


def tap_sums(d_pre, shifted):
    sums = [jnp.sum(d_pre * shifted[3 - k], axis=0, keepdims=True) for k in range(4)]
    sums.append(jnp.sum(d_pre, axis=0, keepdims=True))
    return jnp.concatenate(sums + [jnp.zeros((3, LANES), F32)], axis=0)


def silu_grad(pre):
    gate = sigmoid(pre)
    return gate * (1.0 + pre * (1.0 - gate))


def backward_finish_kernel(
    value_ref, ss_ref, rim_v_ref, rim_ss_ref, x_ref, dy_ref, scan_ref, dxw_ref, dbc_ref,
    state_ref, decay_ref, in_ref, grad_ref, back_ref, out_ref,
    bc_ref, step_ref, run_ref, cols_ref, conv_ref, conv_ss_ref, heads_ref, gains_ref,
    low_ref, tail_ref, rim_ref, taps_ref, low_ss_ref, tail_ss_ref, rim_ss_out_ref, taps_ss_ref, small_ref,
    pad, d_pre, same, cont, last, d_run, d_step, d_bc,
):
    pair = pl.program_id(0)
    rows = value_ref.shape[0]
    spans = rows // ROWS

    @pl.when(pair == 0)
    def _():
        def masks(q):
            row = span_start(q)
            for k in range(3):
                same[k, pl.ds(row, ROWS), :] = spread(cols_ref, row, k)
            cont[pl.ds(row, ROWS), :] = spread(cols_ref, row, 3)
            last[pl.ds(row, ROWS), :] = spread(cols_ref, row, 4)

        loop(spans, masks)
        same[:, rows:, :] = jnp.zeros((3, RIM, LANES), F32)
        d_pre[rows:, :] = jnp.zeros((RIM, LANES), F32)
        d_run[...] = jnp.zeros_like(d_run)
        d_step[...] = jnp.zeros_like(d_step)
        d_bc[...] = dbc_ref[...]

    pad[0:RIM, :] = rim_v_ref[...]
    pad[RIM:, :] = value_ref[...]
    taps, bias = conv_ref[0:4], conv_ref[4:5]
    skip = gains_ref[0:1]
    incoming, outgoing = in_ref[...], out_ref[...]
    selector = head_selector(pair)
    taps_ref[...] = jnp.zeros_like(taps_ref)
    final_row = row_ids(ROWS) == ROWS - 1

    def span(q):
        row = span_start(q)
        at = pl.ds(row, ROWS)
        x, dy = x_ref[at, :], dy_ref[at, :]
        size = head_pair(step_ref[at, :], pair)
        run = head_pair(run_ref[at, :], pair)
        enter = jnp.exp(run) * cont[at, :]
        to_end = jnp.exp(run[ROWS - 1 :] - run) * last[at, :]
        state, state_rest = two_parts(entering(state_ref, decay_ref, incoming, q, q - 1))
        after = state_ref[q] + decay_ref[q, 0:1, :] * incoming
        ahead = jnp.minimum(q + 1, spans - 1)
        grad = jnp.where(
            q + 1 < spans, grad_ref[ahead] + back_ref[ahead, 0:1, :] * outgoing, outgoing
        )
        weighted = x * size
        low_grad = grad.astype(BF16)
        d_weighted = dxw_ref[at, :] + to_end * dot(b_parts(bc_ref, at), twice(low_grad))
        entered = in_two(dy * enter)
        d_bc[at, LANES:] += dot(
            entered, jnp.concatenate([state, state], axis=1), CONTRACT_COLS
        ) + dot(entered[:, :LANES], state_rest, CONTRACT_COLS)
        d_bc[at, :LANES] += dot((weighted * to_end).astype(BF16), low_grad, CONTRACT_COLS)
        turn = dy.astype(BF16).astype(F32) * scan_ref[at, :]
        turn = turn - d_weighted * weighted.astype(BF16).astype(F32)
        turn = turn + jnp.where(final_row, jnp.sum(grad * after, axis=0, keepdims=True), 0.0)
        d_run[at, :] += split_sum(turn, selector)
        d_step[at, :] += split_sum(d_weighted * x, selector)
        pre, shifted = conv_span(pad, same, row, taps, bias)
        d_act = (d_weighted * size + skip * dy) * silu_grad(pre)
        d_pre[at, :] = d_act
        taps_ref[...] += tap_sums(d_act, shifted)

    loop(spans, span)

    def keep(q, total):
        low_ref[pl.ds(span_start(q), ROWS), :] = total.astype(BF16)

        @pl.when(q == spans - 1)
        def _():
            tail_ref[...] = total[ROWS - RIM :]

    def keep_rim(total):
        rim_ref[...] = total

    conv_back(pad, d_pre, same, taps, spans, keep, keep_rim)

    @pl.when(pair == pl.num_programs(0) - 1)
    def _():
        for part in range(2):
            lanes = slice(part * LANES, (part + 1) * LANES)
            pad[0:RIM, :] = rim_ss_ref[:, lanes]
            pad[RIM:, :] = ss_ref[:, lanes]
            part_taps, part_bias = conv_ss_ref[0:4, lanes], conv_ss_ref[4:5, lanes]
            taps_ss_ref[:, lanes] = jnp.zeros((8, LANES), F32)

            def shared(q):
                row = span_start(q)
                at = pl.ds(row, ROWS)
                pre, shifted = conv_span(pad, same, row, part_taps, part_bias)
                d_act = d_bc[at, lanes] * silu_grad(pre)
                d_pre[at, :] = d_act
                taps_ss_ref[:, lanes] += tap_sums(d_act, shifted)

            loop(spans, shared)

            def keep_ss(q, total):
                low_ss_ref[pl.ds(span_start(q), ROWS), lanes] = total.astype(BF16)

                @pl.when(q == spans - 1)
                def _():
                    tail_ss_ref[:, lanes] = total[ROWS - RIM :]

            def keep_rim_ss(total):
                rim_ss_out_ref[:, lanes] = total

            conv_back(pad, d_pre, same, part_taps, spans, keep_ss, keep_rim_ss)

        step_bias, rate = heads_ref[0:1, :], heads_ref[1:2, :]
        small_ref[...] = jnp.zeros_like(small_ref)
        tri_t = upper_ones()

        def steps(q):
            at = pl.ds(span_start(q), ROWS)
            d_decay = sum(dot(tri_t, part) for part in three_parts(d_run[at, :]))
            slope = sigmoid(ss_ref[at, 2 * LANES :] + step_bias)
            d_raw = (d_step[at, :] - d_decay * rate) * slope
            low_ss_ref[at, 2 * LANES :] = d_raw.astype(BF16)
            small_ref[0:1] += jnp.sum(d_raw, axis=0, keepdims=True)
            small_ref[1:2] -= jnp.sum(d_decay * step_ref[at, :] * rate, axis=0, keepdims=True)

        loop(spans, steps)


def store_tiles(slots_ref, out_ref, value, scatter):
    if not scatter:
        out_ref[...] = value
        return
    tile = value.shape[0] // slots_ref.shape[0]
    for k in range(slots_ref.shape[0]):
        start = pl.multiple_of(slots_ref[k] * tile, tile)
        out_ref[pl.ds(start, tile), :] = value[k * tile : (k + 1) * tile]


def branch_kernel(scatter, slots_ref, rows_ref, weight_ref, out_ref):
    store_tiles(slots_ref, out_ref, dot(rows_ref[...], weight_ref[...]).astype(BF16), scatter)


def normed_grad_kernel(
    scatter, slots_ref, gate_ref, value_ref, ss_ref, gate_w, value_w, ss_w, normed_ref, out_ref, diag_ref
):
    total = dot(gate_ref[...], gate_w[...], CONTRACT_COLS)
    total = total + dot(value_ref[...], value_w[...], CONTRACT_COLS)
    total = total + dot(ss_ref[...], ss_w[...], CONTRACT_COLS)
    store_tiles(slots_ref, out_ref, total.astype(BF16), scatter)
    sums = jnp.sum(total * normed_ref[...].astype(F32), axis=0, keepdims=True)
    diag_ref[...] = jnp.broadcast_to(sums, diag_ref.shape)


def whole(shape):
    return pl.BlockSpec(shape, lambda j: (0,) * len(shape))


def columns(rows, width=LANES):
    return pl.BlockSpec((rows, width), lambda j: (0, j))


def value_columns(rows):
    return pl.BlockSpec((rows, LANES), lambda j: (0, j + 3))


def stacks(count, rows):
    return pl.BlockSpec((count, rows, LANES), lambda j: (0, 0, j))


def params():
    return pltpu.CompilerParams(vmem_limit_bytes=VMEM_BYTES, dimension_semantics=("arbitrary",))


def shaped(shape, dtype):
    return jax.ShapeDtypeStruct(shape, dtype)


def scratch(*shape, dtype=F32):
    return pltpu.VMEM(shape, dtype)


class Sizes:
    def __init__(self, rows, inner, heads):
        self.rows, self.inner, self.heads = rows, inner, heads
        self.spans, self.pairs = rows // ROWS, inner // LANES
        self.width = max(8, heads)

    def cost(self):
        cells = self.rows * self.inner
        return pl.CostEstimate(flops=1, bytes_accessed=1, transcendentals=0)


def forward_states(s, both, rim, cols, conv_v, conv_ss, heads):
    return pl.pallas_call(
        forward_states_kernel,
        grid=(s.pairs,),
        in_specs=[
            value_columns(s.rows), whole((s.rows, 3 * LANES)), value_columns(RIM), whole((RIM, 3 * LANES)),
            whole((s.rows, 8)), columns(8), whole((8, 2 * LANES)), whole((8, LANES)),
        ],
        out_specs=[
            columns(s.rows), whole((s.rows, 4 * LANES)), whole((s.rows, LANES)), whole((s.rows, LANES)),
            whole((s.spans, s.width, LANES)), stacks(s.spans, LANES), stacks(s.spans, 8),
        ],
        out_shape=[
            shaped((s.rows, s.inner), F32), shaped((s.rows, 4 * LANES), BF16),
            shaped((s.rows, LANES), F32), shaped((s.rows, LANES), F32),
            shaped((s.spans, s.width, LANES), F32),
            shaped((s.spans, LANES, s.inner), F32), shaped((s.spans, 8, s.inner), F32),
        ],
        scratch_shapes=[
            scratch(s.rows + RIM, LANES), scratch(3, s.rows, LANES), scratch(s.rows, LANES),
            scratch(s.rows, LANES), scratch(s.spans, LANES, 2 * ROWS, dtype=BF16),
        ],
        compiler_params=params(),
        cost_estimate=s.cost(),
        name="forward_states",
    )(both, both, rim, rim, cols, conv_v, conv_ss, heads)


def forward_within(s, x, bc, step, run, run_t, cols, seg_rows):
    return pl.pallas_call(
        forward_within_kernel,
        grid=(s.pairs,),
        in_specs=[
            columns(s.rows), whole((s.rows, 4 * LANES)), whole((s.rows, LANES)), whole((s.rows, LANES)),
            whole((s.spans, s.width, LANES)), whole((s.rows, 8)), whole((s.spans, 8, LANES)),
        ],
        out_specs=columns(s.rows),
        out_shape=shaped((s.rows, s.inner), F32),
        scratch_shapes=[scratch(s.spans, ROWS, ROWS), scratch(s.spans, ROWS, ROWS)],
        compiler_params=params(),
        cost_estimate=s.cost(),
        name="forward_within",
    )(x, bc, step, run, run_t, cols, seg_rows)


def forward_finish(s, y, x, z, dgo, state, decay, incoming, bc, run, cols, gains):
    return pl.pallas_call(
        forward_finish_kernel,
        grid=(s.pairs,),
        in_specs=[
            columns(s.rows), columns(s.rows), columns(s.rows), columns(s.rows),
            stacks(s.spans, LANES), stacks(s.spans, 8), columns(LANES),
            whole((s.rows, 4 * LANES)), whole((s.rows, LANES)), whole((s.rows, 8)), columns(8),
        ],
        out_specs=[columns(s.rows), whole((s.spans, 16, LANES))],
        out_shape=[shaped((s.rows, s.inner), F32), shaped((s.spans, 16, LANES), F32)],
        scratch_shapes=[scratch(s.rows, LANES)] * 3,
        compiler_params=params(),
        cost_estimate=s.cost(),
        name="forward_finish",
    )(y, x, z, dgo, state, decay, incoming, bc, run, cols, gains)


def gate_back(s, inner_width, scan, x, z, dgo, sums, bc, run, cols, gains):
    def kernel(*refs):
        gate_back_kernel(inner_width, *refs)

    return pl.pallas_call(
        kernel,
        grid=(s.pairs,),
        in_specs=[
            columns(s.rows), columns(s.rows), columns(s.rows), columns(s.rows),
            whole((s.spans, 8, LANES)), whole((s.rows, 4 * LANES)), whole((s.rows, LANES)),
            whole((s.rows, 8)), columns(8),
        ],
        out_specs=[
            columns(s.rows), columns(s.rows), columns(s.rows), stacks(s.spans, LANES),
            stacks(s.spans, 8), columns(8),
        ],
        out_shape=[
            shaped((s.rows, s.inner), BF16), shaped((s.rows, s.inner), BF16),
            shaped((s.rows, s.inner), F32), shaped((s.spans, LANES, s.inner), F32),
            shaped((s.spans, 8, s.inner), F32), shaped((8, s.inner), F32),
        ],
        scratch_shapes=[scratch(s.rows, LANES)] * 3 + [scratch(s.spans, LANES, 2 * ROWS, dtype=BF16)],
        compiler_params=params(),
        cost_estimate=s.cost(),
        name="gate_back",
    )(scan, x, z, dgo, sums, bc, run, cols, gains)


def backward_within(s, x, dy, bc, step, run, run_t, cols, seg_rows):
    return pl.pallas_call(
        backward_within_kernel,
        grid=(s.pairs,),
        in_specs=[
            columns(s.rows), columns(s.rows), whole((s.rows, 4 * LANES)), whole((s.rows, LANES)),
            whole((s.rows, LANES)), whole((s.spans, s.width, LANES)), whole((s.rows, 8)),
            whole((s.spans, 8, LANES)),
        ],
        out_specs=[columns(s.rows), whole((s.rows, 2 * LANES))],
        out_shape=[shaped((s.rows, s.inner), F32), shaped((s.rows, 2 * LANES), F32)],
        scratch_shapes=[scratch(s.spans, ROWS, ROWS)] * 3,
        compiler_params=params(),
        cost_estimate=s.cost(),
        name="backward_within",
    )(x, dy, bc, step, run, run_t, cols, seg_rows)


def backward_finish(
    s, both, rim, x, dy, scan, dxw, dbc, state, decay, incoming, grad, back, outgoing,
    bc, step, run, cols, conv_v, conv_ss, heads, gains,
):
    return pl.pallas_call(
        backward_finish_kernel,
        grid=(s.pairs,),
        in_specs=[
            value_columns(s.rows), whole((s.rows, 3 * LANES)), value_columns(RIM), whole((RIM, 3 * LANES)),
            columns(s.rows), columns(s.rows), columns(s.rows), columns(s.rows), whole((s.rows, 2 * LANES)),
            stacks(s.spans, LANES), stacks(s.spans, 8), columns(LANES),
            stacks(s.spans, LANES), stacks(s.spans, 8), columns(LANES),
            whole((s.rows, 4 * LANES)), whole((s.rows, LANES)), whole((s.rows, LANES)), whole((s.rows, 8)),
            columns(8), whole((8, 2 * LANES)), whole((8, LANES)), columns(8),
        ],
        out_specs=[
            columns(s.rows), columns(RIM), columns(RIM), columns(8),
            whole((s.rows, 3 * LANES)), whole((RIM, 2 * LANES)), whole((RIM, 2 * LANES)),
            whole((8, 2 * LANES)), whole((8, LANES)),
        ],
        out_shape=[
            shaped((s.rows, s.inner), BF16), shaped((RIM, s.inner), F32), shaped((RIM, s.inner), F32),
            shaped((8, s.inner), F32), shaped((s.rows, 3 * LANES), BF16), shaped((RIM, 2 * LANES), F32),
            shaped((RIM, 2 * LANES), F32), shaped((8, 2 * LANES), F32), shaped((8, LANES), F32),
        ],
        scratch_shapes=[
            scratch(s.rows + RIM, LANES), scratch(s.rows + RIM, LANES), scratch(3, s.rows + RIM, LANES),
            scratch(s.rows, LANES), scratch(s.rows, LANES), scratch(s.rows, LANES), scratch(s.rows, LANES),
            scratch(s.rows, 2 * LANES),
        ],
        compiler_params=params(),
        cost_estimate=s.cost(),
        name="backward_finish",
    )(
        both, both, rim, rim, x, dy, scan, dxw, dbc, state, decay, incoming, grad, back, outgoing,
        bc, step, run, cols, conv_v, conv_ss, heads, gains,
    )


WIDE = 256


def tile_product(kernel, slots, operands, specs, outs, out_specs, blocks, flops):
    rows = operands[0].shape[0]
    scatter = (rows // slots.shape[0]) % 16 == 0

    def body(*refs):
        kernel(scatter, *refs)

    results = pl.pallas_call(
        body,
        grid_spec=pltpu.PrefetchScalarGridSpec(
            num_scalar_prefetch=1, grid=(blocks,), in_specs=specs, out_specs=out_specs
        ),
        out_shape=outs,
        compiler_params=params(),
        cost_estimate=pl.CostEstimate(flops=1, bytes_accessed=1, transcendentals=0),
        name=kernel.__name__,
    )(slots, *operands)
    return results, scatter


def fixed(shape):
    return pl.BlockSpec(shape, lambda j, slots: (0,) * len(shape))


def branch_rows(slots, back_index, gated_low, out_proj):
    rows, inner = gated_low.shape
    width = out_proj.shape[1]
    [out], scatter = tile_product(
        branch_kernel,
        slots,
        (gated_low, out_proj),
        [fixed((rows, inner)), pl.BlockSpec((inner, WIDE), lambda j, slots: (0, j))],
        [shaped((rows, width), BF16)],
        [pl.BlockSpec((rows, WIDE), lambda j, slots: (0, j))],
        width // WIDE,
        2 * rows * inner * width,
    )
    return out if scatter else move_tiles(out, back_index)


def normed_grad(slots, back_index, lows, weights, normed):
    rows, width = normed.shape
    (out, diag), scatter = tile_product(
        normed_grad_kernel,
        slots,
        (*lows, *weights, normed),
        [fixed(low.shape) for low in lows]
        + [pl.BlockSpec((WIDE, w.shape[1]), lambda j, slots: (j, 0)) for w in weights]
        + [pl.BlockSpec((rows, WIDE), lambda j, slots: (0, j))],
        [shaped((rows, width), BF16), shaped((8, width), F32)],
        [pl.BlockSpec((rows, WIDE), lambda j, slots: (0, j)), pl.BlockSpec((8, WIDE), lambda j, slots: (0, j))],
        width // WIDE,
        2 * rows * width * sum(low.shape[1] for low in lows),
    )
    return (out if scatter else move_tiles(out, back_index)), diag[0]


def cot_kernel(slots_ref, arrived_ref, weight_ref, out_ref, packed_ref, rows, sems, packed_sem):
    step = pl.program_id(0)
    tiles = slots_ref.shape[0]
    tile = rows.shape[0] // tiles
    keep = pltpu.make_async_copy(rows, packed_ref, packed_sem)

    @pl.when(step == 0)
    def _():
        copies = []
        for k in range(tiles):
            start = pl.multiple_of(slots_ref[k] * tile, tile)
            copies.append(
                pltpu.make_async_copy(
                    arrived_ref.at[pl.ds(start, tile)], rows.at[pl.ds(k * tile, tile)], sems.at[k]
                )
            )
        for copy in copies:
            copy.start()
        for copy in copies:
            copy.wait()
        keep.start()

    out_ref[...] = dot(rows[...], weight_ref[...], CONTRACT_COLS)

    @pl.when(step == pl.num_programs(0) - 1)
    def _():
        keep.wait()


def cot_product(slots, arrived, weight):
    rows, width = arrived.shape
    inner, tiles = weight.shape[0], slots.shape[0]
    if (rows // tiles) % 16:
        packed = move_tiles(arrived, slots)
        return packed, dot(packed, weight, CONTRACT_COLS)
    out, packed = pl.pallas_call(
        cot_kernel,
        grid_spec=pltpu.PrefetchScalarGridSpec(
            num_scalar_prefetch=1,
            grid=(inner // WIDE,),
            in_specs=[
                pl.BlockSpec(memory_space=pl.ANY),
                pl.BlockSpec((WIDE, width), lambda j, slots: (j, 0)),
            ],
            out_specs=[
                pl.BlockSpec((rows, WIDE), lambda j, slots: (0, j)),
                pl.BlockSpec(memory_space=pl.ANY),
            ],
            scratch_shapes=[
                pltpu.VMEM((rows, width), BF16),
                pltpu.SemaphoreType.DMA((tiles,)),
                pltpu.SemaphoreType.DMA(()),
            ],
        ),
        out_shape=[shaped((rows, inner), F32), shaped((rows, width), BF16)],
        compiler_params=params(),
        cost_estimate=pl.CostEstimate(flops=1, bytes_accessed=1, transcendentals=0),
        name="cot_product",
    )(slots, arrived, weight)
    return packed, out


def swapped(value, axis, bit):
    count = lax.axis_size(axis)
    return lax.ppermute(value, axis, [(k, k ^ (1 << bit)) for k in range(count)])


def axis_bits(axis):
    return lax.axis_size(axis).bit_length() - 1


class RowsOverSeq:
    def __init__(self, grads, seq_index, backwards):
        bits, count = axis_bits("seq"), lax.axis_size("seq")
        self.here = seq_index
        self.total = grads.reshape((2,) * bits + (grads.shape[0] // count, grads.shape[1]))
        self.left = list(range(bits))[::-1]
        self.order = [0] + (list(range(1, bits))[::-1] if backwards else list(range(1, bits)))

    def swap(self):
        bit = self.order.pop(0)
        at, own = self.left.index(bit), (self.here >> bit) & 1
        self.left.pop(at)
        self.keep = lax.dynamic_index_in_dim(self.total, own, at, keepdims=False)
        self.send = lax.dynamic_index_in_dim(self.total, 1 - own, at, keepdims=False)
        return swapped(self.send, "seq", bit)

    def join(self, got):
        total = self.keep.astype(F32) + got.astype(F32)
        self.total = total.astype(self.total.dtype) if self.order else total


class SumByPairs:
    def __init__(self, value, axis):
        self.size, self.axis = value.shape[0], axis
        padded = jnp.pad(value, (0, -self.size % (8 * LANES)))
        self.total, self.order = padded.reshape(-1, LANES), list(range(axis_bits(axis)))

    def swap(self):
        self.keep = self.send = self.total
        return swapped(self.send, self.axis, self.order.pop(0))

    def join(self, got):
        self.total = self.keep + got
        if not self.order:
            self.total = self.total.reshape(-1)[: self.size]


class SumByHalves:
    def __init__(self, value, axis):
        self.total, self.axis, self.here = value, axis, lax.axis_index(axis)
        bits = list(range(axis_bits(axis)))
        self.order = [(bit, True) for bit in bits[::-1]] + [(bit, False) for bit in bits]

    def swap(self):
        bit, self.adds = self.order.pop(0)
        self.own = (self.here >> bit) & 1
        if self.adds:
            half = self.total.shape[0] // 2
            self.keep = lax.dynamic_slice_in_dim(self.total, self.own * half, half, 0)
            self.send = lax.dynamic_slice_in_dim(self.total, (1 - self.own) * half, half, 0)
        else:
            self.keep = self.send = self.total.astype(BF16)
        return swapped(self.send, self.axis, bit)

    def join(self, got):
        if self.adds:
            self.total = self.keep.astype(F32) + got.astype(F32)
            return
        mine, upper = self.keep, self.own == 1
        self.total = jnp.concatenate(
            [jnp.where(upper, got, mine), jnp.where(upper, mine, got)], axis=0
        )


class Chain:
    def __init__(self, part, *makers):
        self.part, self.makers, self.totals = part, list(makers), []

    @property
    def order(self):
        while not self.part.order and self.makers:
            self.totals.append(self.part.total)
            self.part = self.makers.pop(0)(self.part.total)
        return self.part.order

    @property
    def total(self):
        return self.part.total

    def swap(self):
        return self.part.swap()

    def join(self, got):
        self.part.join(got)


def swap_all(parts):
    return [(part, part.swap()) for part in parts if part.order]


def join_all(parts, got, *tokens):
    if not got:
        return
    arrived = lax.optimization_barrier((tuple(piece for _, piece in got), *tokens))[0]
    for (part, _), piece in zip(got, arrived):
        part.join(piece)


def finish_all(parts):
    while any(part.order for part in parts):
        join_all(parts, swap_all(parts))


def carried_states(states, decay, reverse, *covers, results=None):
    count = lax.axis_size("seq")
    sign = -1 if reverse else 1
    both = jnp.concatenate([states, decay], axis=0)
    results = [] if results is None else results

    def cover(reach, got):
        if len(results) == len(covers):
            return got
        result, token = covers[len(results)](reach)
        results.append(result)
        return after(got, token)

    def joined(near, far):
        through = near[LANES : LANES + 1]
        return jnp.concatenate([near[:LANES], jnp.zeros_like(near[LANES:])], axis=0) + through * far

    near, far = (from_behind(both, "seq", sign * k) for k in (1, 2))
    near, far = cover(both, (near, far))
    reach, width = joined(near, far), 2
    while width < count - 1:
        reach = joined(reach, cover(reach, from_behind(reach, "seq", sign * width)))
        width *= 2
    while len(results) < len(covers):
        cover(reach, reach)
    return reach[:LANES], results


def after(value, *tokens):
    return lax.optimization_barrier((value, *tokens))[0]


def from_behind(value, axis, steps):
    count = lax.axis_size(axis)
    initial, last = (max(0, -steps), min(count, count - steps))
    return lax.ppermute(value, axis, [(source, source + steps) for source in range(initial, last)])


def move_tiles(rows, index):
    tile_total = index.shape[0]
    shaped_rows = rows.reshape((tile_total, rows.shape[0] // tile_total) + rows.shape[1:])
    return jnp.take(shaped_rows, index, axis=0, mode="clip").reshape(rows.shape)


def carry_weights(decays, here, reverse):
    count = decays.shape[0]
    ids = jnp.arange(count, dtype=jnp.int32)
    if reverse:
        between = (ids[None, :] < ids[:, None]) & (ids[None, :] > here)
        reached = ids > here
    else:
        between = (ids[None, :] > ids[:, None]) & (ids[None, :] < here)
        reached = ids < here
    chain = jnp.prod(jnp.where(between[:, :, None], decays[None, :, :], 1.0), axis=1)
    return jnp.where(reached[:, None], chain, 0.0)


def padded_rows(parts, rows=8):
    stacked = jnp.concatenate([part.reshape(-1, part.shape[-1]) for part in parts], axis=0)
    return jnp.pad(stacked, ((0, rows - stacked.shape[0]), (0, 0)))


def local(
    tokens,
    packing,
    segment_ids,
    norm_gain,
    gate_proj,
    value_proj,
    shared_proj,
    step_proj,
    conv_value,
    conv_value_bias,
    conv_shared,
    conv_shared_bias,
    step_bias,
    log_decay,
    skip_gain,
    gated_gain,
    out_proj,
    cotangent,
):
    own_rows = tokens.shape[0]
    head_shards = lax.axis_size("head")
    seq_shards = lax.axis_size("seq")
    head_index = lax.axis_index("head")
    seq_index = lax.axis_index("seq")
    shard_rows = own_rows * head_shards
    inner_local = gate_proj.shape[1]
    heads_local = step_proj.shape[1]
    inner_width = inner_local * head_shards
    tile_rows = own_rows // seq_shards
    tile_count = shard_rows // tile_rows
    s = Sizes(shard_rows, inner_local, heads_local)

    packed_tiles = packing.reshape(-1, tile_rows)[:, 0] // tile_rows
    own_device = seq_index * head_shards + head_index
    seq_ids = jnp.arange(seq_shards, dtype=jnp.int32)
    own_tiles = own_device * seq_shards + seq_ids
    tile_match = (own_tiles[:, None] == packed_tiles[None, :]).astype(jnp.int32)
    tile_shard = jnp.arange(packed_tiles.shape[0], dtype=jnp.int32) // tile_count
    dest_shard = jnp.sum(tile_match * tile_shard[None, :], axis=1)
    send_index = jnp.sum(
        (dest_shard[None, :] == seq_ids[:, None]).astype(jnp.int32) * seq_ids[None, :], axis=1
    )
    own_packed = lax.dynamic_slice_in_dim(packed_tiles, seq_index * tile_count, tile_count, 0)
    source_device = own_packed // seq_shards
    arrival = source_device % head_shards * seq_shards + source_device // head_shards
    slot_ids = jnp.arange(tile_count, dtype=jnp.int32)
    back_index = jnp.sum(
        (arrival[None, :] == slot_ids[:, None]).astype(jnp.int32) * slot_ids[None, :], axis=1
    )

    shard_start = seq_index * shard_rows
    around = jnp.concatenate([jnp.full((RIM,), -1, jnp.int32), segment_ids])
    around = lax.dynamic_slice_in_dim(around, shard_start, shard_rows + RIM, 0)
    seg = around[RIM:]
    span_last = around[RIM - 1 :: ROWS]
    before_span = jnp.repeat(span_last[:-1], ROWS)
    end_of_span = jnp.repeat(span_last[1:], ROWS)
    facts = [around[RIM - k : RIM - k + shard_rows] == seg for k in (1, 2, 3)]
    facts += [before_span == seg, end_of_span == seg, seg, seg, seg]
    cols = jnp.stack([fact.astype(F32) for fact in facts], axis=1)
    seg_rows = jnp.broadcast_to(seg.astype(F32).reshape(s.spans, 1, ROWS), (s.spans, 8, ROWS))

    head_pad = ((0, 0), (0, LANES - heads_local))
    heads = padded_rows([step_bias, jnp.exp(log_decay)])
    heads = jnp.pad(heads, head_pad)
    conv_v = padded_rows([conv_value, conv_value_bias])
    conv_ss = padded_rows([conv_shared, conv_shared_bias])
    gains = padded_rows([jnp.repeat(skip_gain, inner_local // heads_local), gated_gain])
    ss_proj = jnp.concatenate([shared_proj, jnp.pad(step_proj, head_pad)], axis=1)

    tok_float = tokens.astype(F32)
    tok_rstd = lax.rsqrt(jnp.mean(tok_float * tok_float, axis=1, keepdims=True) + EPS)
    normed = (tok_float * tok_rstd * norm_gain[None, :]).astype(BF16)

    def to_shard(rows):
        sent = lax.all_to_all(
            move_tiles(rows, send_index), "seq", split_axis=0, concat_axis=0, tiled=True
        )
        return lax.all_gather(sent, "head", axis=0, tiled=True)

    packed_normed = move_tiles(to_shard(normed), arrival)
    arrived_cot = to_shard(cotangent)

    both = dot(packed_normed, jnp.concatenate([ss_proj, value_proj], axis=1))
    rim = from_behind(both[shard_rows - RIM :], "seq", 1)
    x, bc, step, run, run_t, state, decay = forward_states(
        s, both, rim, cols, conv_v, conv_ss, heads
    )

    def project_gate(reach):
        z = dot(after(packed_normed, reach), gate_proj)
        return z, z

    def within(reach):
        y = forward_within(s, after(x, reach), bc, step, run, run_t, cols, seg_rows)
        return y, y

    def cot_products(reach):
        cot, product = cot_product(after(arrival, reach), arrived_cot, out_proj)
        return (cot, product), product

    incoming, (y, gate_z, (packed_cot, dgo)) = carried_states(
        state[s.spans - 1], decay[s.spans - 1], False, within, project_gate, cot_products
    )
    scan, sums = forward_finish(
        s, y, x, gate_z, dgo, state, decay, incoming, bc, run, cols, gains
    )
    sums = lax.psum(jnp.stack([sums[:, 0, :], sums[:, 8, :]], axis=1), "head")
    sums = jnp.pad(sums, ((0, 0), (0, 6), (0, 0)))
    gated_low, low_gate, dy, grad, back, gate_rows = gate_back(
        s, inner_width, scan, x, gate_z, dgo, sums, bc, run, cols, gains
    )

    starts = lax.all_gather(jnp.concatenate([grad[0], decay[s.spans - 1]], axis=0), "seq")
    branch = branch_rows(arrival, back_index, gated_low, out_proj)
    dxw, dbc = backward_within(s, x, after(dy, branch), bc, step, run, run_t, cols, seg_rows)
    out_grads = dot(after(gated_low, dbc), packed_cot, CONTRACT_ROWS).astype(BF16)
    gate_grads = dot(after(packed_normed, out_grads), low_gate, CONTRACT_ROWS).astype(BF16)
    branch = lax.psum_scatter(
        after(branch, gate_grads), "head", scatter_dimension=0, tiled=True
    )
    out_sum = RowsOverSeq(out_grads, seq_index, True)
    gate_sum = RowsOverSeq(gate_grads, seq_index, False)
    early = [out_sum, gate_sum]
    got = swap_all(early)
    decays = starts[:, LANES, :]
    outgoing = jnp.sum(
        carry_weights(decays, seq_index, True)[:, None, :] * starts[:, :LANES, :], axis=0
    )
    dy = after(dy, gate_grads, *[part.keep for part in early], *[part.send for part in early])
    low_value, tail, rim_out, taps_v, low_ss, tail_ss, rim_ss_out, taps_ss, small = backward_finish(
        s, both, rim, x, dy, scan, dxw, dbc, state, decay, incoming, grad, back,
        outgoing, bc, step, run, cols, conv_v, conv_ss, heads, gains,
    )
    join_all(early, got, small)
    got = swap_all(early)
    rim_out = after(rim_out, *[part.send for part in early])
    rim_back = from_behind(jnp.concatenate([rim_out, rim_ss_out], axis=1), "seq", -1)
    tail = (jnp.concatenate([tail, tail_ss], axis=1) + rim_back).astype(BF16)
    low_value = lax.dynamic_update_slice(low_value, tail[:, :inner_local], (shard_rows - RIM, 0))
    low_ss = lax.dynamic_update_slice(low_ss, tail[:, inner_local:], (shard_rows - RIM, 0))

    ss_grads = dot(packed_normed, low_ss, CONTRACT_ROWS)
    shared_sum = Chain(
        RowsOverSeq(ss_grads[:, : 2 * LANES], seq_index, False), lambda total: SumByHalves(total, "head")
    )
    step_rows = RowsOverSeq(ss_grads[:, 2 * LANES :].astype(BF16), seq_index, False)
    got += swap_all([shared_sum, step_rows])
    low_gate = after(low_gate, ss_grads)
    d_normed, grad_norm_rows = normed_grad(
        arrival,
        back_index,
        (low_gate, low_value, low_ss),
        (gate_proj, value_proj, ss_proj),
        packed_normed,
    )
    arrived, low_value = lax.optimization_barrier(
        (tuple(piece for _, piece in got), after(low_value, d_normed))
    )
    d_normed = lax.psum_scatter(
        after(d_normed, branch), "head", scatter_dimension=0, tiled=True
    )
    for (part, _), piece in zip(got, arrived):
        part.join(piece)
    value_grads = dot(packed_normed, low_value, CONTRACT_ROWS).astype(BF16)

    first = swap_all([shared_sum, step_rows])
    gate_rows, small, taps_v, taps_ss, grad_norm_rows = after(
        (gate_rows, small, taps_v, taps_ss, grad_norm_rows), shared_sum.part.send
    )
    per_head = [jnp.sum(gate_rows[1].reshape(heads_local, -1), axis=1)]
    per_head += [small[0, :heads_local], small[1, :heads_local]]
    pieces = [taps_v[:5].reshape(-1), gate_rows[0]] + per_head
    own_size = sum(piece.shape[0] for piece in pieces)
    shared_pieces = [taps_ss[:5].reshape(-1), grad_norm_rows]
    flat_sum = Chain(
        SumByPairs(jnp.concatenate(pieces + shared_pieces), "seq"),
        lambda total: SumByPairs(total[own_size:], "head"),
    )
    half = inner_local // 2
    short = [shared_sum, flat_sum, step_rows]
    got = first + swap_all([flat_sum])
    arrived, value_grads = lax.optimization_barrier((tuple(piece for _, piece in got), value_grads))
    for (part, _), piece in zip(got, arrived):
        part.join(piece)
    values = [
        RowsOverSeq(value_grads[:, :half], seq_index, False),
        RowsOverSeq(value_grads[:, half:], seq_index, True),
    ]
    beside = [values, [], values, [], values]
    while any(part.order for part in short):
        got = swap_all(short + (beside.pop(0) if beside else []))
        if len(beside) == 1:
            arrived, branch_back = lax.optimization_barrier(
                (tuple(piece for _, piece in got), branch_back)
            )
            got = [(part, piece) for (part, _), piece in zip(got, arrived)]
        join_all(None, got)
        if len(beside) == 3:
            branch = after(branch, shared_sum.total)
            branch_back = lax.all_to_all(branch, "seq", split_axis=0, concat_axis=0, tiled=True)
    last = swap_all(early)
    normed_back = lax.all_to_all(d_normed, "seq", split_axis=0, concat_axis=0, tiled=True)
    arrived, normed_back = lax.optimization_barrier(
        (tuple(piece for _, piece in last), normed_back)
    )
    for (part, _), piece in zip(last, arrived):
        part.join(piece)
    finish_all(values + early)
    everything, grad_shared, shared_sums = flat_sum.totals[0], shared_sum.total, flat_sum.total
    grad_out_proj, grad_gate = out_sum.total, gate_sum.total
    grad_value = jnp.concatenate([part.total for part in values], axis=1)
    grad_step_proj = step_rows.total[:, :heads_local]
    grad_shared = lax.all_gather(grad_shared, "seq", axis=0, tiled=True).astype(F32)

    branch_given = move_tiles(branch_back, dest_shard).astype(F32)
    d_normed_given = move_tiles(normed_back, dest_shard).astype(F32)
    mixed_rows = (tok_float + branch_given).astype(BF16)
    scaled = d_normed_given * norm_gain[None, :]
    row_dot = jnp.sum(scaled * tok_float, axis=1, keepdims=True) / tokens.shape[1]
    d_tok = tok_rstd * scaled - tok_float * (tok_rstd * tok_rstd * tok_rstd * row_dot)
    grad_tokens = (cotangent.astype(F32) + d_tok).astype(BF16)

    own_taps = everything[: 5 * inner_local].reshape(5, inner_local)
    rest = everything[5 * inner_local : own_size]
    grad_gated = rest[:inner_local]
    rest = rest[inner_local:]
    grad_skip = rest[:heads_local]
    grad_step_bias = rest[heads_local : 2 * heads_local]
    grad_log_decay = rest[2 * heads_local :]
    shared_taps = shared_sums[: 10 * LANES].reshape(5, 2 * LANES)
    grad_norm_gain = shared_sums[10 * LANES : 10 * LANES + norm_gain.shape[0]] / norm_gain
    return (
        mixed_rows,
        grad_tokens,
        grad_norm_gain,
        grad_gate,
        grad_value,
        grad_shared,
        grad_step_proj,
        own_taps[:4],
        own_taps[4],
        shared_taps[:4],
        shared_taps[4],
        grad_step_bias,
        grad_log_decay,
        grad_skip,
        grad_gated,
        grad_out_proj,
    )


def solution(mesh):
    placed = (
        P(("seq", "head"), None),
        P(),
        P(),
        P(),
        P(None, "head"),
        P(None, "head"),
        P(),
        P(None, "head"),
        P(None, "head"),
        P("head"),
        P(),
        P(),
        P("head"),
        P("head"),
        P("head"),
        P("head"),
        P("head", None),
        P(("seq", "head"), None),
    )
    return jax.shard_map(
        local,
        mesh=mesh,
        in_specs=placed,
        out_specs=(
            P(("seq", "head"), None),
            P(("seq", "head"), None),
            P(),
            P("seq", "head"),
            P("seq", "head"),
            P(),
            P("seq", "head"),
            P(None, "head"),
            P("head"),
            P(),
            P(),
            P("head"),
            P("head"),
            P("head"),
            P("head"),
            P(("head", "seq"), None),
        ),
        check_vma=False,
    )
```
